32 devices in a mesh: dp: 4 (over x, core), fsdp: 8 (over z, y).
Axes of the slice: x: 2, y: 2, z: 4, core: 2. Of those that a mesh axis runs over, the one named last changes fastest.
Arguments:
- tokens: bfloat16 [2, 4096, 1024], P(None, ('dp', 'fsdp')), may hold values from -6 to 6
- scene_ids: int32 [2, 4, 1024], P(None, 'dp', 'fsdp'), may hold values from 0 to 1, never falling along the last dimension, each value on 1 to 682 neighbouring positions
- w_qkv: bfloat16 [1024, 3072], P(('dp', 'fsdp')), may hold values from -0.1875 to 0.1875
- w_out: bfloat16 [1024, 1024], P(('dp', 'fsdp')), may hold values from -6 to 6
- w_up: bfloat16 [1024, 4096], P(('dp', 'fsdp')), may hold values from -0.1875 to 0.1875
- w_down: bfloat16 [4096, 1024], P(('dp', 'fsdp')), may hold values from -0.09375 to 0.09375
- gain_one: bfloat16 [1024], P(('dp', 'fsdp')), may hold values from 0.5 to 1.5
- bias_one: bfloat16 [1024], P(('dp', 'fsdp')), may hold values from -1 to 1
- gain_two: bfloat16 [1024], P(('dp', 'fsdp')), may hold values from 0.5 to 1.5
- bias_two: bfloat16 [1024], P(('dp', 'fsdp')), may hold values from -1 to 1
- cotangent: bfloat16 [2, 4096, 1024], P(None, ('dp', 'fsdp')), may hold values from -6 to 6
Outputs:
- output: bfloat16 [2, 4096, 1024], P(None, ('dp', 'fsdp'))
- input_grad: float32 [2, 4096, 1024], P(None, ('dp', 'fsdp'))
- grad_qkv: float32 [1024, 3072], P(('dp', 'fsdp'))
- grad_out: float32 [1024, 1024], P(('dp', 'fsdp'))
- grad_up: float32 [1024, 4096], P(('dp', 'fsdp'))
- grad_down: float32 [4096, 1024], P(('dp', 'fsdp'))
- grad_gain_one: float32 [1024], P(('dp', 'fsdp'))
- grad_bias_one: float32 [1024], P(('dp', 'fsdp'))
- grad_gain_two: float32 [1024], P(('dp', 'fsdp'))
- grad_bias_two: float32 [1024], P(('dp', 'fsdp'))
The draws below stay inside these ranges and needn't reach their ends.
Inputs may be any that keep to these rules, and one draw needn't show every extreme that they name: `scene_ids`: in each scene group of a micro-batch the scene numbers never fall, each of the 2 scenes holds 1 to 682 tokens.
All inputs are finite; a program needn't handle non-finite values.
Results may differ from the reference program's by a relative error of at most 0.012.
Values may be sent and summed in bfloat16 or wider, within the bound.
No kernel may reach another device: no remote copies, remote signals or barrier semaphores. Data moves between devices by JAX's collectives and lax.ppermute only.
A program may use at most 320 MiB of HBM per device.

```python
import math
import jax
import jax.numpy as jnp
import numpy as np
from jax import lax

D = 1024
HEADS = 16
HEAD_DIM = 64
FF = 4096
MICRO = 2
GROUP_TOK = 1024
SCENE_MOST = 682
SCENES = 2
TOKENS = 4096
N_DP = 4


def block_levels(key, extent, shards, smallest, largest):
    level, own = 1.0, jax.random.fold_in(key, 6)
    for dim, parts in shards:
        heights = jnp.exp(jax.random.uniform(jax.random.fold_in(own, dim), (parts,), jnp.float32, smallest / len(shards), largest / len(shards)))
        level = level * jnp.repeat(heights, extent[dim] // parts).reshape([-1 if axis == dim else 1 for axis in range(len(extent))])
    return level


def length_profile(count, total, bound, skew):
    loads = [(1 << 20) // math.isqrt(standing ** skew) + 1 for standing in range(2, count + 1)]
    surplus, counts = total - bound - (count - 1), [1] * (count - 1)
    while surplus > 0:
        candidates = [i for i in range(count - 1) if counts[i] < bound]
        mass, left = sum([loads[i] for i in candidates]), surplus
        for i in candidates:
            more = min(bound - counts[i], max(1, left * loads[i] // mass), surplus)
            counts[i] = counts[i] + more
            surplus = surplus - more
    return np.array([bound] + counts)


def ragged_sizes(key, number_of, total, reach, lean):
    if number_of == 2:
        one = jax.random.randint(key, (), max(1, total - reach), min(reach, total - 1) + 1)
        return jnp.stack([one, total - one])
    tallies = jnp.asarray(length_profile(number_of, total, reach, lean), jnp.int32)
    twos = (number_of - 1) // 2
    source_of, receiver = tallies[1:1 + 2 * twos:2], tallies[2:2 + 2 * twos:2]
    room = jnp.minimum(source_of - 1, reach - receiver)
    passed = jax.random.randint(jax.random.fold_in(key, 1), (twos,), 0, 1 << 20) % (room + 1)
    tallies = tallies.at[1:1 + 2 * twos:2].set(source_of - passed).at[2:2 + 2 * twos:2].set(receiver + passed)
    return tallies[jax.random.permutation(jax.random.fold_in(key, 2), number_of)]


def noise(stream_key, extent, deviation, reach, split=(), held_as=jnp.bfloat16):
    entries = deviation * jax.random.normal(stream_key, extent, jnp.float32)
    if split:
        entries = entries * block_levels(stream_key, extent, split, -0.22, 0.18)
    return jnp.clip(entries, -reach, reach).astype(held_as)


def setup_inputs(seed: int = 0) -> dict:
    key_of = jax.random.split(jax.random.key(seed), 12)
    tokens = noise(key_of[0], (MICRO, TOKENS, D), 1.0, 6.0, ((1, 32),))
    scene_ids = jax.vmap(lambda own: jnp.searchsorted(jnp.cumsum(ragged_sizes(own, SCENES, GROUP_TOK, SCENE_MOST, 2)), jnp.arange(GROUP_TOK), side="right"))(jax.random.split(key_of[1], MICRO * N_DP)).reshape((MICRO, N_DP, GROUP_TOK)).astype(jnp.int32)
    w_qkv = noise(key_of[2], (D, 3 * D), D ** -0.5, 0.1875, ((0, 32),))
    w_out = noise(key_of[3], (D, D), 1 ** -0.5, 6.0, ((0, 32),))
    w_up = noise(key_of[4], (D, FF), D ** -0.5, 0.1875, ((0, 32),))
    w_down = noise(key_of[5], (FF, D), FF ** -0.5, 0.09375, ((0, 32),))
    gain_one = jnp.clip(1.0 + 0.1 * jax.random.normal(key_of[6], (D,), jnp.float32), 0.5, 1.5).astype(jnp.bfloat16)
    bias_one = noise(key_of[7], (D,), 0.2, 1.0, ((0, 32),))
    gain_two = jnp.clip(1.0 + 0.1 * jax.random.normal(key_of[8], (D,), jnp.float32), 0.5, 1.5).astype(jnp.bfloat16)
    bias_two = noise(key_of[9], (D,), 0.2, 1.0, ((0, 32),))
    cotangent = noise(key_of[10], (MICRO, TOKENS, D), 1.0, 6.0, ((1, 32),))
    return {"tokens": tokens, "scene_ids": scene_ids, "w_qkv": w_qkv, "w_out": w_out, "w_up": w_up, "w_down": w_down, "gain_one": gain_one, "bias_one": bias_one, "gain_two": gain_two, "bias_two": bias_two, "cotangent": cotangent}


@jax.custom_vjp
def low(v):
    return lax.optimization_barrier(v.astype(jnp.bfloat16)).astype(jnp.float32)

@jax.custom_vjp
def low_back(v):
    return v

def low_keep(v):
    return (low(v), None)

def low_pass(kept, grad):
    return (grad,)

def back_keep(v):
    return (v, None)

def back_low(kept, grad):
    return (low(grad),)
low.defvjp(low_keep, low_pass)
low_back.defvjp(back_keep, back_low)
eps_norm = 1e-05
highest = lax.Precision.HIGHEST

def layer_norm(values, gain, shift):
    average = lax.optimization_barrier(jnp.mean(values, axis=-1, keepdims=True))
    centered = values - average
    variance = lax.optimization_barrier(jnp.mean(centered * centered, axis=-1, keepdims=True))
    return centered * lax.rsqrt(variance + eps_norm) * gain + shift

def attend_rows(query_rows, scene_rows, key_heads, value_heads, key_scene):
    scores = jnp.einsum('qhd,khd->hqk', query_rows, key_heads, precision=highest) * (1.0 / math.sqrt(HEAD_DIM))
    scores = low_back(scores)
    same_scene = scene_rows[:, None] == key_scene[None, :]
    masked = jnp.where(same_scene[None], scores, -1000000000.0)
    probs = low(jax.nn.softmax(masked, axis=-1))
    return jnp.einsum('hqk,khd->qhd', probs, value_heads, precision=highest)

def group_forward(group_tokens, scene_row, w_qkv, w_out, w_up, w_down, gain_one, bias_one, gain_two, bias_two):
    row_count = group_tokens.shape[0]
    normed_one = low(layer_norm(group_tokens, gain_one, bias_one))
    projected = low_back(low(jnp.dot(normed_one, w_qkv, precision=highest)))
    queries = projected[:, :D].reshape(row_count, HEADS, HEAD_DIM)
    key_heads = projected[:, D:2 * D].reshape(row_count, HEADS, HEAD_DIM)
    value_heads = projected[:, 2 * D:].reshape(row_count, HEADS, HEAD_DIM)
    query_block = 512 if row_count % 512 == 0 else row_count
    query_blocks = queries.reshape(row_count // query_block, query_block, HEADS, HEAD_DIM)
    scene_blocks = scene_row.reshape(row_count // query_block, query_block)

    def one_block(pair):
        return attend_rows(pair[0], pair[1], key_heads, value_heads, scene_row)
    mixed = lax.map(jax.checkpoint(one_block), (query_blocks, scene_blocks)).reshape(row_count, D)
    mixed = low_back(low(mixed))
    hidden = group_tokens + low_back(jnp.dot(mixed, w_out, precision=highest))
    normed_two = low(layer_norm(hidden, gain_two, bias_two))
    upward = low_back(jnp.dot(normed_two, w_up, precision=highest))
    activated = low(jax.nn.gelu(upward, approximate=False))
    return hidden + low_back(jnp.dot(activated, w_down, precision=highest))

def reference(tokens, scene_ids, w_qkv, w_out, w_up, w_down, gain_one, bias_one, gain_two, bias_two, cotangent):
    params = (w_qkv.astype(jnp.float32), w_out.astype(jnp.float32), w_up.astype(jnp.float32), w_down.astype(jnp.float32), gain_one.astype(jnp.float32), bias_one.astype(jnp.float32), gain_two.astype(jnp.float32), bias_two.astype(jnp.float32))
    group_total = MICRO * N_DP
    token_groups = tokens.astype(jnp.float32).reshape(group_total, GROUP_TOK, D)
    grad_groups = cotangent.astype(jnp.float32).reshape(group_total, GROUP_TOK, D)
    scene_groups = scene_ids.reshape(group_total, GROUP_TOK)

    def step_group(totals, inputs):
        group_tokens, scene_row, group_grad = inputs

        def local_layer(tok_in, qkv_in, out_in, up_in, down_in, gone_in, bone_in, gtwo_in, btwo_in):
            return group_forward(tok_in, scene_row, qkv_in, out_in, up_in, down_in, gone_in, bone_in, gtwo_in, btwo_in)
        result, pullback = jax.vjp(local_layer, group_tokens, params[0], params[1], params[2], params[3], params[4], params[5], params[6], params[7])
        grads = pullback(group_grad)
        totals = jax.tree.map(jnp.add, totals, tuple(grads[1:]))
        return (totals, (result.astype(jnp.bfloat16), grads[0]))
    init = tuple((jnp.zeros(weight.shape, jnp.float32) for weight in params))
    totals, (results, input_grads) = lax.scan(step_group, init, (token_groups, scene_groups, grad_groups))
    output = results.reshape(MICRO, TOKENS, D)
    input_grad = input_grads.reshape(MICRO, TOKENS, D)
    return (output, input_grad, totals[0], totals[1], totals[2], totals[3], totals[4], totals[5], totals[6], totals[7])
```

```python
import functools
import math

import jax
import jax.numpy as jnp
from jax import lax
from jax.experimental import pallas as pl
from jax.experimental.pallas import tpu as pltpu
from jax.sharding import PartitionSpec as P

AXES = ("dp", "fsdp")
HEAD_DIM = 64
EPS = 1e-05
LOWEST = -1000000000.0
F32 = jnp.float32
BF16 = jnp.bfloat16
NT = (((1,), (1,)), ((), ()))
TN = (((0,), (0,)), ((), ()))
NN = (((1,), (0,)), ((), ()))


def dot(left, right, dims):
    return lax.dot_general(left, right, dims, preferred_element_type=F32)


def head_lanes(rows, width, head):
    lane = lax.broadcasted_iota(jnp.int32, (rows, width), 1)
    return (lane >= head * HEAD_DIM) & (lane < (head + 1) * HEAD_DIM)


def attend_kernel(heads, ksc_ref, qsc_ref, q_ref, k_ref, v_ref, mixed_ref, lse_ref, vt_ref):
    @pl.when(pl.program_id(0) == 0)
    def _():
        vt_ref[...] = v_ref[...].astype(F32).T.astype(BF16)

    rows, width = q_ref.shape
    same = ksc_ref[...] == qsc_ref[...]
    q = q_ref[...].astype(F32) * (1.0 / math.sqrt(HEAD_DIM))
    outs = []
    for h in range(heads):
        qh = jnp.where(head_lanes(rows, width, h), q, 0.0).astype(BF16)
        s = jnp.where(same, dot(k_ref[...], qh, NT), LOWEST)
        peak = jnp.max(s, axis=0, keepdims=True)
        e = jnp.exp(s - peak)
        total = jnp.sum(e, axis=0, keepdims=True)
        lse_ref[h : h + 1, :] = peak + jnp.log(total)
        p = (e * (1.0 / total)).astype(BF16)
        outs.append(dot(vt_ref[h * HEAD_DIM : (h + 1) * HEAD_DIM, :], p, NN))
    mixed_ref[...] = jnp.concatenate(outs, axis=0).T.astype(BF16)


def attend_back_kernel(
    heads, ksc_ref, qsc_ref, lse_ref, q_ref, do_ref, k_ref, v_ref, dq_ref, dk_ref, dv_ref, kt_ref, dka_ref, dva_ref
):
    step = pl.program_id(0)

    @pl.when(step == 0)
    def _():
        kt_ref[...] = k_ref[...].astype(F32).T.astype(BF16)
        dka_ref[...] = jnp.zeros_like(dka_ref)
        dva_ref[...] = jnp.zeros_like(dva_ref)

    rows, width = q_ref.shape
    scale = 1.0 / math.sqrt(HEAD_DIM)
    same = ksc_ref[...] == qsc_ref[...]
    q = q_ref[...].astype(F32) * scale
    do = do_ref[...].astype(F32)
    outs = []
    for h in range(heads):
        mine = head_lanes(rows, width, h)
        qh = jnp.where(mine, q, 0.0).astype(BF16)
        doh = jnp.where(mine, do, 0.0).astype(BF16)
        s = jnp.where(same, dot(k_ref[...], qh, NT), LOWEST)
        p = jnp.exp(s - lse_ref[h : h + 1, :])
        dp = dot(v_ref[...], doh, NT)
        inner = jnp.sum(p * dp, axis=0, keepdims=True)
        ds = (p * (dp - inner)).astype(BF16)
        dva_ref[...] += dot(p.astype(BF16), doh, NN)
        dka_ref[...] += dot(ds, qh, NN)
        outs.append(dot(kt_ref[h * HEAD_DIM : (h + 1) * HEAD_DIM, :], ds, NN))
    dq_ref[...] = (jnp.concatenate(outs, axis=0).T * scale).astype(BF16)

    @pl.when(step == pl.num_programs(0) - 1)
    def _():
        dk_ref[...] = dka_ref[...].astype(BF16)
        dv_ref[...] = dva_ref[...].astype(BF16)


VMEM_LIMIT = 56 * 1024 * 1024


def attend(q, k, v, qsc, ksc):
    rows, width = q.shape
    keys = k.shape[0]
    heads = width // HEAD_DIM
    block = 256
    return pl.pallas_call(
        functools.partial(attend_kernel, heads),
        out_shape=(
            jax.ShapeDtypeStruct((rows, width), BF16),
            jax.ShapeDtypeStruct((heads, rows), F32),
        ),
        grid=(rows // block,),
        in_specs=[
            pl.BlockSpec((keys, 1), lambda i: (0, 0)),
            pl.BlockSpec((1, block), lambda i: (0, i)),
            pl.BlockSpec((block, width), lambda i: (i, 0)),
            pl.BlockSpec((keys, width), lambda i: (0, 0)),
            pl.BlockSpec((keys, width), lambda i: (0, 0)),
        ],
        out_specs=(
            pl.BlockSpec((block, width), lambda i: (i, 0)),
            pl.BlockSpec((heads, block), lambda i: (0, i)),
        ),
        scratch_shapes=[pltpu.VMEM((width, keys), BF16)],
        compiler_params=pltpu.CompilerParams(vmem_limit_bytes=VMEM_LIMIT),
        cost_estimate=pl.CostEstimate(
            flops=4 * rows * keys * width, bytes_accessed=8 * rows * width, transcendentals=rows * keys * heads
        ),
        name="attend",
    )(ksc, qsc, q, k, v)


def attend_back(q, k, v, qsc, ksc, lse, do):
    rows, width = q.shape
    keys = k.shape[0]
    heads = width // HEAD_DIM
    block = 256
    row_block = pl.BlockSpec((block, width), lambda i: (i, 0))
    whole = pl.BlockSpec((keys, width), lambda i: (0, 0))
    return pl.pallas_call(
        functools.partial(attend_back_kernel, heads),
        out_shape=(
            jax.ShapeDtypeStruct((rows, width), BF16),
            jax.ShapeDtypeStruct((keys, width), BF16),
            jax.ShapeDtypeStruct((keys, width), BF16),
        ),
        grid=(rows // block,),
        in_specs=[
            pl.BlockSpec((keys, 1), lambda i: (0, 0)),
            pl.BlockSpec((1, block), lambda i: (0, i)),
            pl.BlockSpec((heads, block), lambda i: (0, i)),
            row_block,
            row_block,
            whole,
            whole,
        ],
        out_specs=(row_block, whole, whole),
        scratch_shapes=[
            pltpu.VMEM((width, keys), BF16),
            pltpu.VMEM((keys, width), F32),
            pltpu.VMEM((keys, width), F32),
        ],
        compiler_params=pltpu.CompilerParams(vmem_limit_bytes=VMEM_LIMIT),
        cost_estimate=pl.CostEstimate(
            flops=10 * rows * keys * width, bytes_accessed=14 * rows * width, transcendentals=rows * keys * heads
        ),
        name="attend_back",
    )(ksc, qsc, lse, q, do, k, v)


class Places:
    def __init__(self, mesh):
        self.n_dp, self.n_fsdp = mesh.shape["dp"], mesh.shape["fsdp"]
        self.xs, self.zs = self.n_dp // 2, self.n_fsdp // 2
        self.nodes = self.xs * self.zs
        self.all = [
            (x, c, z, y) for x in range(self.xs) for c in range(2) for z in range(self.zs) for y in range(2)
        ]

    def lin(self, x, c, z, y):
        return (x * 2 + c) * self.n_fsdp + z * 2 + y

    def perm(self, move):
        return [(self.lin(*d), self.lin(*move(*d))) for d in self.all]

    def spot(self, x, z):
        return x * self.zs + (z if x % 2 == 0 else self.zs - 1 - z)

    def node(self, spot):
        x, z = spot // self.zs, spot % self.zs
        return (x, z if x % 2 == 0 else self.zs - 1 - z)

    def ring(self, by):
        def move(x, c, z, y):
            x2, z2 = self.node((self.spot(x, z) + by) % self.nodes)
            return (x2, c, z2, y)

        return self.perm(move)


def permute(array, pairs):
    return lax.ppermute(array, AXES, pairs)


def body(places, tokens, scene_ids, w_qkv, w_out, w_up, w_down, gain_one, bias_one, gain_two, bias_two, cotangent):
    pc = places
    micro, run, width = tokens.shape
    n_dev = pc.n_dp * pc.n_fsdp
    rows = w_qkv.shape[0]
    ff = w_up.shape[1]
    hid = w_down.shape[0]
    quarter = width // 4
    dp, fsdp = lax.axis_index("dp"), lax.axis_index("fsdp")
    x, core, z, y = dp // 2, dp % 2, fsdp // 2, fsdp % 2
    rank = y * 2 + core
    spot = x * pc.zs + jnp.where(x % 2 == 0, z, pc.zs - 1 - z)
    groups = micro * 2
    quads = pc.zs // groups

    p_core = pc.perm(lambda x, c, z, y: (x, 1 - c, z, y))
    p_y = pc.perm(lambda x, c, z, y: (x, c, z, 1 - y))
    p_diag = pc.perm(lambda x, c, z, y: (x, 1 - c, z, 1 - y))
    p_cw, p_ccw = pc.ring(1), pc.ring(-1)

    def place_perm(flip):
        def move(x, c, z, y):
            m = (z % 2) ^ flip
            return (x, (z // 2) % 2, (m * 2 + c) * quads + z // 4, y)

        return pc.perm(move)

    p_place = [place_perm(0), place_perm(1)]
    p_back = [[(b, a) for a, b in pairs] for pairs in p_place]

    def node_of(s):
        nx = s // pc.zs
        nz = s % pc.zs
        return nx, jnp.where(nx % 2 == 0, nz, pc.zs - 1 - nz)

    def quad_gather(a):
        across = permute(a, p_y)
        return [a, permute(a, p_core), across, permute(across, p_core)]

    def quad_swap(parts):
        return [parts[0], permute(parts[1], p_core), permute(parts[2], p_y), permute(parts[3], p_diag)]

    def quad_sum(parts):
        got = permute(jnp.concatenate([parts[1], parts[3]], 0).astype(BF16), p_core).astype(F32)
        half = parts[0].shape[0]
        far = parts[2] + got[half:]
        near = parts[0] + got[:half]
        return near + permute(far.astype(BF16), p_y).astype(F32)

    def by_rank(parts):
        odd, top = rank % 2 == 1, rank // 2 == 1
        parts = [jnp.where(odd, parts[i ^ 1], parts[i]) for i in range(4)]
        return [jnp.where(top, parts[i ^ 2], parts[i]) for i in range(4)]

    half_ring = pc.nodes // 2

    def ring_gather(shard):
        pieces = {0: shard}
        cw = ccw = shard
        for k in range(1, half_ring):
            cw, ccw = permute(cw, p_cw), permute(ccw, p_ccw)
            pieces[-k], pieces[k] = cw, ccw
        h = shard.shape[0] // 2
        pieces[half_ring] = jnp.concatenate([permute(cw[:h], p_cw), permute(ccw[h:], p_ccw)], 0)
        return pieces

    def lay(pieces, shape, put):
        out = jnp.zeros(shape, BF16)
        for k, piece in pieces.items():
            nx, nz = node_of((spot + k) % pc.nodes)
            out = put(out, piece, nx, nz)
        return out

    def ring_scatter(share):
        def half(v):
            return v.shape[0] // 2

        far = share((spot + half_ring) % pc.nodes)
        h = half(far)
        cw, ccw = permute(far[:h].astype(BF16), p_cw), permute(far[h:].astype(BF16), p_ccw)
        for s in range(1, half_ring):
            one = share((spot + half_ring - s) % pc.nodes)
            two = share((spot - half_ring + s) % pc.nodes)
            if s == 1:
                one = jnp.concatenate([one[:h] + cw.astype(F32), one[h:]], 0)
                two = jnp.concatenate([two[:h], two[h:] + ccw.astype(F32)], 0)
            else:
                one, two = one + cw.astype(F32), two + ccw.astype(F32)
            cw, ccw = permute(one.astype(BF16), p_cw), permute(two.astype(BF16), p_ccw)
        return share(spot) + cw.astype(F32) + ccw.astype(F32)

    lin = dp * pc.n_fsdp + fsdp
    small = jnp.concatenate(
        [gain_one, bias_one, gain_two, bias_two, scene_ids.astype(BF16).reshape(micro * run)], 0
    )[None]
    bit = 1
    while bit < n_dev:
        other = permute(small, [(i, i ^ bit) for i in range(n_dev)])
        upper = (lin & bit) != 0
        small = jnp.where(
            upper, jnp.concatenate([other, small], 0), jnp.concatenate([small, other], 0)
        )
        bit *= 2
    norms = small[:, : 4 * rows].reshape(n_dev, 4, rows).transpose(1, 0, 2).reshape(4, width).astype(F32)
    gone, bone, gtwo, btwo = norms[0:1], norms[1:2], norms[2:3], norms[3:4]
    scenes = small[:, 4 * rows :].astype(F32).reshape(pc.xs, 2, pc.zs, 2, micro, run)

    z_odd = z % 2

    def place(a):
        one = jnp.where(z_odd == 0, a[0], a[1])
        two = jnp.where(z_odd == 0, a[1], a[0])
        return jnp.concatenate([permute(one, p_place[0]), permute(two, p_place[1])], 0)

    def place_back(a):
        one, two = permute(a[:run], p_back[0]), permute(a[run:], p_back[1])
        return jnp.stack([jnp.where(z_odd == 0, one, two), jnp.where(z_odd == 0, two, one)], 0)

    group = z // quads
    my_quad = z % quads
    my_micro = group // 2
    g_scenes = lax.dynamic_slice(
        scenes, (x, group % 2, 0, 0, my_micro, 0), (1, 1, pc.zs, 2, 1, run)
    ).reshape(quads, 2, 2, 2, run)
    g_scenes = jnp.where(core == 1, g_scenes[:, ::-1], g_scenes)
    g_scenes = jnp.where(my_micro == 1, g_scenes[:, :, ::-1], g_scenes)
    g_scenes = jnp.where(y == 1, g_scenes[:, :, :, ::-1], g_scenes)
    g_scenes = g_scenes.transpose(0, 3, 1, 2, 4).reshape(quads, 8 * run)
    q_scenes = lax.dynamic_slice(g_scenes, (my_quad, 0), (1, 8 * run))
    k_scenes = jnp.concatenate(
        [lax.dynamic_slice(g_scenes, ((my_quad - s) % quads, 0), (1, 8 * run)) for s in range(quads)], 1
    ).reshape(quads * 8 * run, 1)

    wq = w_qkv.reshape(rows, 3, 4, quarter)
    parts = [
        lax.dynamic_index_in_dim(wq, rank ^ p, axis=2, keepdims=False).reshape(rows, 3 * quarter) for p in range(4)
    ]
    qkv_shard = jnp.concatenate(by_rank_order(by_rank(quad_swap(parts))), 0).reshape(2, 2 * rows, 3 * quarter)

    def put_rows(out, piece, nx, nz):
        return lax.dynamic_update_slice(out, piece[None, :, None], (nx, 0, nz, 0, 0))

    full_qkv = lay(
        ring_gather(qkv_shard), (pc.xs, 2, pc.zs, 2 * rows, 3 * quarter), put_rows
    ).reshape(width, 3 * quarter)

    wu = w_up.reshape(rows, pc.xs, 2, pc.zs, 2, hid)

    def up_part(p):
        c2, y2 = core ^ (p & 1), y ^ (p >> 1)
        return lax.dynamic_slice(wu, (0, 0, c2, 0, y2, 0), (rows, pc.xs, 1, pc.zs, 1, hid)).reshape(rows, ff // 4)

    up_shard = jnp.concatenate(by_rank_order(by_rank(quad_swap([up_part(p) for p in range(4)]))), 0)
    over = permute(w_out, p_y)
    out_shard = jnp.where(
        y == 0, jnp.concatenate([w_out, over], 0), jnp.concatenate([over, w_out], 0)
    )
    pieces = ring_gather(jnp.concatenate([out_shard, up_shard, w_down], 0))
    e1, e2 = 2 * rows, 6 * rows
    near_out = lay(
        {k: v[:e1] for k, v in pieces.items()},
        (pc.xs, pc.zs, 2 * rows, width),
        lambda out, piece, nx, nz: lax.dynamic_update_slice(out, piece[None, None], (nx, nz, 0, 0)),
    )
    far_out = permute(near_out, p_core)
    full_out = jnp.where(
        core == 0, jnp.stack([near_out, far_out], 1), jnp.stack([far_out, near_out], 1)
    ).reshape(width, width)
    full_up = lay(
        {k: v[e1:e2].reshape(2, 2 * rows, ff // 4) for k, v in pieces.items()},
        (pc.xs, 2, pc.zs, 2 * rows, ff // 4),
        put_rows,
    ).reshape(width, ff // 4)
    full_down = lay(
        {k: v[e2:] for k, v in pieces.items()},
        (pc.xs, pc.zs, hid, width),
        lambda out, piece, nx, nz: lax.dynamic_update_slice(out, piece[None, None], (nx, nz, 0, 0)),
    ).reshape(ff // 4, width)

    def standardize(v):
        centered = v - jnp.mean(v, axis=-1, keepdims=True)
        inv = lax.rsqrt(jnp.mean(centered * centered, axis=-1, keepdims=True) + EPS)
        return centered * inv, inv

    def norm_back(d_norm, std, inv, gain):
        d_std = d_norm * gain
        return inv * (
            d_std
            - jnp.mean(d_std, axis=-1, keepdims=True)
            - std * jnp.mean(d_std * std, axis=-1, keepdims=True)
        )

    own = place(tokens).astype(F32)
    own_rows = own.shape[0]
    std_one, inv_one = standardize(own)
    n_one = jnp.concatenate(quad_gather((std_one * gone + bone).astype(BF16)), 0)
    projected = dot(n_one, full_qkv, NN).astype(BF16)
    q, kv = projected[:, :quarter], projected[:, quarter:]

    def group_perm(by):
        return pc.perm(lambda x, c, z, y: (x, c, z // quads * quads + (z + by) % quads, y))

    kv_all = jnp.concatenate([kv] + [permute(kv, group_perm(s)) for s in range(1, quads)], 0)
    k, v = kv_all[:, :quarter], kv_all[:, quarter:]
    mixed, lse = attend(q, k, v, q_scenes, k_scenes)

    def pieces_of(a):
        return [a[i * own_rows : (i + 1) * own_rows] for i in range(4)]

    mixed_own = jnp.concatenate(by_rank(quad_swap(pieces_of(mixed))), 1)
    hidden = own + dot(mixed_own, full_out, NN)
    std_two, inv_two = standardize(hidden)
    n_two = jnp.concatenate(quad_gather((std_two * gtwo + btwo).astype(BF16)), 0)
    upward = dot(n_two, full_up, NN)
    cdf = 0.5 * (1.0 + lax.erf(upward * math.sqrt(0.5)))
    activated = (upward * cdf).astype(BF16)
    slope = cdf + upward * jnp.exp(-0.5 * upward * upward) * (1.0 / math.sqrt(2.0 * math.pi))
    dy_own = place(cotangent)
    dy = jnp.concatenate(quad_gather(dy_own), 0)
    d_act = dot(dy, full_down, NT)
    d_up = (d_act * slope).astype(BF16)
    d_norm_two = quad_sum(pieces_of(dot(d_up, full_up, NT)))
    result = hidden + quad_sum(pieces_of(dot(activated, full_down, NN)))
    output = place_back(result.astype(BF16))
    grad_down = dot(activated, dy, TN).reshape(pc.xs, pc.zs, hid, width)
    grad_up = dot(n_two, d_up, TN).reshape(pc.xs, 2, pc.zs, 2 * rows, ff // 4)

    def share_ff(s):
        nx, nz = node_of(s)
        a = lax.dynamic_slice(grad_up, (nx, 0, nz, 0, 0), (1, 2, 1, 2 * rows, ff // 4)).reshape(4 * rows, ff // 4)
        b = lax.dynamic_slice(grad_down, (nx, nz, 0, 0), (1, 1, hid, width)).reshape(hid, width)
        return jnp.concatenate([a, b], 0)

    summed_ff = ring_scatter(share_ff)

    d_hidden = dy_own.astype(F32) + norm_back(d_norm_two, std_two, inv_two, gtwo)
    d_hidden_low = d_hidden.astype(BF16)
    d_mixed_own = dot(d_hidden_low, full_out, NT).astype(BF16)
    d_cols = by_rank([d_mixed_own[:, i * quarter : (i + 1) * quarter] for i in range(4)])
    d_mixed = jnp.concatenate(quad_swap(d_cols), 0)
    dq, dk, dv = attend_back(q, k, v, q_scenes, k_scenes, lse, d_mixed)
    dkv = jnp.concatenate([dk, dv], 1)
    n_rows = dkv.shape[0] // quads
    if quads > 1:
        total = dkv[:n_rows].astype(F32)
        for s in range(1, quads):
            total = total + permute(dkv[s * n_rows : (s + 1) * n_rows], group_perm(-s)).astype(F32)
        dkv = total.astype(BF16)
    d_projected = jnp.concatenate([dq, dkv], 1)
    d_norm_one = quad_sum(pieces_of(dot(d_projected, full_qkv, NT)))
    grad_qkv = dot(n_one, d_projected, TN).reshape(pc.xs, 2, pc.zs, 2 * rows, 3 * quarter)

    def share_qkv(s):
        nx, nz = node_of(s)
        return lax.dynamic_slice(grad_qkv, (nx, 0, nz, 0, 0), (1, 2, 1, 2 * rows, 3 * quarter)).reshape(
            4 * rows, 3 * quarter
        )

    summed_qkv = ring_scatter(share_qkv)
    grad_out = dot(mixed_own, d_hidden_low, TN).reshape(pc.xs, 2, pc.zs, 2 * rows, width)
    mine = lax.dynamic_index_in_dim(grad_out, core, axis=1, keepdims=False)
    other = lax.dynamic_index_in_dim(grad_out, 1 - core, axis=1, keepdims=False)
    core_out = mine + permute(other.astype(BF16), p_core).astype(F32)

    def share_out(s):
        nx, nz = node_of(s)
        return lax.dynamic_slice(core_out, (nx, nz, 0, 0), (1, 1, 2 * rows, width)).reshape(2 * rows, width)

    summed_out = ring_scatter(share_out).reshape(2, rows, width)
    mine = lax.dynamic_index_in_dim(summed_out, y, axis=0, keepdims=False)
    other = lax.dynamic_index_in_dim(summed_out, 1 - y, axis=0, keepdims=False)
    own_out = mine + permute(other.astype(BF16), p_y).astype(F32)

    d_tokens = d_hidden + norm_back(d_norm_one, std_one, inv_one, gone)
    input_grad = place_back(d_tokens.astype(BF16)).astype(F32)

    def home(summed):
        blocks = by_rank(by_rank_order([summed[i * rows : (i + 1) * rows].astype(BF16) for i in range(4)]))
        return quad_swap(blocks)

    own_qkv = jnp.stack(
        by_rank([b.reshape(rows, 3, quarter) for b in home(summed_qkv)]), 2
    ).reshape(rows, 3 * width).astype(F32)
    ups = by_rank([b.reshape(rows, pc.xs, pc.zs, hid) for b in home(summed_ff[: 4 * rows])])
    own_up = (
        jnp.stack([jnp.stack([ups[0], ups[2]], 3), jnp.stack([ups[1], ups[3]], 3)], 2)
        .reshape(rows, ff)
        .astype(F32)
    )
    own_down = summed_ff[4 * rows :]

    vectors = jnp.stack(
        [
            jnp.sum(d_norm_one * std_one, axis=0),
            jnp.sum(d_norm_one, axis=0),
            jnp.sum(d_norm_two * std_two, axis=0),
            jnp.sum(d_norm_two, axis=0),
        ],
        0,
    )
    bit = n_dev // 2
    while bit:
        h = vectors.shape[1] // 2
        low_half, top_half = vectors[:, :h], vectors[:, h:]
        upper = (lin & bit) != 0
        vectors = jnp.where(upper, top_half, low_half) + permute(
            jnp.where(upper, low_half, top_half), [(i, i ^ bit) for i in range(n_dev)]
        )
        bit //= 2
    return (
        output,
        input_grad,
        own_qkv,
        own_out,
        own_up,
        own_down,
        vectors[0],
        vectors[1],
        vectors[2],
        vectors[3],
    )


def by_rank_order(parts):
    return [parts[0], parts[2], parts[1], parts[3]]


def solution(mesh):
    both = AXES
    vector, matrix, batch = P(both), P(both, None), P(None, both, None)
    return jax.shard_map(
        functools.partial(body, Places(mesh)),
        mesh=mesh,
        in_specs=(batch, P(None, "dp", "fsdp")) + (matrix,) * 4 + (vector,) * 4 + (batch,),
        out_specs=(batch, batch) + (matrix,) * 4 + (vector,) * 4,
        check_vma=False,
    )
```

```python
import functools
import math

import jax
import jax.numpy as jnp
from jax import lax
from jax.experimental import pallas as pl
from jax.experimental.pallas import tpu as pltpu
from jax.sharding import PartitionSpec as P

AXES = ("dp", "fsdp")
HEAD_DIM = 64
EPS = 1e-05
LOWEST = -1000000000.0
F32 = jnp.float32
BF16 = jnp.bfloat16
NT = (((1,), (1,)), ((), ()))
TN = (((0,), (0,)), ((), ()))
NN = (((1,), (0,)), ((), ()))


def dot(left, right, dims):
    return lax.dot_general(left, right, dims, preferred_element_type=F32)


def head_lanes(rows, width, head):
    lane = lax.broadcasted_iota(jnp.int32, (rows, width), 1)
    return (lane >= head * HEAD_DIM) & (lane < (head + 1) * HEAD_DIM)


def attend_kernel(heads, ksc_ref, qsc_ref, q_ref, k_ref, v_ref, mixed_ref, lse_ref, vt_ref):
    @pl.when(pl.program_id(0) == 0)
    def _():
        vt_ref[...] = v_ref[...].astype(F32).T.astype(BF16)

    rows, width = q_ref.shape
    same = ksc_ref[...] == qsc_ref[...]
    q = q_ref[...].astype(F32) * (1.0 / math.sqrt(HEAD_DIM))
    outs = []
    for h in range(heads):
        qh = jnp.where(head_lanes(rows, width, h), q, 0.0).astype(BF16)
        s = jnp.where(same, dot(k_ref[...], qh, NT), LOWEST)
        peak = jnp.max(s, axis=0, keepdims=True)
        e = jnp.exp(s - peak)
        total = jnp.sum(e, axis=0, keepdims=True)
        lse_ref[h : h + 1, :] = peak + jnp.log(total)
        p = (e * (1.0 / total)).astype(BF16)
        outs.append(dot(vt_ref[h * HEAD_DIM : (h + 1) * HEAD_DIM, :], p, NN))
    mixed_ref[...] = jnp.concatenate(outs, axis=0).T.astype(BF16)


def attend_back_kernel(
    heads, ksc_ref, qsc_ref, lse_ref, q_ref, do_ref, k_ref, v_ref, dq_ref, dk_ref, dv_ref, kt_ref, dka_ref, dva_ref
):
    step = pl.program_id(0)

    @pl.when(step == 0)
    def _():
        kt_ref[...] = k_ref[...].astype(F32).T.astype(BF16)
        dka_ref[...] = jnp.zeros_like(dka_ref)
        dva_ref[...] = jnp.zeros_like(dva_ref)

    rows, width = q_ref.shape
    scale = 1.0 / math.sqrt(HEAD_DIM)
    same = ksc_ref[...] == qsc_ref[...]
    q = q_ref[...].astype(F32) * scale
    do = do_ref[...].astype(F32)
    outs = []
    for h in range(heads):
        mine = head_lanes(rows, width, h)
        qh = jnp.where(mine, q, 0.0).astype(BF16)
        doh = jnp.where(mine, do, 0.0).astype(BF16)
        s = jnp.where(same, dot(k_ref[...], qh, NT), LOWEST)
        p = jnp.exp(s - lse_ref[h : h + 1, :])
        dp = dot(v_ref[...], doh, NT)
        inner = jnp.sum(p * dp, axis=0, keepdims=True)
        ds = (p * (dp - inner)).astype(BF16)
        dva_ref[...] += dot(p.astype(BF16), doh, NN)
        dka_ref[...] += dot(ds, qh, NN)
        outs.append(dot(kt_ref[h * HEAD_DIM : (h + 1) * HEAD_DIM, :], ds, NN))
    dq_ref[...] = (jnp.concatenate(outs, axis=0).T * scale).astype(BF16)

    @pl.when(step == pl.num_programs(0) - 1)
    def _():
        dk_ref[...] = dka_ref[...].astype(BF16)
        dv_ref[...] = dva_ref[...].astype(BF16)


VMEM_LIMIT = 56 * 1024 * 1024


def attend(q, k, v, qsc, ksc):
    rows, width = q.shape
    keys = k.shape[0]
    heads = width // HEAD_DIM
    block = 256
    return pl.pallas_call(
        functools.partial(attend_kernel, heads),
        out_shape=(
            jax.ShapeDtypeStruct((rows, width), BF16),
            jax.ShapeDtypeStruct((heads, rows), F32),
        ),
        grid=(rows // block,),
        in_specs=[
            pl.BlockSpec((keys, 1), lambda i: (0, 0)),
            pl.BlockSpec((1, block), lambda i: (0, i)),
            pl.BlockSpec((block, width), lambda i: (i, 0)),
            pl.BlockSpec((keys, width), lambda i: (0, 0)),
            pl.BlockSpec((keys, width), lambda i: (0, 0)),
        ],
        out_specs=(
            pl.BlockSpec((block, width), lambda i: (i, 0)),
            pl.BlockSpec((heads, block), lambda i: (0, i)),
        ),
        scratch_shapes=[pltpu.VMEM((width, keys), BF16)],
        compiler_params=pltpu.CompilerParams(vmem_limit_bytes=VMEM_LIMIT),
        cost_estimate=pl.CostEstimate(
            flops=4 * rows * keys * width, bytes_accessed=8 * rows * width, transcendentals=rows * keys * heads
        ),
        name="attend",
    )(ksc, qsc, q, k, v)


def attend_back(q, k, v, qsc, ksc, lse, do):
    rows, width = q.shape
    keys = k.shape[0]
    heads = width // HEAD_DIM
    block = 256
    row_block = pl.BlockSpec((block, width), lambda i: (i, 0))
    whole = pl.BlockSpec((keys, width), lambda i: (0, 0))
    return pl.pallas_call(
        functools.partial(attend_back_kernel, heads),
        out_shape=(
            jax.ShapeDtypeStruct((rows, width), BF16),
            jax.ShapeDtypeStruct((keys, width), BF16),
            jax.ShapeDtypeStruct((keys, width), BF16),
        ),
        grid=(rows // block,),
        in_specs=[
            pl.BlockSpec((keys, 1), lambda i: (0, 0)),
            pl.BlockSpec((1, block), lambda i: (0, i)),
            pl.BlockSpec((heads, block), lambda i: (0, i)),
            row_block,
            row_block,
            whole,
            whole,
        ],
        out_specs=(row_block, whole, whole),
        scratch_shapes=[
            pltpu.VMEM((width, keys), BF16),
            pltpu.VMEM((keys, width), F32),
            pltpu.VMEM((keys, width), F32),
        ],
        compiler_params=pltpu.CompilerParams(vmem_limit_bytes=VMEM_LIMIT),
        cost_estimate=pl.CostEstimate(
            flops=10 * rows * keys * width, bytes_accessed=14 * rows * width, transcendentals=rows * keys * heads
        ),
        name="attend_back",
    )(ksc, qsc, lse, q, do, k, v)


class Places:
    def __init__(self, mesh):
        self.n_dp, self.n_fsdp = mesh.shape["dp"], mesh.shape["fsdp"]
        self.xs, self.zs = self.n_dp // 2, self.n_fsdp // 2
        self.nodes = self.xs * self.zs
        self.all = [
            (x, c, z, y) for x in range(self.xs) for c in range(2) for z in range(self.zs) for y in range(2)
        ]

    def lin(self, x, c, z, y):
        return (x * 2 + c) * self.n_fsdp + z * 2 + y

    def perm(self, move):
        return [(self.lin(*d), self.lin(*move(*d))) for d in self.all]

    def spot(self, x, z):
        return x * self.zs + (z if x % 2 == 0 else self.zs - 1 - z)

    def node(self, spot):
        x, z = spot // self.zs, spot % self.zs
        return (x, z if x % 2 == 0 else self.zs - 1 - z)

    def ring(self, by):
        def move(x, c, z, y):
            x2, z2 = self.node((self.spot(x, z) + by) % self.nodes)
            return (x2, c, z2, y)

        return self.perm(move)


def permute(array, pairs):
    return lax.ppermute(array, AXES, pairs)


def body(places, tokens, scene_ids, w_qkv, w_out, w_up, w_down, gain_one, bias_one, gain_two, bias_two, cotangent):
    pc = places
    micro, run, width = tokens.shape
    rows = w_qkv.shape[0]
    ff = w_up.shape[1]
    hid = w_down.shape[0]
    quarter = width // 4
    dp, fsdp = lax.axis_index("dp"), lax.axis_index("fsdp")
    x, core, z, y = dp // 2, dp % 2, fsdp // 2, fsdp % 2
    rank = y * 2 + core
    spot = x * pc.zs + jnp.where(x % 2 == 0, z, pc.zs - 1 - z)
    groups = micro * 2
    quads = pc.zs // groups

    p_core = pc.perm(lambda x, c, z, y: (x, 1 - c, z, y))
    p_y = pc.perm(lambda x, c, z, y: (x, c, z, 1 - y))
    p_diag = pc.perm(lambda x, c, z, y: (x, 1 - c, z, 1 - y))
    p_cw, p_ccw = pc.ring(1), pc.ring(-1)

    def place_perm(flip):
        def move(x, c, z, y):
            m = (z % 2) ^ flip
            return (x, (z // 2) % 2, (m * 2 + c) * quads + z // 4, y)

        return pc.perm(move)

    p_place = [place_perm(0), place_perm(1)]
    p_back = [[(b, a) for a, b in pairs] for pairs in p_place]

    def node_of(s):
        nx = s // pc.zs
        nz = s % pc.zs
        return nx, jnp.where(nx % 2 == 0, nz, pc.zs - 1 - nz)

    def quad_gather(a):
        across = permute(a, p_y)
        return [a, permute(a, p_core), across, permute(across, p_core)]

    def quad_swap(parts):
        return [parts[0], permute(parts[1], p_core), permute(parts[2], p_y), permute(parts[3], p_diag)]

    def quad_sum(parts):
        got = permute(jnp.concatenate([parts[1], parts[3]], 0).astype(BF16), p_core).astype(F32)
        half = parts[0].shape[0]
        far = parts[2] + got[half:]
        near = parts[0] + got[:half]
        return near + permute(far.astype(BF16), p_y).astype(F32)

    def by_rank(parts):
        odd, top = rank % 2 == 1, rank // 2 == 1
        parts = [jnp.where(odd, parts[i ^ 1], parts[i]) for i in range(4)]
        return [jnp.where(top, parts[i ^ 2], parts[i]) for i in range(4)]

    half_ring = pc.nodes // 2

    def ring_gather(shard):
        pieces = {0: shard}
        cw = ccw = shard
        for k in range(1, half_ring):
            cw, ccw = permute(cw, p_cw), permute(ccw, p_ccw)
            pieces[-k], pieces[k] = cw, ccw
        h = shard.shape[0] // 2
        pieces[half_ring] = jnp.concatenate([permute(cw[:h], p_cw), permute(ccw[h:], p_ccw)], 0)
        return pieces

    def lay(pieces):
        cols = pieces[0].shape[1]
        out = jnp.zeros((pc.xs, 2, pc.zs, 2 * rows, cols), BF16)
        for k, piece in pieces.items():
            nx, nz = node_of((spot + k) % pc.nodes)
            out = lax.dynamic_update_slice(out, piece.reshape(1, 2, 1, 2 * rows, cols), (nx, 0, nz, 0, 0))
        return out.reshape(width, cols)

    def ring_scatter(arrays):
        def share(s):
            nx, nz = node_of(s % pc.nodes)
            return jnp.concatenate(
                [
                    lax.dynamic_slice(
                        a.reshape(pc.xs, 2, pc.zs, 2 * rows, a.shape[1]),
                        (nx, 0, nz, 0, 0),
                        (1, 2, 1, 2 * rows, a.shape[1]),
                    ).reshape(4 * rows, a.shape[1])
                    for a in arrays
                ],
                1,
            ).astype(F32)

        far = share(spot + half_ring)
        h = 2 * rows
        cw, ccw = permute(far[:h].astype(BF16), p_cw), permute(far[h:].astype(BF16), p_ccw)
        for s in range(1, half_ring):
            one = share(spot + half_ring - s)
            two = share(spot + half_ring + s)
            if s == 1:
                one = jnp.concatenate([one[:h] + cw.astype(F32), one[h:]], 0)
                two = jnp.concatenate([two[:h], two[h:] + ccw.astype(F32)], 0)
            else:
                one, two = one + cw.astype(F32), two + ccw.astype(F32)
            cw, ccw = permute(one.astype(BF16), p_cw), permute(two.astype(BF16), p_ccw)
        return share(spot) + cw.astype(F32) + ccw.astype(F32)

    def pair_up(own, other):
        return jnp.concatenate([jnp.where(core == 0, own, other), jnp.where(core == 0, other, own)], 1)

    half_width = width // 2
    small = jnp.concatenate(
        [jnp.stack([gain_one, bias_one, gain_two, bias_two], 1), scene_ids.astype(BF16).reshape(rows, -1)], 1
    )
    n_small = small.shape[1]
    small = jnp.pad(small, ((0, 0), (0, 128 - n_small)))
    wq = w_qkv.reshape(rows, 3, 4, quarter)
    wo = w_out.reshape(rows, 2, half_width)

    def first_part(p):
        return jnp.concatenate(
            [
                lax.dynamic_index_in_dim(wq, rank ^ p, axis=2, keepdims=False).reshape(rows, 3 * quarter),
                lax.dynamic_index_in_dim(wo, core ^ (p & 1), axis=1, keepdims=False),
                small,
            ],
            1,
        )

    first = lay(
        ring_gather(jnp.concatenate(by_rank_order(by_rank(quad_swap([first_part(p) for p in range(4)]))), 0))
    )
    c_out, c_small = 3 * quarter, 3 * quarter + half_width
    full_qkv = first[:, :c_out]
    near_out = first[:, c_out:c_small]
    full_out = pair_up(near_out, permute(near_out, p_core))
    norms = first[:, c_small : c_small + 4].astype(F32).T
    gone, bone, gtwo, btwo = norms[0:1], norms[1:2], norms[2:3], norms[3:4]
    scenes = (
        first[:, c_small + 4 : c_small + n_small].astype(F32).reshape(pc.xs, 2, pc.zs, 2, micro, run)
    )

    wu = w_up.reshape(rows, pc.xs, 2, pc.zs, 2, 2, hid // 2)

    def up_part(p):
        c2, y2 = core ^ (p & 1), y ^ (p >> 1)
        return (
            lax.dynamic_slice(wu, (0, 0, c2, 0, y2, 0, 0), (rows, pc.xs, 1, pc.zs, 1, 2, hid // 2))
            .reshape(rows, pc.xs, pc.zs, 2, hid // 2)
            .transpose(0, 1, 3, 2, 4)
            .reshape(rows, ff // 4)
        )

    up_shard = jnp.concatenate(by_rank_order(by_rank(quad_swap([up_part(p) for p in range(4)]))), 0)
    second = lay(ring_gather(jnp.concatenate([up_shard, w_down], 1)))
    full_up, full_down = second[:, : ff // 4], second[:, ff // 4 :]

    z_odd = z % 2

    def place(a):
        one = jnp.where(z_odd == 0, a[0], a[1])
        two = jnp.where(z_odd == 0, a[1], a[0])
        return jnp.concatenate([permute(one, p_place[0]), permute(two, p_place[1])], 0)

    def place_back(a):
        one, two = permute(a[:run], p_back[0]), permute(a[run:], p_back[1])
        return jnp.stack([jnp.where(z_odd == 0, one, two), jnp.where(z_odd == 0, two, one)], 0)

    group = z // quads
    my_quad = z % quads
    my_micro = group // 2
    g_scenes = lax.dynamic_slice(
        scenes, (x, group % 2, 0, 0, my_micro, 0), (1, 1, pc.zs, 2, 1, run)
    ).reshape(quads, 2, 2, 2, run)
    g_scenes = jnp.where(core == 1, g_scenes[:, ::-1], g_scenes)
    g_scenes = jnp.where(my_micro == 1, g_scenes[:, :, ::-1], g_scenes)
    g_scenes = jnp.where(y == 1, g_scenes[:, :, :, ::-1], g_scenes)
    g_scenes = g_scenes.transpose(0, 3, 1, 2, 4).reshape(quads, 8 * run)
    q_scenes = lax.dynamic_slice(g_scenes, (my_quad, 0), (1, 8 * run))
    k_scenes = jnp.concatenate(
        [lax.dynamic_slice(g_scenes, ((my_quad - s) % quads, 0), (1, 8 * run)) for s in range(quads)], 1
    ).reshape(quads * 8 * run, 1)

    def standardize(v):
        centered = v - jnp.mean(v, axis=-1, keepdims=True)
        inv = lax.rsqrt(jnp.mean(centered * centered, axis=-1, keepdims=True) + EPS)
        return centered * inv, inv

    def norm_back(d_norm, std, inv, gain):
        d_std = d_norm * gain
        return inv * (
            d_std
            - jnp.mean(d_std, axis=-1, keepdims=True)
            - std * jnp.mean(d_std * std, axis=-1, keepdims=True)
        )

    taken = jnp.concatenate(quad_gather(place(tokens)), 0).astype(F32)
    own_rows = micro * run
    std_one, inv_one = standardize(taken)
    n_one = (std_one * gone + bone).astype(BF16)
    projected = dot(n_one, full_qkv, NN).astype(BF16)
    q, kv = projected[:, :quarter], projected[:, quarter:]

    def group_perm(by):
        return pc.perm(lambda x, c, z, y: (x, c, z // quads * quads + (z + by) % quads, y))

    kv_all = jnp.concatenate([kv] + [permute(kv, group_perm(s)) for s in range(1, quads)], 0)
    k, v = kv_all[:, :quarter], kv_all[:, quarter:]
    mixed, lse = attend(q, k, v, q_scenes, k_scenes)

    def pieces_of(a):
        return [a[i * own_rows : (i + 1) * own_rows] for i in range(4)]

    mixed_own = jnp.concatenate(by_rank(quad_swap(pieces_of(mixed))), 1)
    hidden = taken[:own_rows] + dot(mixed_own, full_out, NN)
    std_two, inv_two = standardize(hidden)
    n_two = jnp.concatenate(quad_gather((std_two * gtwo + btwo).astype(BF16)), 0)
    upward = dot(n_two, full_up, NN)
    cdf = 0.5 * (1.0 + lax.erf(upward * math.sqrt(0.5)))
    activated = (upward * cdf).astype(BF16)
    slope = cdf + upward * jnp.exp(-0.5 * upward * upward) * (1.0 / math.sqrt(2.0 * math.pi))
    dy_own = place(cotangent)
    dy = jnp.concatenate(quad_gather(dy_own), 0)
    d_act = dot(dy, full_down, NT)
    d_up = (d_act * slope).astype(BF16)
    d_norm_two = quad_sum(pieces_of(dot(d_up, full_up, NT)))
    result = hidden + quad_sum(pieces_of(dot(activated, full_down, NN)))
    output = place_back(result.astype(BF16))
    summed_two = ring_scatter([dot(n_two, d_up, TN), dot(activated, dy, TN)])

    d_hidden = dy_own.astype(F32) + norm_back(d_norm_two, std_two, inv_two, gtwo)
    d_hidden_low = d_hidden.astype(BF16)
    d_mixed_own = dot(d_hidden_low, full_out, NT).astype(BF16)
    d_cols = by_rank([d_mixed_own[:, i * quarter : (i + 1) * quarter] for i in range(4)])
    d_mixed = jnp.concatenate(quad_swap(d_cols), 0)
    dq, dk, dv = attend_back(q, k, v, q_scenes, k_scenes, lse, d_mixed)
    dkv = jnp.concatenate([dk, dv], 1)
    n_rows = dkv.shape[0] // quads
    if quads > 1:
        total = dkv[:n_rows].astype(F32)
        for s in range(1, quads):
            total = total + permute(dkv[s * n_rows : (s + 1) * n_rows], group_perm(-s)).astype(F32)
        dkv = total.astype(BF16)
    d_projected = jnp.concatenate([dq, dkv], 1)
    d_norm_one_part = dot(d_projected, full_qkv, NT)
    d_norm_one = quad_sum(pieces_of(d_norm_one_part))
    grad_qkv = dot(n_one, d_projected, TN)
    low_halves = d_hidden_low.reshape(own_rows, 2, half_width)
    near, far = (
        dot(mixed_own, lax.dynamic_index_in_dim(low_halves, c, axis=1, keepdims=False), TN)
        for c in (core, 1 - core)
    )
    grad_out = near + permute(far.astype(BF16), p_core).astype(F32)
    vectors = jnp.stack(
        [
            jnp.sum(d_norm_one_part * std_one, axis=0),
            jnp.sum(d_norm_one_part, axis=0),
            jnp.sum(d_norm_two * std_two, axis=0),
            jnp.sum(d_norm_two, axis=0),
        ],
        1,
    )
    summed_one = ring_scatter([grad_qkv, grad_out, jnp.pad(vectors, ((0, 0), (0, 124)))])

    d_tokens = d_hidden + norm_back(d_norm_one, std_one[:own_rows], inv_one[:own_rows], gone)
    input_grad = place_back(d_tokens.astype(BF16)).astype(F32)

    def home(summed):
        blocks = by_rank(by_rank_order([summed[i * rows : (i + 1) * rows].astype(BF16) for i in range(4)]))
        return by_rank(quad_swap(blocks))

    ones = home(summed_one)
    own_qkv = jnp.stack([b[:, :c_out].reshape(rows, 3, quarter) for b in ones], 2).reshape(rows, 3 * width)
    wide = [b[:, c_out:].astype(F32) for b in ones]
    own_out = jnp.concatenate([wide[c][:, :half_width] + wide[2 + c][:, :half_width] for c in range(2)], 1)
    vectors = (wide[0] + wide[1] + wide[2] + wide[3])[:, half_width : half_width + 4].T
    ups = [
        b.reshape(rows, pc.xs, 2, pc.zs, hid // 2).transpose(0, 1, 3, 2, 4).reshape(rows, pc.xs, pc.zs, hid)
        for b in home(summed_two[:, : ff // 4])
    ]
    own_up = jnp.stack(
        [jnp.stack([ups[0], ups[2]], 3), jnp.stack([ups[1], ups[3]], 3)], 2
    ).reshape(rows, ff)
    own_down = summed_two[:, ff // 4 :]
    return (
        output,
        input_grad,
        own_qkv.astype(F32),
        own_out,
        own_up.astype(F32),
        own_down,
        vectors[0],
        vectors[1],
        vectors[2],
        vectors[3],
    )


def by_rank_order(parts):
    return [parts[0], parts[2], parts[1], parts[3]]


def solution(mesh):
    both = AXES
    vector, matrix, batch = P(both), P(both, None), P(None, both, None)
    return jax.shard_map(
        functools.partial(body, Places(mesh)),
        mesh=mesh,
        in_specs=(batch, P(None, "dp", "fsdp")) + (matrix,) * 4 + (vector,) * 4 + (batch,),
        out_specs=(batch, batch) + (matrix,) * 4 + (vector,) * 4,
        check_vma=False,
    )
```

```python
import functools
import math

import jax
import jax.numpy as jnp
from jax import lax
from jax.experimental import pallas as pl
from jax.experimental.pallas import tpu as pltpu
from jax.sharding import PartitionSpec as P

AXES = ("dp", "fsdp")
HEAD_DIM = 64
EPS = 1e-05
LOWEST = -1000000000.0
F32 = jnp.float32
BF16 = jnp.bfloat16
NT = (((1,), (1,)), ((), ()))
TN = (((0,), (0,)), ((), ()))
NN = (((1,), (0,)), ((), ()))
VMEM_LIMIT = 58 * 1024 * 1024
HINTS = {"grad_up": 0, "hidden_units": 8, "hidden_back": 300, "attend_back": 12, "grad_down": 8, "project_back": 50}


def dot(left, right, dims):
    return lax.dot_general(left, right, dims, preferred_element_type=F32)


def at(start, size, step):
    return pl.ds(pl.multiple_of(start, step), size)


def call(kernel, name, args, outs, scratch=(), grid=None, flops=0, transcendentals=0, in_specs=None, out_specs=None):
    whole = pl.BlockSpec(memory_space=pltpu.VMEM) if grid is None else None

    def spec(shape):
        return whole or pl.BlockSpec(shape, lambda i, n=len(shape): (0,) * n)

    specs = [pl.BlockSpec(memory_space=pltpu.SMEM)]
    specs += [(in_specs or {}).get(n) or spec(a.shape) for n, a in enumerate(args[1:])]
    size = sum(math.prod(a.shape) * a.dtype.itemsize for a in list(args) + list(outs))
    return pl.pallas_call(
        kernel,
        out_shape=tuple(outs),
        in_specs=specs,
        out_specs=tuple((out_specs or {}).get(n) or spec(o.shape) for n, o in enumerate(outs)),
        scratch_shapes=list(scratch),
        compiler_params=pltpu.CompilerParams(vmem_limit_bytes=VMEM_LIMIT),
        cost_estimate=pl.CostEstimate(
            flops=HINTS.get(name, 8) * flops, bytes_accessed=HINTS.get(name, 8) * size, transcendentals=transcendentals
        ),
        name=name,
        **({} if grid is None else {"grid": grid}),
    )(*args)


def shape_of(shape, dtype=BF16):
    return jax.ShapeDtypeStruct(shape, dtype)


def centre(v):
    c = v - jnp.mean(v, axis=-1, keepdims=True)
    inv = lax.rsqrt(jnp.mean(c * c, axis=-1, keepdims=True) + EPS)
    return c * inv, inv


def norm_back(d_norm, std, inv, gain):
    d_std = d_norm * gain
    return inv * (
        d_std - jnp.mean(d_std, axis=-1, keepdims=True) - std * jnp.mean(d_std * std, axis=-1, keepdims=True)
    )


def pack_kernel(aligned, spots, ix, qkv, out, gains, tokens, scenes, dy, up, *refs):
    parts, ups, (one, two, dy_one, dy_two, tile) = refs[:4], refs[4:8], refs[8:]
    rank, core, odd, y = ix[0], ix[1], ix[2], ix[3]
    rows, width = qkv.shape[0], out.shape[1]
    quarter, half = width // 4, width // 2
    tile[...] = jnp.zeros_like(tile)
    tile[0:4, 0:rows] = gains[...].astype(F32)
    small = tile[...].T[:rows].astype(BF16)
    c1, c2 = 3 * quarter, 3 * quarter + half
    hid, units = 128, up.shape[1] // 4
    zs = len(spots) // 2
    for p in range(4):
        a = rank ^ p
        for t in range(3):
            parts[p][:, t * quarter : (t + 1) * quarter] = qkv[:, at(t * width + a * quarter, quarter, 128)]
        parts[p][:, c1:c2] = out[:, at((core ^ (p & 1)) * half, half, 128)]
        parts[p][:, c2 : c2 + 128] = small
        if aligned:
            for b, (nx, nz) in enumerate(spots):
                src = ((nx * 2 + (core ^ (p & 1))) * zs + nz) * 2 + (y ^ (p >> 1))
                ups[p][:, b * hid : (b + 1) * hid] = up[:, at(src * hid, hid, 128)]
        else:
            ups[p][...] = up[:, p * units : (p + 1) * units]
    run = tokens.shape[1]
    for ref, low, m in ((one, dy_one, odd), (two, dy_two, 1 - odd)):
        ref[0:run, :] = tokens[m]
        ref[run:, :] = jnp.zeros((ref.shape[0] - run, width), BF16)
        ref[run : run + 1, 0:run] = scenes[pl.ds(m, 1), :].astype(F32).astype(BF16)
        low[...] = dy[m]


def row_blocks(spots, size):
    zs = len(spots) // 2
    return [
        ((2 * i + c) * size, ((nx * 2 + c) * zs + nz) * size, size) for i, (nx, nz) in enumerate(spots) for c in (0, 1)
    ]


def project_kernel(blocks, run, ix, *refs):
    taken, first = refs[:4], refs[4]
    n_ref, p_ref, w_ref, near_ref, gains_ref, scene_ref, g_all = refs[5:]
    step = pl.program_id(0)
    c_out, c_small = w_ref.shape[1], w_ref.shape[1] + near_ref.shape[1]

    @pl.when(step == 0)
    def _():
        for src, dst, size in blocks:
            v = first[src : src + size, :]
            w_ref[dst : dst + size, :] = v[:, :c_out]
            near_ref[dst : dst + size, :] = v[:, c_out:c_small]
            g_all[dst : dst + size, :] = v[:, c_small:].astype(F32)
        gains_ref[...] = g_all[...].T[0:8, :]
        for p in range(4):
            for s in range(2):
                row = taken[p][s * (run + 8) + run : s * (run + 8) + run + 1, 0:run]
                scene_ref[0:1, (2 * p + s) * run : (2 * p + s + 1) * run] = row.astype(F32)

    for p in range(4):

        @pl.when(step == p)
        def _():
            x = taken[p]
            v = jnp.concatenate([x[0:run, :], x[run + 8 : 2 * run + 8, :]], 0).astype(F32)
            std, _ = centre(v)
            n = (std * gains_ref[0:1, :] + gains_ref[1:2, :]).astype(BF16)
            n_ref[...] = n
            p_ref[...] = dot(n, w_ref[...], NN).astype(BF16)


def head_lanes(rows, width, head):
    lane = lax.broadcasted_iota(jnp.int32, (rows, width), 1)
    return (lane >= head * HEAD_DIM) & (lane < (head + 1) * HEAD_DIM)


def column(row):
    return jnp.broadcast_to(row, (128, row.shape[1])).T


def same_scene(ksc, qrow):
    return jnp.concatenate([ksc == qrow[:, i : i + 128] for i in range(0, qrow.shape[1], 128)], 1)


def attend_kernel(heads, ix, krow_ref, qrow_ref, q_ref, k_ref, v_ref, *refs):
    outs_ref, (lse_ref, vt_ref, ksc_ref) = refs[:2], refs[2:]
    step = pl.program_id(0)

    @pl.when(step == 0)
    def _():
        vt_ref[...] = v_ref[...].astype(F32).T.astype(BF16)
        ksc_ref[...] = column(krow_ref[...])

    rows, width = q_ref.shape
    same = same_scene(ksc_ref[...], qrow_ref[...])
    q = q_ref[...].astype(F32) * (1.0 / math.sqrt(HEAD_DIM))
    outs = []
    for h in range(heads):
        qh = jnp.where(head_lanes(rows, width, h), q, 0.0).astype(BF16)
        s = jnp.where(same, dot(k_ref[...], qh, NT), LOWEST)
        peak = jnp.max(s, axis=0, keepdims=True)
        e = jnp.exp(s - peak)
        total = jnp.sum(e, axis=0, keepdims=True)
        lse_ref[h : h + 1, :] = peak + jnp.log(total)
        p = (e * (1.0 / total)).astype(BF16)
        outs.append(dot(vt_ref[h * HEAD_DIM : (h + 1) * HEAD_DIM, :], p, NN))
    mixed = jnp.concatenate(outs, axis=0).T.astype(BF16)
    for i in range(2):

        @pl.when(step == i)
        def _():
            outs_ref[i][...] = mixed


def attend(ix, q, k, v, quarter, qrow, krow, first):
    rows, keys = q[0].shape[0], k[0].shape[0]
    heads, block = quarter // HEAD_DIM, rows // 4
    return call(
        functools.partial(attend_kernel, heads),
        "attend",
        (ix, krow, qrow, q[0], k[0], v[0]),
        [shape_of((block, quarter))] * 2 + [shape_of((heads, 2 * block), F32)],
        scratch=[pltpu.VMEM((quarter, keys), BF16), pltpu.VMEM((keys, 128), F32)],
        grid=(2,),
        flops=2 * rows * keys * quarter,
        transcendentals=rows * keys * heads // 2,
        in_specs={
            1: pl.BlockSpec((1, block), lambda i: (0, i + first)),
            2: pl.BlockSpec((block, quarter), lambda i, c=q[1]: (i + first, c)),
            3: pl.BlockSpec((keys, quarter), lambda i, c=k[1]: (0, c)),
            4: pl.BlockSpec((keys, quarter), lambda i, c=v[1]: (0, c)),
        },
        out_specs={2: pl.BlockSpec((heads, block), lambda i: (0, i))},
    )


def attend_back_kernel(heads, more, ix, krow_ref, qrow_ref, lse_ref, q_ref, k_ref, v_ref, *refs):
    do_refs, kept, refs = refs[:2], refs[2 : 2 + more], refs[2 + more :]
    dq_ref, dkv_ref, kt_ref, ksc_ref, dka_ref, dva_ref, do_ref = refs
    width = q_ref.shape[1]
    step = pl.program_id(0)

    @pl.when(step == 0)
    def _():
        kt_ref[...] = k_ref[...].astype(F32).T.astype(BF16)
        ksc_ref[...] = column(krow_ref[...])
        if more:
            dka_ref[...] = kept[0][:, :width]
            dva_ref[...] = kept[0][:, width:]
        else:
            dka_ref[...] = jnp.zeros_like(dka_ref)
            dva_ref[...] = jnp.zeros_like(dva_ref)

    for i in range(2):

        @pl.when(step == i)
        def _():
            do_ref[...] = do_refs[i][...].astype(F32)

    rows, width = q_ref.shape
    scale = 1.0 / math.sqrt(HEAD_DIM)
    same = same_scene(ksc_ref[...], qrow_ref[...])
    q = q_ref[...].astype(F32) * scale
    do = do_ref[...]
    outs = []
    for h in range(heads):
        mine = head_lanes(rows, width, h)
        qh = jnp.where(mine, q, 0.0).astype(BF16)
        doh = jnp.where(mine, do, 0.0).astype(BF16)
        s = jnp.where(same, dot(k_ref[...], qh, NT), LOWEST)
        p = jnp.exp(s - lse_ref[h : h + 1, :])
        dp = dot(v_ref[...], doh, NT)
        inner = jnp.sum(p * dp, axis=0, keepdims=True)
        ds = (p * (dp - inner)).astype(BF16)
        dva_ref[...] += dot(p.astype(BF16), doh, NN)
        dka_ref[...] += dot(ds, qh, NN)
        outs.append(dot(kt_ref[h * HEAD_DIM : (h + 1) * HEAD_DIM, :], ds, NN))
    dq_ref[...] = (jnp.concatenate(outs, axis=0).T * scale).astype(BF16)

    @pl.when(step == pl.num_programs(0) - 1)
    def _():
        dkv_ref[:, :width] = dka_ref[...].astype(dkv_ref.dtype)
        dkv_ref[:, width:] = dva_ref[...].astype(dkv_ref.dtype)


def attend_back(ix, q, k, v, quarter, qrow, krow, lse, do, first, kept):
    rows, keys = q[0].shape[0], k[0].shape[0]
    heads, block = quarter // HEAD_DIM, rows // 4
    return call(
        functools.partial(attend_back_kernel, heads, len(kept)),
        "attend_back",
        (ix, krow, qrow, lse, q[0], k[0], v[0], *do, *kept),
        [shape_of((2 * block, quarter)), shape_of((keys, 2 * quarter), BF16 if kept else F32)],
        scratch=[
            pltpu.VMEM((quarter, keys), BF16),
            pltpu.VMEM((keys, 128), F32),
            pltpu.VMEM((keys, quarter), F32),
            pltpu.VMEM((keys, quarter), F32),
            pltpu.VMEM((block, quarter), F32),
        ],
        grid=(2,),
        flops=5 * rows * keys * quarter,
        transcendentals=rows * keys * heads // 2,
        in_specs={
            1: pl.BlockSpec((1, block), lambda i: (0, i + first)),
            2: pl.BlockSpec((heads, block), lambda i: (0, i)),
            3: pl.BlockSpec((block, quarter), lambda i, c=q[1]: (i + first, c)),
            4: pl.BlockSpec((keys, quarter), lambda i, c=k[1]: (0, c)),
            5: pl.BlockSpec((keys, quarter), lambda i, c=v[1]: (0, c)),
        },
        out_specs={0: pl.BlockSpec((block, quarter), lambda i: (i, 0))},
    )


def mix_out_kernel(run, ix, m0, m1, m2, m3, near, far, x, gains, mixed_ref, hidden_ref, n_ref):
    rank, core = ix[0], ix[1]
    quarter, half = m0.shape[1], near.shape[1]
    for p, m in enumerate((m0, m1, m2, m3)):
        mixed_ref[:, at((rank ^ p) * quarter, quarter, 128)] = m[...]
    mixed = mixed_ref[...]
    hidden_ref[0:run, :] = x[0:run, :].astype(F32)
    hidden_ref[run:, :] = x[run + 8 : 2 * run + 8, :].astype(F32)
    hidden_ref[:, at(core * half, half, 128)] += dot(mixed, near[...], NN)
    hidden_ref[:, at((1 - core) * half, half, 128)] += dot(mixed, far[...], NN)
    std, _ = centre(hidden_ref[...])
    n_ref[...] = (std * gains[2:3, :] + gains[3:4, :]).astype(BF16)


def hidden_units_kernel(parts, blocks, ix, *refs):
    n, rows = len(parts), refs[0].shape[0]
    norms, dys, refs = refs[:n], refs[n : 2 * n], refs[2 * n :]
    if blocks:
        second, act_ref, dup_ref, *term_refs, up_ref, down_ref = refs
        units = up_ref.shape[1]
        for src, dst, size in blocks:
            up_ref[dst : dst + size, :] = second[src : src + size, :units]
        down_ref[...] = second[:, units:]
    else:
        up_ref, down_ref, act_ref, dup_ref, *term_refs = refs
    for i in range(n):
        span = slice(i * rows, (i + 1) * rows)
        u = dot(norms[i][...], up_ref[...], NN)
        cdf = 0.5 * (1.0 + lax.erf(u * math.sqrt(0.5)))
        act_ref[span, :] = (u * cdf).astype(BF16)
        slope = cdf + u * jnp.exp(-0.5 * u * u) * (1.0 / math.sqrt(2.0 * math.pi))
        dup = (dot(dys[i][...], down_ref[...], NT) * slope).astype(BF16)
        dup_ref[span, :] = dup
        term_refs[i][...] = dot(dup, up_ref[...], NT).astype(term_refs[i].dtype)


def hidden_back_kernel(ix, keep, got, across, hidden, dy, gains, near, far, *refs):
    parts, (dh_ref, low_ref, sums_ref) = refs[:4], refs[4:]
    rank, core = ix[0], ix[1]
    rows = hidden.shape[0]
    half, quarter = near.shape[1], parts[0].shape[1]
    d_norm = keep[...] + got[...].astype(F32) + across[...].astype(F32)
    std, inv = centre(hidden[...])
    sums_ref[...] = jnp.zeros_like(sums_ref)
    sums_ref[2:3, :] = jnp.sum(d_norm * std, axis=0, keepdims=True)
    sums_ref[3:4, :] = jnp.sum(d_norm, axis=0, keepdims=True)
    d_hidden = dy[...].astype(F32) + norm_back(d_norm, std, inv, gains[2:3, :])
    dh_ref[...] = d_hidden
    low_ref[...] = d_hidden.astype(BF16)
    a, b = low_ref[:, at(core * half, half, 128)], low_ref[:, at((1 - core) * half, half, 128)]
    for p in range(4):
        rows_p = at((rank ^ p) * quarter, quarter, 16)
        parts[p][...] = (dot(a, near[rows_p, :], NT) + dot(b, far[rows_p, :], NT)).astype(BF16)


def out_grad_kernel(ix, mixed, low, near_ref, far_ref):
    core, half = ix[1], near_ref.shape[1]
    left = mixed[...].astype(F32).T.astype(BF16)
    near_ref[...] = dot(left, low[:, at(core * half, half, 128)], NN)
    far_ref[...] = dot(left, low[:, at((1 - core) * half, half, 128)], NN).astype(BF16)


def project_back_kernel(run, ix, *refs):
    taken, (dq_a, dq_b, dkv, w, sums2, keep_ref, give_ref, cols_ref, sums) = refs[:4], refs[4:]
    step = pl.program_id(0)
    quarter, rows = dq_a.shape[1], dkv.shape[0]

    @pl.when(step == 0)
    def _():
        sums[...] = jnp.zeros_like(sums)
        sums[0:8, :] = sums2[...]

    for i, p in enumerate((1, 3, 0, 2)):

        @pl.when(step == i)
        def _():
            x = taken[p]
            std, _ = centre(jnp.concatenate([x[0:run, :], x[run + 8 : 2 * run + 8, :]], 0).astype(F32))
            dq = (dq_a, dq_b)[p >> 1][(p & 1) * rows : ((p & 1) + 1) * rows, :]
            part = dot(dq, w[:, 0:quarter], NT) + dot(dkv[...], w[:, quarter:], NT)
            sums[0:1, :] += jnp.sum(part * std, axis=0, keepdims=True)
            sums[1:2, :] += jnp.sum(part, axis=0, keepdims=True)
            if p & 1:
                give_ref[(p >> 1) * rows : ((p >> 1) + 1) * rows, :] = part.astype(BF16)
            else:
                keep_ref[(p >> 1) * rows : ((p >> 1) + 1) * rows, :] = part

    @pl.when(step == 3)
    def _():
        cols_ref[...] = sums[...].T.astype(BF16)


def tokens_back_kernel(run, ix, keep, got, across, x, d_hidden, gains, one_ref, two_ref):
    rows = d_hidden.shape[0]
    d_norm = keep[0:rows, :] + got[0:rows, :].astype(F32) + across[...].astype(F32)
    std, inv = centre(jnp.concatenate([x[0:run, :], x[run + 8 : 2 * run + 8, :]], 0).astype(F32))
    d = (d_hidden[...] + norm_back(d_norm, std, inv, gains[0:1, :])).astype(BF16)
    one_ref[...] = d[0:run]
    two_ref[...] = d[run:]


def down_kernel(ix, act3, act2, act10, down, keep_ref, give_ref):
    rows = act3.shape[0]
    give_ref[rows:, :] = dot(act3[...], down[...], NN).astype(BF16)
    keep_ref[rows:, :] = dot(act2[...], down[...], NN)
    give_ref[0:rows, :] = dot(act10[0:rows, :], down[...], NN).astype(BF16)
    keep_ref[0:rows, :] = dot(act10[rows:, :], down[...], NN)


def grads_kernel(blocks, n_left, widths, n_right, extra, ix, *refs):
    lefts, refs = refs[:n_left], refs[n_left:]
    rights, refs = [refs[i * n_right : (i + 1) * n_right] for i in range(len(widths))], refs[len(widths) * n_right :]
    out_ref, left_t, *right_refs = refs[extra:]
    step = pl.program_id(0)
    cols = sum(widths)

    @pl.when(step == 0)
    def _():
        at_col = 0
        for piece in lefts:
            t = piece[...].T
            stop = at_col + t.shape[1]
            for dst, src, size in blocks:
                left_t[dst : dst + size, at_col:stop] = t[src : src + size, :]
            at_col = stop
        for pieces, ref in zip(rights, right_refs):
            row = 0
            for piece in pieces:
                ref[row : row + piece.shape[0], :] = piece[...]
                row += piece.shape[0]

    rows = out_ref.shape[0]
    mine = left_t[at(step * rows, rows, 16), :]
    start = 0
    for ref, w in zip(right_refs, widths):
        out_ref[:, start : start + w] = dot(mine, ref[...], NN).astype(BF16)
        start += w
    if extra:
        near, far, columns = refs[:3]
        half = near.shape[1]
        for i in range(left_t.shape[0] // rows):

            @pl.when(step == i)
            def _():
                for dst, src, size in blocks:
                    if i * rows <= dst < (i + 1) * rows:
                        span = slice(dst - i * rows, dst - i * rows + size)
                        both = near[src : src + size, :] + far[src : src + size, :].astype(F32)
                        out_ref[span, cols : cols + half] = both.astype(BF16)
                        out_ref[span, cols + half :] = columns[src : src + size, :]


def home_kernel(ix, summed, *parts):
    core, y = ix[1], ix[3]
    rows, cols = parts[0].shape
    for p in range(4):
        block = (core ^ (p & 1)) * 2 + (y ^ (p >> 1))
        parts[p][...] = summed[at(block * rows, rows, 8), 0:cols]


def settle_kernel(ix, p0, p1, p2, p3, qkv_ref, out_ref, vec_ref, tile):
    rank, core = ix[0], ix[1]
    parts = (p0, p1, p2, p3)
    rows, width = out_ref.shape
    quarter, half = width // 4, width // 2
    for p in range(4):
        a = rank ^ p
        for t in range(3):
            qkv_ref[:, at(t * width + a * quarter, quarter, 128)] = parts[p][:, t * quarter : (t + 1) * quarter].astype(F32)
    c1, c2 = 3 * quarter, 3 * quarter + half
    for p in range(2):
        out_ref[:, at((core ^ p) * half, half, 128)] = parts[p][:, c1:c2].astype(F32) + parts[p + 2][:, c1:c2].astype(F32)
    tile[...] = jnp.zeros_like(tile)
    tile[0:rows, :] = sum(v[:, c2:].astype(F32) for v in parts)
    vec_ref[...] = tile[...].T[0:8, :]


def settle_ff_kernel(spots, ix, p0, p1, p2, p3, up_ref):
    core, y = ix[1], ix[3]
    hid, zs = 128, len(spots) // 2
    for p, part in enumerate((p0, p1, p2, p3)):
        c2, y2 = core ^ (p & 1), y ^ (p >> 1)
        for b, (nx, nz) in enumerate(spots):
            dst = ((nx * 2 + c2) * zs + nz) * 2 + y2
            up_ref[:, at(dst * hid, hid, 128)] = part[:, b * hid : (b + 1) * hid].astype(F32)


class Places:
    def __init__(self, mesh):
        self.n_dp, self.n_fsdp = mesh.shape["dp"], mesh.shape["fsdp"]
        self.xs, self.zs = self.n_dp // 2, self.n_fsdp // 2
        self.nodes = self.xs * self.zs
        self.all = [
            (x, c, z, y) for x in range(self.xs) for c in range(2) for z in range(self.zs) for y in range(2)
        ]

    def lin(self, x, c, z, y):
        return (x * 2 + c) * self.n_fsdp + z * 2 + y

    def perm(self, move):
        return [(self.lin(*d), self.lin(*move(*d))) for d in self.all]

    def spot(self, x, z):
        return x * self.zs + (z if x % 2 == 0 else self.zs - 1 - z)

    def node(self, spot):
        x, z = spot // self.zs, spot % self.zs
        return (x, z if x % 2 == 0 else self.zs - 1 - z)

    def rings(self):
        return [
            [self.lin(x, c, z, y) for x, z in map(self.node, range(self.nodes))] for c in range(2) for y in range(2)
        ]


def permute(array, pairs):
    return lax.ppermute(array, AXES, pairs)


def after(value, *done):
    return lax.optimization_barrier((value,) + done)[0]


def body(pc, tokens, scene_ids, w_qkv, w_out, w_up, w_down, gain_one, bias_one, gain_two, bias_two, cotangent):
    micro, run, width = tokens.shape
    rows = w_qkv.shape[0]
    ff = w_up.shape[1]
    units = ff // 4
    hid = w_down.shape[0]
    quarter, half = width // 4, width // 2
    own = micro * run
    dp, fsdp = lax.axis_index("dp"), lax.axis_index("fsdp")
    x, core, z, y = dp // 2, dp % 2, fsdp // 2, fsdp % 2
    rank = y * 2 + core
    groups = micro * 2
    quads = pc.zs // groups
    rings = pc.rings()
    spots = [pc.node(i) for i in range(pc.nodes)]
    blocks = row_blocks(spots, 2 * rows)
    aligned = hid % 128 == 0

    p_core = pc.perm(lambda x, c, z, y: (x, 1 - c, z, y))
    p_y = pc.perm(lambda x, c, z, y: (x, c, z, 1 - y))
    p_diag = pc.perm(lambda x, c, z, y: (x, 1 - c, z, 1 - y))

    def place_perm(flip):
        def move(x, c, z, y):
            m = (z % 2) ^ flip
            return (x, (z // 2) % 2, (m * 2 + c) * quads + z // 4, y)

        return pc.perm(move)

    p_place = [place_perm(0), place_perm(1)]
    p_back = [[(b, a) for a, b in pairs] for pairs in p_place]

    def group_perm(by):
        return pc.perm(lambda x, c, z, y: (x, c, z // quads * quads + (z + by) % quads, y))

    ix = jnp.stack([rank, core, z % 2, y]).astype(jnp.int32)

    def quad_swap(parts):
        return [parts[0], permute(parts[1], p_core), permute(parts[2], p_y), permute(parts[3], p_diag)]

    def by_rank(parts):
        odd, top = rank % 2 == 1, rank // 2 == 1
        parts = [jnp.where(odd, parts[i ^ 1], parts[i]) for i in range(4)]
        return [jnp.where(top, parts[i ^ 2], parts[i]) for i in range(4)]

    def by_rows(parts):
        r = by_rank(parts)
        return jnp.concatenate([r[0], r[2], r[1], r[3]], 0)

    def ring_gather(shard):
        return lax.all_gather(shard, AXES, axis=0, tiled=True, axis_index_groups=rings)

    def ring_sum(terms):
        return lax.psum_scatter(terms, AXES, scatter_dimension=0, tiled=True, axis_index_groups=rings)

    c_out, c_small, wide = 3 * quarter, 3 * quarter + half, 3 * quarter + half + 128
    wu = w_up
    if not aligned:
        wu = w_up.reshape(rows, pc.xs, 2, pc.zs, 2, hid)
        wu = [
            lax.dynamic_slice(
                wu, (0, 0, core ^ (p & 1), 0, y ^ (p >> 1), 0), (rows, pc.xs, 1, pc.zs, 1, hid)
            ).reshape(rows, pc.xs, pc.zs, hid)
            for p in range(4)
        ]
        wu = jnp.concatenate([w[:, nx, nz] for w in wu for nx, nz in spots], 1)
    *packed, x_one, x_two, dy_one, dy_two = call(
        functools.partial(pack_kernel, aligned, spots),
        "pack",
        (
            ix,
            w_qkv,
            w_out,
            jnp.stack([gain_one, bias_one, gain_two, bias_two]),
            tokens,
            scene_ids.reshape(micro, run),
            cotangent,
            wu,
        ),
        [shape_of((rows, wide))] * 4 + [shape_of((rows, units))] * 4 + [shape_of((run + 8, width))] * 2 + [shape_of((run, width))] * 2,
        scratch=[pltpu.VMEM((128, 128), F32)],
    )
    shard = by_rows(quad_swap(packed[:4]))
    x_own = jnp.concatenate([permute(x_one, p_place[0]), permute(x_two, p_place[1])], 0)
    first = ring_gather(after(shard, x_own))
    x_across = permute(x_own, p_y)
    taken = [x_own, permute(x_own, p_core), x_across, permute(x_across, p_core)]
    up_shard = by_rows(quad_swap(after(packed[4:], x_across)))
    second = ring_gather(after(jnp.concatenate([up_shard, w_down], 1), taken))
    dy_one, dy_two = after((dy_one, dy_two), first)
    dy_own = jnp.concatenate([permute(dy_one, p_place[0]), permute(dy_two, p_place[1])], 0)

    block = (own, width)
    n_one, projected, full_qkv, near_out, gains, qrow = call(
        functools.partial(project_kernel, blocks, run),
        "project",
        (ix, *taken, first),
        [
            shape_of((4 * own, width)),
            shape_of((4 * own, 3 * quarter)),
            shape_of((width, 3 * quarter)),
            shape_of((width, half)),
            shape_of((8, width), F32),
            shape_of((1, 4 * own), F32),
        ],
        scratch=[pltpu.VMEM((width, 128), F32)],
        grid=(4,),
        flops=2 * 4 * own * width * 3 * quarter,
        out_specs={
            0: pl.BlockSpec(block, lambda i: (i, 0)),
            1: pl.BlockSpec((own, 3 * quarter), lambda i: (i, 0)),
        },
    )
    far_out = permute(near_out, p_core)
    if quads == 1:
        q, k, v, krow = (projected, 0), (projected, 1), (projected, 2), qrow
    else:
        kv = projected[:, quarter:]
        kv_all = jnp.concatenate([kv] + [permute(kv, group_perm(s)) for s in range(1, quads)], 0)
        krow = jnp.concatenate([qrow] + [permute(qrow, group_perm(s)) for s in range(1, quads)], 1)
        q, k, v = (projected, 0), (kv_all, 0), (kv_all, 1)
    *m_far, lse_far = attend(ix, q, k, v, quarter, qrow, krow, 2)
    dy_across = permute(after(dy_own, m_far), p_y)
    *m_near, lse_near = attend(ix, q, k, v, quarter, after(qrow, m_far, dy_own), krow, 0)
    mixed = quad_swap([*m_near, *m_far])
    mixed_own, hidden, n_two = call(
        functools.partial(mix_out_kernel, run),
        "mix_out",
        (ix, *mixed, near_out, far_out, taken[0], after(gains, dy_across)),
        [shape_of(block), shape_of(block, F32), shape_of(block)],
        flops=2 * own * width * width,
    )
    def far_sum(keep, got):
        return (keep + got.astype(F32)).astype(BF16)

    n_across = permute(n_two, p_y)
    norms = [n_two, permute(n_two, p_core), n_across, permute(n_across, p_core)]
    dys = [dy_own, permute(dy_own, p_core), dy_across, permute(dy_across, p_core)]

    def hidden_units(parts, weights, kinds, order):
        outs = [shape_of((len(parts) * own, units))] * 2 + [shape_of(block, kind) for kind in kinds]
        return call(
            functools.partial(hidden_units_kernel, parts, order),
            "hidden_units",
            (ix, *[norms[p] for p in parts], *[dys[p] for p in parts], *weights),
            outs + ([shape_of((width, units)), shape_of((units, width))] if order else []),
            flops=6 * len(parts) * own * width * units,
            transcendentals=2 * len(parts) * own * units,
        )

    act3, up3, give3, full_up, full_down = hidden_units((3,), (second,), (BF16,), blocks)
    got3 = permute(give3, p_core)
    act2, up2, keep2 = hidden_units((2,), (after(full_up, give3), full_down), (F32,), None)
    far = far_sum(keep2, got3)
    across = permute(far, p_y)
    act10, up10, give1, keep0 = hidden_units((1, 0), (after(full_up, far), full_down), (BF16, F32), None)
    got = permute(give1, p_core)
    in_order = [(i, i, n) for i, _, n in blocks]

    def grads(name, lefts, rights, order, extra=()):
        widths = tuple(r[0].shape[1] for r in rights)
        depth, cols = sum(a.shape[0] for a in lefts), sum(widths)
        height = lefts[0].shape[1]
        total = cols + sum(e.shape[1] for e in extra[1:])
        return call(
            functools.partial(grads_kernel, order, len(lefts), widths, len(rights[0]), len(extra)),
            name,
            (ix, *lefts, *[piece for r in rights for piece in r], *extra),
            [shape_of((height, total))],
            scratch=[pltpu.VMEM((height, depth), BF16)] + [pltpu.VMEM((depth, w), BF16) for w in widths],
            grid=(4,),
            flops=2 * depth * height * cols,
            out_specs={0: pl.BlockSpec((height // 4, total), lambda i: (i, 0))},
        )[0]

    order = (3, 2, 1, 0)
    up_terms = grads("grad_up", [norms[p] for p in order], [[up3, up2, up10]], blocks)
    up_sum = ring_sum(up_terms)
    *d_parts, d_hidden, d_low, sums_two = call(
        hidden_back_kernel,
        "hidden_back",
        (ix, keep0, got, across, hidden, dys[0], after(gains, up_terms), near_out, far_out),
        [shape_of((own, quarter))] * 4 + [shape_of(block, F32), shape_of(block), shape_of((8, width), F32)],
        flops=2 * own * width * width,
    )
    d_mixed = quad_swap(d_parts)
    near_parts, far_parts = d_mixed[:2], d_mixed[2:]
    dq_near, kept = attend_back(ix, q, k, v, quarter, qrow, krow, lse_near, near_parts, 0, ())
    down_terms = grads(
        "grad_down", [after(act3, kept), act2, act10], [[dys[p] for p in order]], [(i, i, n) for i, _, n in blocks]
    )
    down_sum = ring_sum(down_terms)
    dq_far, dkv = attend_back(ix, q, k, v, quarter, qrow, krow, lse_far, far_parts, 2, (after(kept, down_terms),))
    n_rows = dkv.shape[0] // quads
    if quads > 1:
        total = dkv[:n_rows].astype(F32)
        for s in range(1, quads):
            total = total + permute(dkv[s * n_rows : (s + 1) * n_rows], group_perm(-s)).astype(F32)
        dkv = total.astype(BF16)

    keep_one, give_one, columns = call(
        functools.partial(project_back_kernel, run),
        "project_back",
        (ix, *taken, dq_near, dq_far, dkv, full_qkv, after(sums_two, up_sum)),
        [shape_of((2 * own, width), F32), shape_of((2 * own, width)), shape_of((width, 128))],
        scratch=[pltpu.VMEM((128, width), F32)],
        grid=(4,),
        flops=2 * 4 * own * width * 3 * quarter,
        in_specs={
            6: pl.BlockSpec((own, 2 * quarter), lambda i: (jnp.where(i == 0, 1, jnp.where(i == 1, 3, (i - 2) * 2)), 0)),
        },
    )
    got_one = permute(give_one, p_core)
    far_one = far_sum(keep_one[own:], got_one[own:])
    across_one = permute(far_one, p_y)
    grad_near, grad_far = call(
        out_grad_kernel,
        "out_grad",
        (ix, after(mixed_own, give_one), d_low),
        [shape_of((width, half), F32), shape_of((width, half))],
        flops=2 * own * width * width,
    )
    at_terms = grads(
        "grad_at",
        [after(n_one, far_one)],
        [[jnp.concatenate([dq_near, dq_far], 0)], [dkv]],
        blocks,
        (grad_near, permute(grad_far, p_core), columns),
    )
    r_keep, r_give = call(
        down_kernel,
        "down",
        (ix, after(act3, at_terms), act2, act10, full_down),
        [shape_of((2 * own, width), F32), shape_of((2 * own, width))],
        flops=2 * 4 * own * width * units,
    )
    r_got = permute(r_give, p_core)
    r_far = far_sum(r_keep[own:], r_got[own:])
    r_across = permute(after(r_far, across_one), p_y)
    r_own = (hidden + r_keep[:own] + r_got[:own].astype(F32) + r_across.astype(F32)).astype(BF16)
    one_sum = ring_sum(after(at_terms, down_sum))
    def place_back(one, two):
        one, two = permute(one, p_back[0]), permute(two, p_back[1])
        return jnp.stack([jnp.where(z % 2 == 0, one, two), jnp.where(z % 2 == 0, two, one)], 0)

    output = place_back(r_own[:run], r_own[run:])
    d_one, d_two = call(
        functools.partial(tokens_back_kernel, run),
        "tokens_back",
        (ix, keep_one, got_one, across_one, taken[0], d_hidden, gains),
        [shape_of((run, width))] * 2,
    )

    input_grad = place_back(d_one, d_two).astype(F32)

    def home(name, summed):
        return quad_swap(call(home_kernel, name, (ix, summed), [shape_of((rows, summed.shape[1]))] * 4))

    ff_home = home("home_up", up_sum)
    own_down = down_sum.astype(F32)
    if aligned:
        (own_up,) = call(
            functools.partial(settle_ff_kernel, spots), "settle_ff", (ix, *ff_home), [shape_of((rows, 4 * units), F32)])
    else:
        ups = [b.reshape(rows, pc.nodes, hid) for b in ff_home]
        at_spot = [[spots.index((nx, nz)) for nz in range(pc.zs)] for nx in range(pc.xs)]
        ups = by_rank([jnp.stack([jnp.stack([b[:, i] for i in row], 1) for row in at_spot], 1) for b in ups])
        own_up = (
            jnp.stack([jnp.stack([ups[0], ups[2]], 3), jnp.stack([ups[1], ups[3]], 3)], 2)
            .reshape(rows, 4 * units)
            .astype(F32)
        )
    own_qkv, own_out, vectors = call(
        settle_kernel,
        "settle",
        (ix, *home("home_at", after(one_sum, own_up))),
        [shape_of((rows, 3 * width), F32), shape_of((rows, width), F32), shape_of((8, 128), F32)],
        scratch=[pltpu.VMEM((128, 128), F32)],
    )
    return (output, input_grad, own_qkv, own_out, own_up, own_down) + tuple(vectors[i, :rows] for i in range(4))


def solution(mesh):
    vector, matrix, batch = P(AXES), P(AXES, None), P(None, AXES, None)
    return jax.shard_map(
        functools.partial(body, Places(mesh)),
        mesh=mesh,
        in_specs=(batch, P(None, "dp", "fsdp")) + (matrix,) * 4 + (vector,) * 4 + (batch,),
        out_specs=(batch, batch) + (matrix,) * 4 + (vector,) * 4,
        check_vma=False,
    )
```

```python
import functools
import math

import jax
import jax.numpy as jnp
from jax import lax
from jax.experimental import pallas as pl
from jax.experimental.pallas import tpu as pltpu
from jax.sharding import PartitionSpec as P

AXES = ("dp", "fsdp")
HEAD_DIM = 64
EPS = 1e-05
LOWEST = -1000000000.0
F32 = jnp.float32
BF16 = jnp.bfloat16
NT = (((1,), (1,)), ((), ()))
TN = (((0,), (0,)), ((), ()))
NN = (((1,), (0,)), ((), ()))
VMEM_LIMIT = 58 * 1024 * 1024
HINTS = {"grad_ff": 3, "hidden_units": 8, "hidden_back": 300, "attend_back": 4, "grad_down": 0, "home_up": 0, "settle_ff": 0, "out_grad": 0, "project_back": 0, "grad_at": 0, "tokens_back": 0, "down": 8}


def dot(left, right, dims):
    return lax.dot_general(left, right, dims, preferred_element_type=F32)


def at(start, size, step):
    return pl.ds(pl.multiple_of(start, step), size)


def call(kernel, name, args, outs, scratch=(), grid=None, flops=0, transcendentals=0, in_specs=None, out_specs=None):
    whole = pl.BlockSpec(memory_space=pltpu.VMEM) if grid is None else None

    def spec(shape):
        return whole or pl.BlockSpec(shape, lambda i, n=len(shape): (0,) * n)

    specs = [pl.BlockSpec(memory_space=pltpu.SMEM)]
    specs += [(in_specs or {}).get(n) or spec(a.shape) for n, a in enumerate(args[1:])]
    size = sum(math.prod(a.shape) * a.dtype.itemsize for a in list(args) + list(outs))
    return pl.pallas_call(
        kernel,
        out_shape=tuple(outs),
        in_specs=specs,
        out_specs=tuple((out_specs or {}).get(n) or spec(o.shape) for n, o in enumerate(outs)),
        scratch_shapes=list(scratch),
        compiler_params=pltpu.CompilerParams(vmem_limit_bytes=VMEM_LIMIT),
        cost_estimate=pl.CostEstimate(
            flops=HINTS.get(name, 8) * flops, bytes_accessed=HINTS.get(name, 8) * size, transcendentals=transcendentals
        ),
        name=name,
        **({} if grid is None else {"grid": grid}),
    )(*args)


def shape_of(shape, dtype=BF16):
    return jax.ShapeDtypeStruct(shape, dtype)


def centre(v):
    c = v - jnp.mean(v, axis=-1, keepdims=True)
    inv = lax.rsqrt(jnp.mean(c * c, axis=-1, keepdims=True) + EPS)
    return c * inv, inv


def norm_back(d_norm, std, inv, gain):
    d_std = d_norm * gain
    return inv * (
        d_std - jnp.mean(d_std, axis=-1, keepdims=True) - std * jnp.mean(d_std * std, axis=-1, keepdims=True)
    )


def pack_kernel(aligned, spots, ix, qkv, out, gains, tokens, scenes, dy, up, *refs):
    parts, ups, (one, two, dy_one, dy_two, tile) = refs[:4], refs[4:8], refs[8:]
    rank, core, odd, y = ix[0], ix[1], ix[2], ix[3]
    rows, width = qkv.shape[0], out.shape[1]
    quarter, half = width // 4, width // 2
    tile[...] = jnp.zeros_like(tile)
    tile[0:4, 0:rows] = gains[...].astype(F32)
    small = tile[...].T[:rows].astype(BF16)
    c1, c2 = 3 * quarter, 3 * quarter + half
    hid, units = 128, up.shape[1] // 4
    zs = len(spots) // 2
    for p in range(4):
        a = rank ^ p
        for t in range(3):
            parts[p][:, t * quarter : (t + 1) * quarter] = qkv[:, at(t * width + a * quarter, quarter, 128)]
        parts[p][:, c1:c2] = out[:, at((core ^ (p & 1)) * half, half, 128)]
        parts[p][:, c2 : c2 + 128] = small
        if aligned:
            for b, (nx, nz) in enumerate(spots):
                src = ((nx * 2 + (core ^ (p & 1))) * zs + nz) * 2 + (y ^ (p >> 1))
                ups[p][:, b * hid : (b + 1) * hid] = up[:, at(src * hid, hid, 128)]
        else:
            ups[p][...] = up[:, p * units : (p + 1) * units]
    run = tokens.shape[1]
    for ref, low, m in ((one, dy_one, odd), (two, dy_two, 1 - odd)):
        ref[0:run, :] = tokens[m]
        ref[run:, :] = jnp.zeros((ref.shape[0] - run, width), BF16)
        ref[run : run + 1, 0:run] = scenes[pl.ds(m, 1), :].astype(F32).astype(BF16)
        low[...] = dy[m]


def row_blocks(spots, size):
    zs = len(spots) // 2
    return [
        ((2 * i + c) * size, ((nx * 2 + c) * zs + nz) * size, size) for i, (nx, nz) in enumerate(spots) for c in (0, 1)
    ]


def project_kernel(blocks, run, ix, *refs):
    taken, first = refs[:4], refs[4]
    n_ref, p_ref, w_ref, near_ref, gains_ref, scene_ref, g_all = refs[5:]
    step = pl.program_id(0)
    c_out, c_small = w_ref.shape[1], w_ref.shape[1] + near_ref.shape[1]

    @pl.when(step == 0)
    def _():
        for src, dst, size in blocks:
            v = first[src : src + size, :]
            w_ref[dst : dst + size, :] = v[:, :c_out]
            near_ref[dst : dst + size, :] = v[:, c_out:c_small]
            g_all[dst : dst + size, :] = v[:, c_small:].astype(F32)
        gains_ref[...] = g_all[...].T[0:8, :]
        for p in range(4):
            for s in range(2):
                row = taken[p][s * (run + 8) + run : s * (run + 8) + run + 1, 0:run]
                scene_ref[0:1, (2 * p + s) * run : (2 * p + s + 1) * run] = row.astype(F32)

    for p in range(4):

        @pl.when(step == p)
        def _():
            x = taken[p]
            v = jnp.concatenate([x[0:run, :], x[run + 8 : 2 * run + 8, :]], 0).astype(F32)
            std, _ = centre(v)
            n = (std * gains_ref[0:1, :] + gains_ref[1:2, :]).astype(BF16)
            n_ref[...] = n
            p_ref[...] = dot(n, w_ref[...], NN).astype(BF16)


def head_lanes(rows, width, head):
    lane = lax.broadcasted_iota(jnp.int32, (rows, width), 1)
    return (lane >= head * HEAD_DIM) & (lane < (head + 1) * HEAD_DIM)


def column(row):
    return jnp.broadcast_to(row, (128, row.shape[1])).T


def same_scene(ksc, qrow):
    return jnp.concatenate([ksc == qrow[:, i : i + 128] for i in range(0, qrow.shape[1], 128)], 1)


def attend_kernel(heads, ix, krow_ref, qrow_ref, q_ref, k_ref, v_ref, *refs):
    outs_ref, (lse_ref, vt_ref, ksc_ref) = refs[:2], refs[2:]
    step = pl.program_id(0)

    @pl.when(step == 0)
    def _():
        vt_ref[...] = v_ref[...].astype(F32).T.astype(BF16)
        ksc_ref[...] = column(krow_ref[...])

    rows, width = q_ref.shape
    same = same_scene(ksc_ref[...], qrow_ref[...])
    q = q_ref[...].astype(F32) * (1.0 / math.sqrt(HEAD_DIM))
    outs = []
    for h in range(heads):
        qh = jnp.where(head_lanes(rows, width, h), q, 0.0).astype(BF16)
        s = jnp.where(same, dot(k_ref[...], qh, NT), LOWEST)
        peak = jnp.max(s, axis=0, keepdims=True)
        e = jnp.exp(s - peak)
        total = jnp.sum(e, axis=0, keepdims=True)
        lse_ref[h : h + 1, :] = peak + jnp.log(total)
        p = (e * (1.0 / total)).astype(BF16)
        outs.append(dot(vt_ref[h * HEAD_DIM : (h + 1) * HEAD_DIM, :], p, NN))
    mixed = jnp.concatenate(outs, axis=0).T.astype(BF16)
    for i in range(2):

        @pl.when(step == i)
        def _():
            outs_ref[i][...] = mixed


def attend(ix, q, k, v, quarter, qrow, krow, first):
    rows, keys = q[0].shape[0], k[0].shape[0]
    heads, block = quarter // HEAD_DIM, rows // 4
    return call(
        functools.partial(attend_kernel, heads),
        "attend",
        (ix, krow, qrow, q[0], k[0], v[0]),
        [shape_of((block, quarter))] * 2 + [shape_of((heads, 2 * block), F32)],
        scratch=[pltpu.VMEM((quarter, keys), BF16), pltpu.VMEM((keys, 128), F32)],
        grid=(2,),
        flops=2 * rows * keys * quarter,
        transcendentals=rows * keys * heads // 2,
        in_specs={
            1: pl.BlockSpec((1, block), lambda i: (0, i + first)),
            2: pl.BlockSpec((block, quarter), lambda i, c=q[1]: (i + first, c)),
            3: pl.BlockSpec((keys, quarter), lambda i, c=k[1]: (0, c)),
            4: pl.BlockSpec((keys, quarter), lambda i, c=v[1]: (0, c)),
        },
        out_specs={2: pl.BlockSpec((heads, block), lambda i: (0, i))},
    )


def attend_back_kernel(heads, more, ix, krow_ref, qrow_ref, lse_ref, q_ref, k_ref, v_ref, *refs):
    do_refs, kept, refs = refs[:2], refs[2 : 2 + more], refs[2 + more :]
    dq_ref, dkv_ref, kt_ref, ksc_ref, dka_ref, dva_ref, do_ref = refs
    width = q_ref.shape[1]
    step = pl.program_id(0)

    @pl.when(step == 0)
    def _():
        kt_ref[...] = k_ref[...].astype(F32).T.astype(BF16)
        ksc_ref[...] = column(krow_ref[...])
        if more:
            dka_ref[...] = kept[0][:, :width]
            dva_ref[...] = kept[0][:, width:]
        else:
            dka_ref[...] = jnp.zeros_like(dka_ref)
            dva_ref[...] = jnp.zeros_like(dva_ref)

    for i in range(2):

        @pl.when(step == i)
        def _():
            do_ref[...] = do_refs[i][...].astype(F32)

    rows, width = q_ref.shape
    scale = 1.0 / math.sqrt(HEAD_DIM)
    same = same_scene(ksc_ref[...], qrow_ref[...])
    q = q_ref[...].astype(F32) * scale
    do = do_ref[...]
    outs = []
    for h in range(heads):
        mine = head_lanes(rows, width, h)
        qh = jnp.where(mine, q, 0.0).astype(BF16)
        doh = jnp.where(mine, do, 0.0).astype(BF16)
        s = jnp.where(same, dot(k_ref[...], qh, NT), LOWEST)
        p = jnp.exp(s - lse_ref[h : h + 1, :])
        dp = dot(v_ref[...], doh, NT)
        inner = jnp.sum(p * dp, axis=0, keepdims=True)
        ds = (p * (dp - inner)).astype(BF16)
        dva_ref[...] += dot(p.astype(BF16), doh, NN)
        dka_ref[...] += dot(ds, qh, NN)
        outs.append(dot(kt_ref[h * HEAD_DIM : (h + 1) * HEAD_DIM, :], ds, NN))
    dq_ref[...] = (jnp.concatenate(outs, axis=0).T * scale).astype(BF16)

    @pl.when(step == pl.num_programs(0) - 1)
    def _():
        dkv_ref[:, :width] = dka_ref[...].astype(dkv_ref.dtype)
        dkv_ref[:, width:] = dva_ref[...].astype(dkv_ref.dtype)


def attend_back(ix, q, k, v, quarter, qrow, krow, lse, do, first, kept):
    rows, keys = q[0].shape[0], k[0].shape[0]
    heads, block = quarter // HEAD_DIM, rows // 4
    return call(
        functools.partial(attend_back_kernel, heads, len(kept)),
        "attend_back",
        (ix, krow, qrow, lse, q[0], k[0], v[0], *do, *kept),
        [shape_of((2 * block, quarter)), shape_of((keys, 2 * quarter), BF16 if kept else F32)],
        scratch=[
            pltpu.VMEM((quarter, keys), BF16),
            pltpu.VMEM((keys, 128), F32),
            pltpu.VMEM((keys, quarter), F32),
            pltpu.VMEM((keys, quarter), F32),
            pltpu.VMEM((block, quarter), F32),
        ],
        grid=(2,),
        flops=5 * rows * keys * quarter,
        transcendentals=rows * keys * heads // 2,
        in_specs={
            1: pl.BlockSpec((1, block), lambda i: (0, i + first)),
            2: pl.BlockSpec((heads, block), lambda i: (0, i)),
            3: pl.BlockSpec((block, quarter), lambda i, c=q[1]: (i + first, c)),
            4: pl.BlockSpec((keys, quarter), lambda i, c=k[1]: (0, c)),
            5: pl.BlockSpec((keys, quarter), lambda i, c=v[1]: (0, c)),
        },
        out_specs={0: pl.BlockSpec((block, quarter), lambda i: (i, 0))},
    )


def mix_out_kernel(run, ix, m0, m1, m2, m3, near, far, x, gains, mixed_ref, hidden_ref, n_ref):
    rank, core = ix[0], ix[1]
    quarter, half = m0.shape[1], near.shape[1]
    for p, m in enumerate((m0, m1, m2, m3)):
        mixed_ref[:, at((rank ^ p) * quarter, quarter, 128)] = m[...]
    mixed = mixed_ref[...]
    hidden_ref[0:run, :] = x[0:run, :].astype(F32)
    hidden_ref[run:, :] = x[run + 8 : 2 * run + 8, :].astype(F32)
    hidden_ref[:, at(core * half, half, 128)] += dot(mixed, near[...], NN)
    hidden_ref[:, at((1 - core) * half, half, 128)] += dot(mixed, far[...], NN)
    std, _ = centre(hidden_ref[...])
    n_ref[...] = (std * gains[2:3, :] + gains[3:4, :]).astype(BF16)


def hidden_units_kernel(parts, blocks, ix, *refs):
    n, rows = len(parts), refs[0].shape[0]
    norms, dys, refs = refs[:n], refs[n : 2 * n], refs[2 * n :]
    if blocks:
        second, act_ref, dup_ref, *term_refs, up_ref, down_ref = refs
        units = up_ref.shape[1]
        for src, dst, size in blocks:
            up_ref[dst : dst + size, :] = second[src : src + size, :units]
        down_ref[...] = second[:, units:]
    else:
        up_ref, down_ref, act_ref, dup_ref, *term_refs = refs
    for i in range(n):
        span = slice(i * rows, (i + 1) * rows)
        u = dot(norms[i][...], up_ref[...], NN)
        cdf = 0.5 * (1.0 + lax.erf(u * math.sqrt(0.5)))
        act = (u * cdf).astype(BF16)
        act_ref[span, :] = act
        term_refs[n + i][...] = dot(act, down_ref[...], NN).astype(term_refs[n + i].dtype)
        slope = cdf + u * jnp.exp(-0.5 * u * u) * (1.0 / math.sqrt(2.0 * math.pi))
        dup = (dot(dys[i][...], down_ref[...], NT) * slope).astype(BF16)
        dup_ref[span, :] = dup
        term_refs[i][...] = dot(dup, up_ref[...], NT).astype(term_refs[i].dtype)


def hidden_back_kernel(ix, keep, got, across, hidden, dy, gains, near, far, *refs):
    parts, (dh_ref, low_ref, sums_ref) = refs[:4], refs[4:]
    rank, core = ix[0], ix[1]
    rows = hidden.shape[0]
    half, quarter = near.shape[1], parts[0].shape[1]
    d_norm = keep[...] + got[...].astype(F32) + across[...].astype(F32)
    std, inv = centre(hidden[...])
    sums_ref[...] = jnp.zeros_like(sums_ref)
    sums_ref[2:3, :] = jnp.sum(d_norm * std, axis=0, keepdims=True)
    sums_ref[3:4, :] = jnp.sum(d_norm, axis=0, keepdims=True)
    d_hidden = dy[...].astype(F32) + norm_back(d_norm, std, inv, gains[2:3, :])
    dh_ref[...] = d_hidden
    low_ref[...] = d_hidden.astype(BF16)
    a, b = low_ref[:, at(core * half, half, 128)], low_ref[:, at((1 - core) * half, half, 128)]
    for p in range(4):
        rows_p = at((rank ^ p) * quarter, quarter, 16)
        parts[p][...] = (dot(a, near[rows_p, :], NT) + dot(b, far[rows_p, :], NT)).astype(BF16)


def out_grad_kernel(ix, mixed, low, near_ref, far_ref):
    core, half = ix[1], near_ref.shape[1]
    left = mixed[...].astype(F32).T.astype(BF16)
    near_ref[...] = dot(left, low[:, at(core * half, half, 128)], NN)
    far_ref[...] = dot(left, low[:, at((1 - core) * half, half, 128)], NN).astype(BF16)


def project_back_kernel(run, ix, *refs):
    taken, (dq_a, dq_b, dkv, w, sums2, keep_ref, give_ref, cols_ref, sums) = refs[:4], refs[4:]
    step = pl.program_id(0)
    quarter, rows = dq_a.shape[1], dkv.shape[0]

    @pl.when(step == 0)
    def _():
        sums[...] = jnp.zeros_like(sums)
        sums[0:8, :] = sums2[...]

    for i, p in enumerate((1, 3, 0, 2)):

        @pl.when(step == i)
        def _():
            x = taken[p]
            std, _ = centre(jnp.concatenate([x[0:run, :], x[run + 8 : 2 * run + 8, :]], 0).astype(F32))
            dq = (dq_a, dq_b)[p >> 1][(p & 1) * rows : ((p & 1) + 1) * rows, :]
            part = dot(dq, w[:, 0:quarter], NT) + dot(dkv[...], w[:, quarter:], NT)
            sums[0:1, :] += jnp.sum(part * std, axis=0, keepdims=True)
            sums[1:2, :] += jnp.sum(part, axis=0, keepdims=True)
            if p & 1:
                give_ref[(p >> 1) * rows : ((p >> 1) + 1) * rows, :] = part.astype(BF16)
            else:
                keep_ref[(p >> 1) * rows : ((p >> 1) + 1) * rows, :] = part

    @pl.when(step == 3)
    def _():
        cols_ref[...] = sums[...].T.astype(BF16)


def tokens_back_kernel(run, ix, keep, got, across, x, d_hidden, gains, one_ref, two_ref):
    rows = d_hidden.shape[0]
    d_norm = keep[0:rows, :] + got[0:rows, :].astype(F32) + across[...].astype(F32)
    std, inv = centre(jnp.concatenate([x[0:run, :], x[run + 8 : 2 * run + 8, :]], 0).astype(F32))
    d = (d_hidden[...] + norm_back(d_norm, std, inv, gains[0:1, :])).astype(BF16)
    one_ref[...] = d[0:run]
    two_ref[...] = d[run:]


def grads_kernel(blocks, n_left, widths, n_right, extra, ix, *refs):
    lefts, refs = refs[:n_left], refs[n_left:]
    rights, refs = [refs[i * n_right : (i + 1) * n_right] for i in range(len(widths))], refs[len(widths) * n_right :]
    out_ref, left_t, *right_refs = refs[extra:]
    step = pl.program_id(0)
    cols = sum(widths)

    @pl.when(step == 0)
    def _():
        at_col = 0
        for piece in lefts:
            t = piece[...].T
            stop = at_col + t.shape[1]
            for dst, src, size in blocks:
                left_t[dst : dst + size, at_col:stop] = t[src : src + size, :]
            at_col = stop
        for pieces, ref in zip(rights, right_refs):
            row = 0
            for piece in pieces:
                ref[row : row + piece.shape[0], :] = piece[...]
                row += piece.shape[0]

    rows = out_ref.shape[0]
    mine = left_t[at(step * rows, rows, 16), :]
    start = 0
    for ref, w in zip(right_refs, widths):
        out_ref[:, start : start + w] = dot(mine, ref[...], NN).astype(BF16)
        start += w
    if extra:
        near, far, columns = refs[:3]
        half = near.shape[1]
        for i in range(left_t.shape[0] // rows):

            @pl.when(step == i)
            def _():
                for dst, src, size in blocks:
                    if i * rows <= dst < (i + 1) * rows:
                        span = slice(dst - i * rows, dst - i * rows + size)
                        both = near[src : src + size, :] + far[src : src + size, :].astype(F32)
                        out_ref[span, cols : cols + half] = both.astype(BF16)
                        out_ref[span, cols + half :] = columns[src : src + size, :]


def grad_ff_kernel(blocks, ix, n3, n2, n1, n0, u3, u2, u10, a3, a2, a10, d3, d2, d1, d0, out_ref, nt, at_t, up, dy):
    step = pl.program_id(0)
    depth = n3.shape[0]

    @pl.when(step == 0)
    def _():
        for i, (n, d) in enumerate(((n3, d3), (n2, d2), (n1, d1), (n0, d0))):
            span = slice(i * depth, (i + 1) * depth)
            t = n[...].T
            for dst, src, size in blocks:
                nt[dst : dst + size, span] = t[src : src + size, :]
            dy[span, :] = d[...]
        for first, a, u in ((0, a3, u3), (1, a2, u2), (2, a10, u10)):
            span = slice(first * depth, first * depth + a.shape[0])
            at_t[:, span] = a[...].T
            up[span, :] = u[...]

    rows, units = out_ref.shape[0], up.shape[1]
    mine = at(step * rows, rows, 16)
    out_ref[:, :units] = dot(nt[mine, :], up[...], NN).astype(BF16)
    out_ref[:, units:] = dot(at_t[mine, :], dy[...], NN).astype(BF16)


def home_kernel(ix, summed, *parts):
    core, y = ix[1], ix[3]
    rows, cols = parts[0].shape
    for p in range(4):
        block = (core ^ (p & 1)) * 2 + (y ^ (p >> 1))
        parts[p][...] = summed[at(block * rows, rows, 8), 0:cols]


def settle_kernel(ix, p0, p1, p2, p3, qkv_ref, out_ref, vec_ref, tile):
    rank, core = ix[0], ix[1]
    parts = (p0, p1, p2, p3)
    rows, width = out_ref.shape
    quarter, half = width // 4, width // 2
    for p in range(4):
        a = rank ^ p
        for t in range(3):
            qkv_ref[:, at(t * width + a * quarter, quarter, 128)] = parts[p][:, t * quarter : (t + 1) * quarter].astype(F32)
    c1, c2 = 3 * quarter, 3 * quarter + half
    for p in range(2):
        out_ref[:, at((core ^ p) * half, half, 128)] = parts[p][:, c1:c2].astype(F32) + parts[p + 2][:, c1:c2].astype(F32)
    tile[...] = jnp.zeros_like(tile)
    tile[0:rows, :] = sum(v[:, c2:].astype(F32) for v in parts)
    vec_ref[...] = tile[...].T[0:8, :]


def settle_ff_kernel(spots, ix, p0, p1, p2, p3, up_ref):
    core, y = ix[1], ix[3]
    hid, zs = 128, len(spots) // 2
    for p, part in enumerate((p0, p1, p2, p3)):
        c2, y2 = core ^ (p & 1), y ^ (p >> 1)
        for b, (nx, nz) in enumerate(spots):
            dst = ((nx * 2 + c2) * zs + nz) * 2 + y2
            up_ref[:, at(dst * hid, hid, 128)] = part[:, b * hid : (b + 1) * hid].astype(F32)


class Places:
    def __init__(self, mesh):
        self.n_dp, self.n_fsdp = mesh.shape["dp"], mesh.shape["fsdp"]
        self.xs, self.zs = self.n_dp // 2, self.n_fsdp // 2
        self.nodes = self.xs * self.zs
        self.all = [
            (x, c, z, y) for x in range(self.xs) for c in range(2) for z in range(self.zs) for y in range(2)
        ]

    def lin(self, x, c, z, y):
        return (x * 2 + c) * self.n_fsdp + z * 2 + y

    def perm(self, move):
        return [(self.lin(*d), self.lin(*move(*d))) for d in self.all]

    def spot(self, x, z):
        return x * self.zs + (z if x % 2 == 0 else self.zs - 1 - z)

    def node(self, spot):
        x, z = spot // self.zs, spot % self.zs
        return (x, z if x % 2 == 0 else self.zs - 1 - z)

    def rings(self):
        return [
            [self.lin(x, c, z, y) for x, z in map(self.node, range(self.nodes))] for c in range(2) for y in range(2)
        ]


def permute(array, pairs):
    return lax.ppermute(array, AXES, pairs)


def after(value, *done):
    return lax.optimization_barrier((value,) + done)[0]


def body(pc, tokens, scene_ids, w_qkv, w_out, w_up, w_down, gain_one, bias_one, gain_two, bias_two, cotangent):
    micro, run, width = tokens.shape
    rows = w_qkv.shape[0]
    ff = w_up.shape[1]
    units = ff // 4
    hid = w_down.shape[0]
    quarter, half = width // 4, width // 2
    own = micro * run
    dp, fsdp = lax.axis_index("dp"), lax.axis_index("fsdp")
    x, core, z, y = dp // 2, dp % 2, fsdp // 2, fsdp % 2
    rank = y * 2 + core
    groups = micro * 2
    quads = pc.zs // groups
    rings = pc.rings()
    spots = [pc.node(i) for i in range(pc.nodes)]
    blocks = row_blocks(spots, 2 * rows)
    aligned = hid % 128 == 0

    p_core = pc.perm(lambda x, c, z, y: (x, 1 - c, z, y))
    p_y = pc.perm(lambda x, c, z, y: (x, c, z, 1 - y))
    p_diag = pc.perm(lambda x, c, z, y: (x, 1 - c, z, 1 - y))

    def place_perm(flip):
        def move(x, c, z, y):
            m = (z % 2) ^ flip
            return (x, (z // 2) % 2, (m * 2 + c) * quads + z // 4, y)

        return pc.perm(move)

    p_place = [place_perm(0), place_perm(1)]
    p_back = [[(b, a) for a, b in pairs] for pairs in p_place]

    def group_perm(by):
        return pc.perm(lambda x, c, z, y: (x, c, z // quads * quads + (z + by) % quads, y))

    ix = jnp.stack([rank, core, z % 2, y]).astype(jnp.int32)

    def quad_swap(parts):
        return [parts[0], permute(parts[1], p_core), permute(parts[2], p_y), permute(parts[3], p_diag)]

    def by_rank(parts):
        odd, top = rank % 2 == 1, rank // 2 == 1
        parts = [jnp.where(odd, parts[i ^ 1], parts[i]) for i in range(4)]
        return [jnp.where(top, parts[i ^ 2], parts[i]) for i in range(4)]

    def by_rows(parts):
        r = by_rank(parts)
        return jnp.concatenate([r[0], r[2], r[1], r[3]], 0)

    def ring_gather(shard):
        return lax.all_gather(shard, AXES, axis=0, tiled=True, axis_index_groups=rings)

    def ring_sum(terms):
        return lax.psum_scatter(terms, AXES, scatter_dimension=0, tiled=True, axis_index_groups=rings)

    c_out, c_small, wide = 3 * quarter, 3 * quarter + half, 3 * quarter + half + 128
    wu = w_up
    if not aligned:
        wu = w_up.reshape(rows, pc.xs, 2, pc.zs, 2, hid)
        wu = [
            lax.dynamic_slice(
                wu, (0, 0, core ^ (p & 1), 0, y ^ (p >> 1), 0), (rows, pc.xs, 1, pc.zs, 1, hid)
            ).reshape(rows, pc.xs, pc.zs, hid)
            for p in range(4)
        ]
        wu = jnp.concatenate([w[:, nx, nz] for w in wu for nx, nz in spots], 1)
    *packed, x_one, x_two, dy_one, dy_two = call(
        functools.partial(pack_kernel, aligned, spots),
        "pack",
        (
            ix,
            w_qkv,
            w_out,
            jnp.stack([gain_one, bias_one, gain_two, bias_two]),
            tokens,
            scene_ids.reshape(micro, run),
            cotangent,
            wu,
        ),
        [shape_of((rows, wide))] * 4 + [shape_of((rows, units))] * 4 + [shape_of((run + 8, width))] * 2 + [shape_of((run, width))] * 2,
        scratch=[pltpu.VMEM((128, 128), F32)],
    )
    shard = by_rows(quad_swap(packed[:4]))
    x_own = jnp.concatenate([permute(x_one, p_place[0]), permute(x_two, p_place[1])], 0)
    first = ring_gather(after(shard, x_own))
    x_across = permute(x_own, p_y)
    taken = [x_own, permute(x_own, p_core), x_across, permute(x_across, p_core)]
    up_shard = by_rows(quad_swap(after(packed[4:], x_across)))
    second = ring_gather(after(jnp.concatenate([up_shard, w_down], 1), taken))
    dy_one, dy_two = after((dy_one, dy_two), first)
    dy_own = jnp.concatenate([permute(dy_one, p_place[0]), permute(dy_two, p_place[1])], 0)

    block = (own, width)
    n_one, projected, full_qkv, near_out, gains, qrow = call(
        functools.partial(project_kernel, blocks, run),
        "project",
        (ix, *taken, first),
        [
            shape_of((4 * own, width)),
            shape_of((4 * own, 3 * quarter)),
            shape_of((width, 3 * quarter)),
            shape_of((width, half)),
            shape_of((8, width), F32),
            shape_of((1, 4 * own), F32),
        ],
        scratch=[pltpu.VMEM((width, 128), F32)],
        grid=(4,),
        flops=2 * 4 * own * width * 3 * quarter,
        out_specs={
            0: pl.BlockSpec(block, lambda i: (i, 0)),
            1: pl.BlockSpec((own, 3 * quarter), lambda i: (i, 0)),
        },
    )
    far_out = permute(near_out, p_core)
    if quads == 1:
        q, k, v, krow = (projected, 0), (projected, 1), (projected, 2), qrow
    else:
        kv = projected[:, quarter:]
        kv_all = jnp.concatenate([kv] + [permute(kv, group_perm(s)) for s in range(1, quads)], 0)
        krow = jnp.concatenate([qrow] + [permute(qrow, group_perm(s)) for s in range(1, quads)], 1)
        q, k, v = (projected, 0), (kv_all, 0), (kv_all, 1)
    *m_far, lse_far = attend(ix, q, k, v, quarter, qrow, krow, 2)
    dy_across = permute(after(dy_own, m_far), p_y)
    *m_near, lse_near = attend(ix, q, k, v, quarter, after(qrow, m_far, dy_own), krow, 0)
    mixed = quad_swap([*m_near, *m_far])
    mixed_own, hidden, n_two = call(
        functools.partial(mix_out_kernel, run),
        "mix_out",
        (ix, *mixed, near_out, far_out, taken[0], after(gains, dy_across)),
        [shape_of(block), shape_of(block, F32), shape_of(block)],
        flops=2 * own * width * width,
    )
    def far_sum(keep, got):
        return (keep + got.astype(F32)).astype(BF16)

    n_across = permute(n_two, p_y)
    norms = [n_two, permute(n_two, p_core), n_across, permute(n_across, p_core)]
    dys = [dy_own, permute(dy_own, p_core), dy_across, permute(dy_across, p_core)]

    def hidden_units(parts, weights, kinds, order):
        outs = [shape_of((len(parts) * own, units))] * 2 + [shape_of(block, kind) for kind in kinds * 2]
        return call(
            functools.partial(hidden_units_kernel, parts, order),
            "hidden_units",
            (ix, *[norms[p] for p in parts], *[dys[p] for p in parts], *weights),
            outs + ([shape_of((width, units)), shape_of((units, width))] if order else []),
            flops=8 * len(parts) * own * width * units,
            transcendentals=2 * len(parts) * own * units,
        )

    act3, up3, give3, r_give3, full_up, full_down = hidden_units((3,), (second,), (BF16,), blocks)
    got3 = permute(give3, p_core)
    act2, up2, keep2, r_keep2 = hidden_units((2,), (after(full_up, give3), full_down), (F32,), None)
    far = far_sum(keep2, got3)
    across = permute(far, p_y)
    act10, up10, give1, keep0, r_give1, r_keep0 = hidden_units((1, 0), (after(full_up, far), full_down), (BF16, F32), None)
    got = permute(give1, p_core)
    in_order = [(i, i, n) for i, _, n in blocks]

    def grads(name, lefts, rights, order, extra=()):
        widths = tuple(r[0].shape[1] for r in rights)
        depth, cols = sum(a.shape[0] for a in lefts), sum(widths)
        height = lefts[0].shape[1]
        total = cols + sum(e.shape[1] for e in extra[1:])
        return call(
            functools.partial(grads_kernel, order, len(lefts), widths, len(rights[0]), len(extra)),
            name,
            (ix, *lefts, *[piece for r in rights for piece in r], *extra),
            [shape_of((height, total))],
            scratch=[pltpu.VMEM((height, depth), BF16)] + [pltpu.VMEM((depth, w), BF16) for w in widths],
            grid=(4,),
            flops=2 * depth * height * cols,
            out_specs={0: pl.BlockSpec((height // 4, total), lambda i: (i, 0))},
        )[0]

    order = (3, 2, 1, 0)
    (ff_terms,) = call(
        functools.partial(grad_ff_kernel, blocks),
        "grad_ff",
        (ix, *[norms[p] for p in order], up3, up2, up10, act3, act2, act10, *[dys[p] for p in order]),
        [shape_of((width, units + width))],
        scratch=[pltpu.VMEM((width, 4 * own), BF16), pltpu.VMEM((units, 4 * own), BF16)]
        + [pltpu.VMEM((4 * own, units), BF16), pltpu.VMEM((4 * own, width), BF16)],
        grid=(4,),
        flops=2 * 4 * own * width * 2 * units,
        out_specs={0: pl.BlockSpec((width // 4, units + width), lambda i: (i, 0))},
    )
    ff_sum = ring_sum(ff_terms)
    up_sum, down_sum = ff_sum[:, :units], ff_sum[:, units:]
    *d_parts, d_hidden, d_low, sums_two = call(
        hidden_back_kernel,
        "hidden_back",
        (ix, keep0, got, across, hidden, dys[0], after(gains, ff_terms), near_out, far_out),
        [shape_of((own, quarter))] * 4 + [shape_of(block, F32), shape_of(block), shape_of((8, width), F32)],
        flops=2 * own * width * width,
    )
    d_mixed = quad_swap(d_parts)
    near_parts, far_parts = d_mixed[:2], d_mixed[2:]
    r_far = far_sum(r_keep2, permute(after(r_give3, d_parts[0]), p_core))
    r_across = permute(r_far, p_y)
    r_got = permute(after(r_give1, d_parts[0]), p_core)
    dq_near, kept = attend_back(ix, q, k, v, quarter, qrow, krow, lse_near, near_parts, 0, ())
    dq_far, dkv = attend_back(ix, q, k, v, quarter, qrow, krow, lse_far, far_parts, 2, (after(kept, r_far),))

    def placed(one, two):
        return [permute(one, p_back[0]), permute(two, p_back[1])]

    r_own = (after(hidden, dq_far) + r_keep0 + r_got.astype(F32) + r_across.astype(F32)).astype(BF16)
    back_out = placed(r_own[:run], r_own[run:])
    n_rows = dkv.shape[0] // quads
    if quads > 1:
        total = dkv[:n_rows].astype(F32)
        for s in range(1, quads):
            total = total + permute(dkv[s * n_rows : (s + 1) * n_rows], group_perm(-s)).astype(F32)
        dkv = total.astype(BF16)

    keep_one, give_one, columns = call(
        functools.partial(project_back_kernel, run),
        "project_back",
        (ix, *taken, dq_near, dq_far, dkv, full_qkv, after(sums_two, r_own)),
        [shape_of((2 * own, width), F32), shape_of((2 * own, width)), shape_of((width, 128))],
        scratch=[pltpu.VMEM((128, width), F32)],
        grid=(4,),
        flops=2 * 4 * own * width * 3 * quarter,
        in_specs={
            6: pl.BlockSpec((own, 2 * quarter), lambda i: (jnp.where(i == 0, 1, jnp.where(i == 1, 3, (i - 2) * 2)), 0)),
        },
    )
    got_one = permute(give_one, p_core)
    grad_near, grad_far = call(
        out_grad_kernel,
        "out_grad",
        (ix, after(mixed_own, give_one), d_low),
        [shape_of((width, half), F32), shape_of((width, half))],
        flops=2 * own * width * width,
    )
    far_one = far_sum(keep_one[own:], after(got_one, grad_near)[own:])
    across_one = permute(far_one, p_y)
    at_terms = grads(
        "grad_at",
        [after(n_one, far_one)],
        [[jnp.concatenate([dq_near, dq_far], 0)], [dkv]],
        blocks,
        (grad_near, permute(grad_far, p_core), columns),
    )
    one_sum = ring_sum(after(at_terms, ff_sum, back_out))

    def home(name, summed):
        return quad_swap(call(home_kernel, name, (ix, summed), [shape_of((rows, summed.shape[1]))] * 4))

    def in_batches(one, two):
        return jnp.stack([jnp.where(z % 2 == 0, one, two), jnp.where(z % 2 == 0, two, one)], 0)

    d_one, d_two = call(
        functools.partial(tokens_back_kernel, run),
        "tokens_back",
        (ix, keep_one, got_one, across_one, taken[0], d_hidden, after(gains, ff_sum, back_out)),
        [shape_of((run, width))] * 2,
    )
    back_grad = placed(d_one, d_two)
    at_home = home("home_at", after(one_sum, back_out, back_grad))
    output = in_batches(*after(back_out, at_home[0]))
    input_grad = in_batches(*after(back_grad, at_home[0])).astype(F32)
    ff_home = home("home_up", after(up_sum, d_one))
    own_down = down_sum.astype(F32)
    if aligned:
        (own_up,) = call(
            functools.partial(settle_ff_kernel, spots), "settle_ff", (ix, *ff_home), [shape_of((rows, 4 * units), F32)])
    else:
        ups = [b.reshape(rows, pc.nodes, hid) for b in ff_home]
        at_spot = [[spots.index((nx, nz)) for nz in range(pc.zs)] for nx in range(pc.xs)]
        ups = by_rank([jnp.stack([jnp.stack([b[:, i] for i in row], 1) for row in at_spot], 1) for b in ups])
        own_up = (
            jnp.stack([jnp.stack([ups[0], ups[2]], 3), jnp.stack([ups[1], ups[3]], 3)], 2)
            .reshape(rows, 4 * units)
            .astype(F32)
        )
    own_qkv, own_out, vectors = call(
        settle_kernel,
        "settle",
        (ix, *at_home),
        [shape_of((rows, 3 * width), F32), shape_of((rows, width), F32), shape_of((8, 128), F32)],
        scratch=[pltpu.VMEM((128, 128), F32)],
    )
    return (output, input_grad, own_qkv, own_out, own_up, own_down) + tuple(vectors[i, :rows] for i in range(4))


def solution(mesh):
    vector, matrix, batch = P(AXES), P(AXES, None), P(None, AXES, None)
    return jax.shard_map(
        functools.partial(body, Places(mesh)),
        mesh=mesh,
        in_specs=(batch, P(None, "dp", "fsdp")) + (matrix,) * 4 + (vector,) * 4 + (batch,),
        out_specs=(batch, batch) + (matrix,) * 4 + (vector,) * 4,
        check_vma=False,
    )
```

```python
import functools
import math

import jax
import jax.numpy as jnp
from jax import lax
from jax.experimental import pallas as pl
from jax.experimental.pallas import tpu as pltpu
from jax.sharding import PartitionSpec as P

AXES = ("dp", "fsdp")
HEAD_DIM = 64
EPS = 1e-05
LOWEST = -1000000000.0
F32 = jnp.float32
BF16 = jnp.bfloat16
NT = (((1,), (1,)), ((), ()))
TN = (((0,), (0,)), ((), ()))
NN = (((1,), (0,)), ((), ()))
ROOM = 20
IN_HBM = ("grad_ff", "grad_at")
HINTS = {"mix_out": 0, "grad_ff": 3, "hidden_units": 8, "hidden_back": 300, "attend_back": 4, "grad_down": 0, "home_up": 0, "settle_ff": 0, "out_grad": 0, "project_back": 0, "grad_at": 0, "tokens_back": 0, "down": 8}


def dot(left, right, dims):
    return lax.dot_general(left, right, dims, preferred_element_type=F32)


def at(start, size, step):
    return pl.ds(pl.multiple_of(start, step), size)


def call(kernel, name, args, outs, scratch=(), grid=None, flops=0, transcendentals=0, in_specs=None, out_specs=None, room=ROOM):
    whole = pl.BlockSpec(memory_space=pltpu.VMEM) if grid is None else None

    def spec(shape):
        return whole or pl.BlockSpec(shape, lambda i, n=len(shape): (0,) * n)

    specs = [pl.BlockSpec(memory_space=pltpu.SMEM)]
    specs += [(in_specs or {}).get(n) or spec(a.shape) for n, a in enumerate(args[1:])]
    size = sum(math.prod(a.shape) * a.dtype.itemsize for a in list(args) + list(outs))
    return pl.pallas_call(
        kernel,
        out_shape=tuple(pltpu.HBM(o.shape, o.dtype) for o in outs) if name in IN_HBM else tuple(outs),
        in_specs=specs,
        out_specs=tuple((out_specs or {}).get(n) or spec(o.shape) for n, o in enumerate(outs)),
        scratch_shapes=list(scratch),
        compiler_params=pltpu.CompilerParams(vmem_limit_bytes=min(room, 58) * 1024 * 1024),
        cost_estimate=pl.CostEstimate(
            flops=HINTS.get(name, 8) * flops, bytes_accessed=HINTS.get(name, 8) * size, transcendentals=transcendentals
        ),
        name=name,
        **({} if grid is None else {"grid": grid}),
    )(*args)


def shape_of(shape, dtype=BF16):
    return jax.ShapeDtypeStruct(shape, dtype)


def centre(v):
    c = v - jnp.mean(v, axis=-1, keepdims=True)
    inv = lax.rsqrt(jnp.mean(c * c, axis=-1, keepdims=True) + EPS)
    return c * inv, inv


def norm_back(d_norm, std, inv, gain):
    d_std = d_norm * gain
    return inv * (
        d_std - jnp.mean(d_std, axis=-1, keepdims=True) - std * jnp.mean(d_std * std, axis=-1, keepdims=True)
    )


def pack_kernel(aligned, spots, ix, qkv, out, gains, tokens, scenes, dy, up, *refs):
    parts, ups, (one, two, dy_one, dy_two, tile) = refs[:4], refs[4:8], refs[8:]
    rank, core, odd, y = ix[0], ix[1], ix[2], ix[3]
    rows, width = qkv.shape[0], out.shape[1]
    quarter, half = width // 4, width // 2
    tile[...] = jnp.zeros_like(tile)
    tile[0:4, 0:rows] = gains[...].astype(F32)
    small = tile[...].T[:rows].astype(BF16)
    c1, c2 = 3 * quarter, 3 * quarter + half
    hid, units = 128, up.shape[1] // 4
    zs = len(spots) // 2
    for p in range(4):
        a = rank ^ p
        for t in range(3):
            parts[p][:, t * quarter : (t + 1) * quarter] = qkv[:, at(t * width + a * quarter, quarter, 128)]
        parts[p][:, c1:c2] = out[:, at((core ^ (p & 1)) * half, half, 128)]
        parts[p][:, c2 : c2 + 128] = small
        if aligned:
            for b, (nx, nz) in enumerate(spots):
                src = ((nx * 2 + (core ^ (p & 1))) * zs + nz) * 2 + (y ^ (p >> 1))
                ups[p][:, b * hid : (b + 1) * hid] = up[:, at(src * hid, hid, 128)]
        else:
            ups[p][...] = up[:, p * units : (p + 1) * units]
    run = tokens.shape[1]
    for ref, low, m in ((one, dy_one, odd), (two, dy_two, 1 - odd)):
        ref[0:run, :] = tokens[m]
        ref[run:, :] = jnp.zeros((ref.shape[0] - run, width), BF16)
        ref[run : run + 1, 0:run] = scenes[pl.ds(m, 1), :].astype(F32).astype(BF16)
        low[...] = dy[m]


def row_blocks(spots, size):
    zs = len(spots) // 2
    return [
        ((2 * i + c) * size, ((nx * 2 + c) * zs + nz) * size, size) for i, (nx, nz) in enumerate(spots) for c in (0, 1)
    ]


def project_kernel(blocks, run, ix, *refs):
    taken, first = refs[:4], refs[4]
    n_ref, p_ref, w_ref, near_ref, gains_ref, scene_ref, g_all = refs[5:]
    step = pl.program_id(0)
    c_out, c_small = w_ref.shape[1], w_ref.shape[1] + near_ref.shape[1]

    @pl.when(step == 0)
    def _():
        for src, dst, size in blocks:
            v = first[src : src + size, :]
            w_ref[dst : dst + size, :] = v[:, :c_out]
            near_ref[dst : dst + size, :] = v[:, c_out:c_small]
            g_all[dst : dst + size, :] = v[:, c_small:].astype(F32)
        gains_ref[...] = g_all[...].T[0:8, :]
        for p in range(4):
            for s in range(2):
                row = taken[p][s * (run + 8) + run : s * (run + 8) + run + 1, 0:run]
                scene_ref[0:1, (2 * p + s) * run : (2 * p + s + 1) * run] = row.astype(F32)

    for p in range(4):

        @pl.when(step == p)
        def _():
            x = taken[p]
            v = jnp.concatenate([x[0:run, :], x[run + 8 : 2 * run + 8, :]], 0).astype(F32)
            std, _ = centre(v)
            n = (std * gains_ref[0:1, :] + gains_ref[1:2, :]).astype(BF16)
            n_ref[...] = n
            p_ref[...] = dot(n, w_ref[...], NN).astype(BF16)


def head_lanes(rows, width, head):
    lane = lax.broadcasted_iota(jnp.int32, (rows, width), 1)
    return (lane >= head * HEAD_DIM) & (lane < (head + 1) * HEAD_DIM)


def column(row):
    return jnp.broadcast_to(row, (128, row.shape[1])).T


def same_scene(ksc, qrow):
    return jnp.concatenate([ksc == qrow[:, i : i + 128] for i in range(0, qrow.shape[1], 128)], 1)


def attend_kernel(heads, ix, krow_ref, qrow_ref, q_ref, k_ref, v_ref, *refs):
    outs_ref, (lse_ref, vt_ref, ksc_ref) = refs[:2], refs[2:]
    step = pl.program_id(0)

    @pl.when(step == 0)
    def _():
        vt_ref[...] = v_ref[...].astype(F32).T.astype(BF16)
        ksc_ref[...] = column(krow_ref[...])

    rows, width = q_ref.shape
    same = same_scene(ksc_ref[...], qrow_ref[...])
    q = q_ref[...].astype(F32) * (1.0 / math.sqrt(HEAD_DIM))
    outs = []
    for h in range(heads):
        qh = jnp.where(head_lanes(rows, width, h), q, 0.0).astype(BF16)
        s = jnp.where(same, dot(k_ref[...], qh, NT), LOWEST)
        peak = jnp.max(s, axis=0, keepdims=True)
        e = jnp.exp(s - peak)
        total = jnp.sum(e, axis=0, keepdims=True)
        lse_ref[h : h + 1, :] = peak + jnp.log(total)
        p = (e * (1.0 / total)).astype(BF16)
        outs.append(dot(vt_ref[h * HEAD_DIM : (h + 1) * HEAD_DIM, :], p, NN))
    mixed = jnp.concatenate(outs, axis=0).T.astype(BF16)
    for i in range(2):

        @pl.when(step == i)
        def _():
            outs_ref[i][...] = mixed


def attend(ix, q, k, v, quarter, qrow, krow, first):
    rows, keys = q[0].shape[0], k[0].shape[0]
    heads, block = quarter // HEAD_DIM, rows // 4
    return call(
        functools.partial(attend_kernel, heads),
        "attend",
        (ix, krow, qrow, q[0], k[0], v[0]),
        [shape_of((block, quarter))] * 2 + [shape_of((heads, 2 * block), F32)],
        scratch=[pltpu.VMEM((quarter, keys), BF16), pltpu.VMEM((keys, 128), F32)],
        grid=(2,),
        room=ROOM * keys // rows,
        flops=2 * rows * keys * quarter,
        transcendentals=rows * keys * heads // 2,
        in_specs={
            1: pl.BlockSpec((1, block), lambda i: (0, i + first)),
            2: pl.BlockSpec((block, quarter), lambda i, c=q[1]: (i + first, c)),
            3: pl.BlockSpec((keys, quarter), lambda i, c=k[1]: (0, c)),
            4: pl.BlockSpec((keys, quarter), lambda i, c=v[1]: (0, c)),
        },
        out_specs={2: pl.BlockSpec((heads, block), lambda i: (0, i))},
    )


def attend_back_kernel(heads, more, ix, krow_ref, qrow_ref, lse_ref, q_ref, k_ref, v_ref, *refs):
    do_refs, kept, refs = refs[:2], refs[2 : 2 + more], refs[2 + more :]
    dq_ref, dkv_ref, kt_ref, ksc_ref, dka_ref, dva_ref, do_ref = refs
    width = q_ref.shape[1]
    step = pl.program_id(0)

    @pl.when(step == 0)
    def _():
        kt_ref[...] = k_ref[...].astype(F32).T.astype(BF16)
        ksc_ref[...] = column(krow_ref[...])
        if more:
            dka_ref[...] = kept[0][:, :width]
            dva_ref[...] = kept[0][:, width:]
        else:
            dka_ref[...] = jnp.zeros_like(dka_ref)
            dva_ref[...] = jnp.zeros_like(dva_ref)

    for i in range(2):

        @pl.when(step == i)
        def _():
            do_ref[...] = do_refs[i][...].astype(F32)

    rows, width = q_ref.shape
    scale = 1.0 / math.sqrt(HEAD_DIM)
    same = same_scene(ksc_ref[...], qrow_ref[...])
    q = q_ref[...].astype(F32) * scale
    do = do_ref[...]
    outs = []
    for h in range(heads):
        mine = head_lanes(rows, width, h)
        qh = jnp.where(mine, q, 0.0).astype(BF16)
        doh = jnp.where(mine, do, 0.0).astype(BF16)
        s = jnp.where(same, dot(k_ref[...], qh, NT), LOWEST)
        p = jnp.exp(s - lse_ref[h : h + 1, :])
        dp = dot(v_ref[...], doh, NT)
        inner = jnp.sum(p * dp, axis=0, keepdims=True)
        ds = (p * (dp - inner)).astype(BF16)
        dva_ref[...] += dot(p.astype(BF16), doh, NN)
        dka_ref[...] += dot(ds, qh, NN)
        outs.append(dot(kt_ref[h * HEAD_DIM : (h + 1) * HEAD_DIM, :], ds, NN))
    dq_ref[...] = (jnp.concatenate(outs, axis=0).T * scale).astype(BF16)

    @pl.when(step == pl.num_programs(0) - 1)
    def _():
        dkv_ref[:, :width] = dka_ref[...].astype(dkv_ref.dtype)
        dkv_ref[:, width:] = dva_ref[...].astype(dkv_ref.dtype)


def attend_back(ix, q, k, v, quarter, qrow, krow, lse, do, first, kept):
    rows, keys = q[0].shape[0], k[0].shape[0]
    heads, block = quarter // HEAD_DIM, rows // 4
    return call(
        functools.partial(attend_back_kernel, heads, len(kept)),
        "attend_back",
        (ix, krow, qrow, lse, q[0], k[0], v[0], *do, *kept),
        [shape_of((2 * block, quarter)), shape_of((keys, 2 * quarter), BF16 if kept else F32)],
        scratch=[
            pltpu.VMEM((quarter, keys), BF16),
            pltpu.VMEM((keys, 128), F32),
            pltpu.VMEM((keys, quarter), F32),
            pltpu.VMEM((keys, quarter), F32),
            pltpu.VMEM((block, quarter), F32),
        ],
        grid=(2,),
        room=ROOM * keys // rows,
        flops=5 * rows * keys * quarter,
        transcendentals=rows * keys * heads // 2,
        in_specs={
            1: pl.BlockSpec((1, block), lambda i: (0, i + first)),
            2: pl.BlockSpec((heads, block), lambda i: (0, i)),
            3: pl.BlockSpec((block, quarter), lambda i, c=q[1]: (i + first, c)),
            4: pl.BlockSpec((keys, quarter), lambda i, c=k[1]: (0, c)),
            5: pl.BlockSpec((keys, quarter), lambda i, c=v[1]: (0, c)),
        },
        out_specs={0: pl.BlockSpec((block, quarter), lambda i: (i, 0))},
    )


def mix_out_kernel(run, ix, m0, m1, m2, m3, near, far, x, gains, mixed_ref, hidden_ref, n_ref):
    rank, core = ix[0], ix[1]
    quarter, half = m0.shape[1], near.shape[1]
    for p, m in enumerate((m0, m1, m2, m3)):
        mixed_ref[:, at((rank ^ p) * quarter, quarter, 128)] = m[...]
    mixed = mixed_ref[...]
    hidden_ref[0:run, :] = x[0:run, :].astype(F32)
    hidden_ref[run:, :] = x[run + 8 : 2 * run + 8, :].astype(F32)
    hidden_ref[:, at(core * half, half, 128)] += dot(mixed, near[...], NN)
    hidden_ref[:, at((1 - core) * half, half, 128)] += dot(mixed, far[...], NN)
    std, _ = centre(hidden_ref[...])
    n_ref[...] = (std * gains[2:3, :] + gains[3:4, :]).astype(BF16)


def hidden_units_kernel(parts, blocks, ix, *refs):
    n, rows = len(parts), refs[0].shape[0]
    norms, dys, refs = refs[:n], refs[n : 2 * n], refs[2 * n :]
    if blocks:
        second, act_ref, dup_ref, *term_refs, up_ref, down_ref = refs
        units = up_ref.shape[1]
        for src, dst, size in blocks:
            up_ref[dst : dst + size, :] = second[src : src + size, :units]
        down_ref[...] = second[:, units:]
    else:
        up_ref, down_ref, act_ref, dup_ref, *term_refs = refs
    for i in range(n):
        span = slice(i * rows, (i + 1) * rows)
        u = dot(norms[i][...], up_ref[...], NN)
        cdf = 0.5 * (1.0 + lax.erf(u * math.sqrt(0.5)))
        act = (u * cdf).astype(BF16)
        act_ref[span, :] = act
        term_refs[n + i][...] = dot(act, down_ref[...], NN).astype(term_refs[n + i].dtype)
        slope = cdf + u * jnp.exp(-0.5 * u * u) * (1.0 / math.sqrt(2.0 * math.pi))
        dup = (dot(dys[i][...], down_ref[...], NT) * slope).astype(BF16)
        dup_ref[span, :] = dup
        term_refs[i][...] = dot(dup, up_ref[...], NT).astype(term_refs[i].dtype)


def hidden_back_kernel(ix, keep, got, across, hidden, dy, gains, near, far, *refs):
    parts, (dh_ref, low_ref, sums_ref) = refs[:4], refs[4:]
    rank, core = ix[0], ix[1]
    rows = hidden.shape[0]
    half, quarter = near.shape[1], parts[0].shape[1]
    d_norm = keep[...] + got[...].astype(F32) + across[...].astype(F32)
    std, inv = centre(hidden[...])
    sums_ref[...] = jnp.zeros_like(sums_ref)
    sums_ref[2:3, :] = jnp.sum(d_norm * std, axis=0, keepdims=True)
    sums_ref[3:4, :] = jnp.sum(d_norm, axis=0, keepdims=True)
    d_hidden = dy[...].astype(F32) + norm_back(d_norm, std, inv, gains[2:3, :])
    dh_ref[...] = d_hidden
    low_ref[...] = d_hidden.astype(BF16)
    a, b = low_ref[:, at(core * half, half, 128)], low_ref[:, at((1 - core) * half, half, 128)]
    for p in range(4):
        rows_p = at((rank ^ p) * quarter, quarter, 16)
        parts[p][...] = (dot(a, near[rows_p, :], NT) + dot(b, far[rows_p, :], NT)).astype(BF16)


def out_grad_kernel(ix, mixed, low, near_ref, far_ref):
    core, half = ix[1], near_ref.shape[1]
    left = mixed[...].astype(F32).T.astype(BF16)
    near_ref[...] = dot(left, low[:, at(core * half, half, 128)], NN)
    far_ref[...] = dot(left, low[:, at((1 - core) * half, half, 128)], NN).astype(BF16)


def project_back_kernel(run, ix, *refs):
    taken, (dq_a, dq_b, dkv, w, sums2, keep_ref, give_ref, cols_ref, sums) = refs[:4], refs[4:]
    step = pl.program_id(0)
    quarter, rows = dq_a.shape[1], dkv.shape[0]

    @pl.when(step == 0)
    def _():
        sums[...] = jnp.zeros_like(sums)
        sums[0:8, :] = sums2[...]

    for i, p in enumerate((1, 3, 0, 2)):

        @pl.when(step == i)
        def _():
            x = taken[p]
            std, _ = centre(jnp.concatenate([x[0:run, :], x[run + 8 : 2 * run + 8, :]], 0).astype(F32))
            dq = (dq_a, dq_b)[p >> 1][(p & 1) * rows : ((p & 1) + 1) * rows, :]
            part = dot(dq, w[:, 0:quarter], NT) + dot(dkv[...], w[:, quarter:], NT)
            sums[0:1, :] += jnp.sum(part * std, axis=0, keepdims=True)
            sums[1:2, :] += jnp.sum(part, axis=0, keepdims=True)
            if p & 1:
                give_ref[(p >> 1) * rows : ((p >> 1) + 1) * rows, :] = part.astype(BF16)
            else:
                keep_ref[(p >> 1) * rows : ((p >> 1) + 1) * rows, :] = part

    @pl.when(step == 3)
    def _():
        cols_ref[...] = sums[...].T.astype(BF16)


def tokens_back_kernel(run, ix, keep, got, across, x, d_hidden, gains, one_ref, two_ref):
    rows = d_hidden.shape[0]
    d_norm = keep[0:rows, :] + got[0:rows, :].astype(F32) + across[...].astype(F32)
    std, inv = centre(jnp.concatenate([x[0:run, :], x[run + 8 : 2 * run + 8, :]], 0).astype(F32))
    d = (d_hidden[...] + norm_back(d_norm, std, inv, gains[0:1, :])).astype(BF16)
    one_ref[...] = d[0:run]
    two_ref[...] = d[run:]


def grads_kernel(blocks, n_left, widths, n_right, extra, ix, *refs):
    lefts, refs = refs[:n_left], refs[n_left:]
    rights, refs = [refs[i * n_right : (i + 1) * n_right] for i in range(len(widths))], refs[len(widths) * n_right :]
    out_ref, left_t, *right_refs = refs[extra:]
    step = pl.program_id(0)
    cols = sum(widths)

    @pl.when(step == 0)
    def _():
        at_col = 0
        for piece in lefts:
            t = piece[...].T
            stop = at_col + t.shape[1]
            for dst, src, size in blocks:
                left_t[dst : dst + size, at_col:stop] = t[src : src + size, :]
            at_col = stop
        for pieces, ref in zip(rights, right_refs):
            row = 0
            for piece in pieces:
                ref[row : row + piece.shape[0], :] = piece[...]
                row += piece.shape[0]

    rows = out_ref.shape[0]
    mine = left_t[at(step * rows, rows, 16), :]
    start = 0
    for ref, w in zip(right_refs, widths):
        out_ref[:, start : start + w] = dot(mine, ref[...], NN).astype(BF16)
        start += w
    if extra:
        near, far, columns = refs[:3]
        half = near.shape[1]
        for i in range(left_t.shape[0] // rows):

            @pl.when(step == i)
            def _():
                for dst, src, size in blocks:
                    if i * rows <= dst < (i + 1) * rows:
                        span = slice(dst - i * rows, dst - i * rows + size)
                        both = near[src : src + size, :] + far[src : src + size, :].astype(F32)
                        out_ref[span, cols : cols + half] = both.astype(BF16)
                        out_ref[span, cols + half :] = columns[src : src + size, :]


def grad_ff_kernel(blocks, ix, n3, n2, n1, n0, u3, u2, u10, a3, a2, a10, d3, d2, d1, d0, out_ref, nt, at_t, up, dy):
    step = pl.program_id(0)
    depth = n3.shape[0]

    @pl.when(step == 0)
    def _():
        for i, (n, d) in enumerate(((n3, d3), (n2, d2), (n1, d1), (n0, d0))):
            span = slice(i * depth, (i + 1) * depth)
            t = n[...].T
            for dst, src, size in blocks:
                nt[dst : dst + size, span] = t[src : src + size, :]
            dy[span, :] = d[...]
        for first, a, u in ((0, a3, u3), (1, a2, u2), (2, a10, u10)):
            span = slice(first * depth, first * depth + a.shape[0])
            at_t[:, span] = a[...].T
            up[span, :] = u[...]

    rows, units = out_ref.shape[0], up.shape[1]
    mine = at(step * rows, rows, 16)
    out_ref[:, :units] = dot(nt[mine, :], up[...], NN).astype(BF16)
    out_ref[:, units:] = dot(at_t[mine, :], dy[...], NN).astype(BF16)


def home_kernel(ix, summed, *parts):
    core, y = ix[1], ix[3]
    rows, cols = parts[0].shape
    for p in range(4):
        block = (core ^ (p & 1)) * 2 + (y ^ (p >> 1))
        parts[p][...] = summed[at(block * rows, rows, 8), 0:cols]


def settle_kernel(ix, p0, p1, p2, p3, qkv_ref, out_ref, vec_ref, tile):
    rank, core = ix[0], ix[1]
    parts = (p0, p1, p2, p3)
    rows, width = out_ref.shape
    quarter, half = width // 4, width // 2
    for p in range(4):
        a = rank ^ p
        for t in range(3):
            qkv_ref[:, at(t * width + a * quarter, quarter, 128)] = parts[p][:, t * quarter : (t + 1) * quarter].astype(F32)
    c1, c2 = 3 * quarter, 3 * quarter + half
    for p in range(2):
        out_ref[:, at((core ^ p) * half, half, 128)] = parts[p][:, c1:c2].astype(F32) + parts[p + 2][:, c1:c2].astype(F32)
    tile[...] = jnp.zeros_like(tile)
    tile[0:rows, :] = sum(v[:, c2:].astype(F32) for v in parts)
    vec_ref[...] = tile[...].T[0:8, :]


def settle_ff_kernel(spots, ix, p0, p1, p2, p3, up_ref):
    core, y = ix[1], ix[3]
    hid, zs = 128, len(spots) // 2
    for p, part in enumerate((p0, p1, p2, p3)):
        c2, y2 = core ^ (p & 1), y ^ (p >> 1)
        for b, (nx, nz) in enumerate(spots):
            dst = ((nx * 2 + c2) * zs + nz) * 2 + y2
            up_ref[:, at(dst * hid, hid, 128)] = part[:, b * hid : (b + 1) * hid].astype(F32)


class Places:
    def __init__(self, mesh):
        self.n_dp, self.n_fsdp = mesh.shape["dp"], mesh.shape["fsdp"]
        self.xs, self.zs = self.n_dp // 2, self.n_fsdp // 2
        self.nodes = self.xs * self.zs
        self.all = [
            (x, c, z, y) for x in range(self.xs) for c in range(2) for z in range(self.zs) for y in range(2)
        ]

    def lin(self, x, c, z, y):
        return (x * 2 + c) * self.n_fsdp + z * 2 + y

    def perm(self, move):
        return [(self.lin(*d), self.lin(*move(*d))) for d in self.all]

    def spot(self, x, z):
        return x * self.zs + (z if x % 2 == 0 else self.zs - 1 - z)

    def node(self, spot):
        x, z = spot // self.zs, spot % self.zs
        return (x, z if x % 2 == 0 else self.zs - 1 - z)

    def rings(self):
        return [
            [self.lin(x, c, z, y) for x, z in map(self.node, range(self.nodes))] for c in range(2) for y in range(2)
        ]


def permute(array, pairs):
    return lax.ppermute(array, AXES, pairs)


def after(value, *done):
    return lax.optimization_barrier((value,) + done)[0]


def body(pc, tokens, scene_ids, w_qkv, w_out, w_up, w_down, gain_one, bias_one, gain_two, bias_two, cotangent):
    micro, run, width = tokens.shape
    rows = w_qkv.shape[0]
    ff = w_up.shape[1]
    units = ff // 4
    hid = w_down.shape[0]
    quarter, half = width // 4, width // 2
    own = micro * run
    dp, fsdp = lax.axis_index("dp"), lax.axis_index("fsdp")
    x, core, z, y = dp // 2, dp % 2, fsdp // 2, fsdp % 2
    rank = y * 2 + core
    groups = micro * 2
    quads = pc.zs // groups
    rings = pc.rings()
    spots = [pc.node(i) for i in range(pc.nodes)]
    blocks = row_blocks(spots, 2 * rows)
    aligned = hid % 128 == 0

    p_core = pc.perm(lambda x, c, z, y: (x, 1 - c, z, y))
    p_y = pc.perm(lambda x, c, z, y: (x, c, z, 1 - y))
    p_diag = pc.perm(lambda x, c, z, y: (x, 1 - c, z, 1 - y))

    def place_perm(flip):
        def move(x, c, z, y):
            m = (z % 2) ^ flip
            return (x, (z // 2) % 2, (m * 2 + c) * quads + z // 4, y)

        return pc.perm(move)

    p_place = [place_perm(0), place_perm(1)]
    p_back = [[(b, a) for a, b in pairs] for pairs in p_place]

    def group_perm(by):
        return pc.perm(lambda x, c, z, y: (x, c, z // quads * quads + (z + by) % quads, y))

    ix = jnp.stack([rank, core, z % 2, y]).astype(jnp.int32)

    def quad_swap(parts):
        return [parts[0], permute(parts[1], p_core), permute(parts[2], p_y), permute(parts[3], p_diag)]

    def by_rank(parts):
        odd, top = rank % 2 == 1, rank // 2 == 1
        parts = [jnp.where(odd, parts[i ^ 1], parts[i]) for i in range(4)]
        return [jnp.where(top, parts[i ^ 2], parts[i]) for i in range(4)]

    def by_rows(parts):
        r = by_rank(parts)
        return jnp.concatenate([r[0], r[2], r[1], r[3]], 0)

    def ring_gather(shard):
        return lax.all_gather(shard, AXES, axis=0, tiled=True, axis_index_groups=rings)

    def ring_sum(terms):
        return lax.psum_scatter(terms, AXES, scatter_dimension=0, tiled=True, axis_index_groups=rings)

    c_out, c_small, wide = 3 * quarter, 3 * quarter + half, 3 * quarter + half + 128
    wu = w_up
    if not aligned:
        wu = w_up.reshape(rows, pc.xs, 2, pc.zs, 2, hid)
        wu = [
            lax.dynamic_slice(
                wu, (0, 0, core ^ (p & 1), 0, y ^ (p >> 1), 0), (rows, pc.xs, 1, pc.zs, 1, hid)
            ).reshape(rows, pc.xs, pc.zs, hid)
            for p in range(4)
        ]
        wu = jnp.concatenate([w[:, nx, nz] for w in wu for nx, nz in spots], 1)
    *packed, x_one, x_two, dy_one, dy_two = call(
        functools.partial(pack_kernel, aligned, spots),
        "pack",
        (
            ix,
            w_qkv,
            w_out,
            jnp.stack([gain_one, bias_one, gain_two, bias_two]),
            tokens,
            scene_ids.reshape(micro, run),
            cotangent,
            wu,
        ),
        [shape_of((rows, wide))] * 4 + [shape_of((rows, units))] * 4 + [shape_of((run + 8, width))] * 2 + [shape_of((run, width))] * 2,
        scratch=[pltpu.VMEM((128, 128), F32)],
        room=58,
    )
    shard = by_rows(quad_swap(packed[:4]))
    x_own = jnp.concatenate([permute(x_one, p_place[0]), permute(x_two, p_place[1])], 0)
    first = ring_gather(after(shard, x_own))
    x_across = permute(x_own, p_y)
    taken = [x_own, permute(x_own, p_core), x_across, permute(x_across, p_core)]
    up_shard = by_rows(quad_swap(after(packed[4:], x_across)))
    second = ring_gather(after(jnp.concatenate([up_shard, w_down], 1), taken))
    dy_one, dy_two = after((dy_one, dy_two), first)
    dy_own = jnp.concatenate([permute(dy_one, p_place[0]), permute(dy_two, p_place[1])], 0)

    block = (own, width)
    n_one, projected, full_qkv, near_out, gains, qrow = call(
        functools.partial(project_kernel, blocks, run),
        "project",
        (ix, *taken, first),
        [
            shape_of((4 * own, width)),
            shape_of((4 * own, 3 * quarter)),
            shape_of((width, 3 * quarter)),
            shape_of((width, half)),
            shape_of((8, width), F32),
            shape_of((1, 4 * own), F32),
        ],
        scratch=[pltpu.VMEM((width, 128), F32)],
        grid=(4,),
        flops=2 * 4 * own * width * 3 * quarter,
        out_specs={
            0: pl.BlockSpec(block, lambda i: (i, 0)),
            1: pl.BlockSpec((own, 3 * quarter), lambda i: (i, 0)),
        },
    )
    far_out = permute(near_out, p_core)
    if quads == 1:
        q, k, v, krow = (projected, 0), (projected, 1), (projected, 2), qrow
    else:
        kv = projected[:, quarter:]
        kv_all = jnp.concatenate([kv] + [permute(kv, group_perm(s)) for s in range(1, quads)], 0)
        krow = jnp.concatenate([qrow] + [permute(qrow, group_perm(s)) for s in range(1, quads)], 1)
        q, k, v = (projected, 0), (kv_all, 0), (kv_all, 1)
    *m_far, lse_far = attend(ix, q, k, v, quarter, qrow, krow, 2)
    dy_across = permute(after(dy_own, m_far), p_y)
    *m_near, lse_near = attend(ix, q, k, v, quarter, after(qrow, m_far, dy_own), krow, 0)
    mixed = quad_swap([*m_near, *m_far])
    mixed_own, hidden, n_two = call(
        functools.partial(mix_out_kernel, run),
        "mix_out",
        (ix, *mixed, near_out, far_out, taken[0], gains),
        [shape_of(block), shape_of(block, F32), shape_of(block)],
        flops=2 * own * width * width,
    )
    def far_sum(keep, got):
        return (keep + got.astype(F32)).astype(BF16)

    n_across = permute(after(n_two, dy_across), p_y)
    norms = [n_two, permute(n_two, p_core), n_across, permute(n_across, p_core)]
    dys = [dy_own, permute(dy_own, p_core), dy_across, permute(dy_across, p_core)]

    def hidden_units(parts, weights, kinds, order):
        outs = [shape_of((len(parts) * own, units))] * 2 + [shape_of(block, kind) for kind in kinds * 2]
        return call(
            functools.partial(hidden_units_kernel, parts, order),
            "hidden_units",
            (ix, *[norms[p] for p in parts], *[dys[p] for p in parts], *weights),
            outs + ([shape_of((width, units)), shape_of((units, width))] if order else []),
            flops=8 * len(parts) * own * width * units,
            transcendentals=2 * len(parts) * own * units,
        )

    act3, up3, give3, r_give3, full_up, full_down = hidden_units((3,), (second,), (BF16,), blocks)
    got3 = permute(give3, p_core)
    act2, up2, keep2, r_keep2 = hidden_units((2,), (after(full_up, give3), full_down), (F32,), None)
    far = far_sum(keep2, got3)
    across = permute(far, p_y)
    act10, up10, give1, keep0, r_give1, r_keep0 = hidden_units((1, 0), (after(full_up, far), full_down), (BF16, F32), None)
    got = permute(give1, p_core)
    in_order = [(i, i, n) for i, _, n in blocks]

    def grads(name, lefts, rights, order, extra=()):
        widths = tuple(r[0].shape[1] for r in rights)
        depth, cols = sum(a.shape[0] for a in lefts), sum(widths)
        height = lefts[0].shape[1]
        total = cols + sum(e.shape[1] for e in extra[1:])
        return call(
            functools.partial(grads_kernel, order, len(lefts), widths, len(rights[0]), len(extra)),
            name,
            (ix, *lefts, *[piece for r in rights for piece in r], *extra),
            [shape_of((height, total))],
            scratch=[pltpu.VMEM((height, depth), BF16)] + [pltpu.VMEM((depth, w), BF16) for w in widths],
            grid=(4,),
            flops=2 * depth * height * cols,
            out_specs={0: pl.BlockSpec((height // 4, total), lambda i: (i, 0))},
        )[0]

    order = (3, 2, 1, 0)
    (ff_terms,) = call(
        functools.partial(grad_ff_kernel, blocks),
        "grad_ff",
        (ix, *[norms[p] for p in order], up3, up2, up10, act3, act2, act10, *[dys[p] for p in order]),
        [shape_of((width, units + width))],
        scratch=[pltpu.VMEM((width, 4 * own), BF16), pltpu.VMEM((units, 4 * own), BF16)]
        + [pltpu.VMEM((4 * own, units), BF16), pltpu.VMEM((4 * own, width), BF16)],
        grid=(4,),
        flops=2 * 4 * own * width * 2 * units,
        out_specs={0: pl.BlockSpec((width // 4, units + width), lambda i: (i, 0))},
    )
    ff_sum = ring_sum(ff_terms)
    up_sum, down_sum = ff_sum[:, :units], ff_sum[:, units:]
    *d_parts, d_hidden, d_low, sums_two = call(
        hidden_back_kernel,
        "hidden_back",
        (ix, keep0, got, across, hidden, dys[0], after(gains, ff_terms), near_out, far_out),
        [shape_of((own, quarter))] * 4 + [shape_of(block, F32), shape_of(block), shape_of((8, width), F32)],
        flops=2 * own * width * width,
    )
    d_mixed = quad_swap(d_parts)
    near_parts, far_parts = d_mixed[:2], d_mixed[2:]
    r_far = far_sum(r_keep2, permute(after(r_give3, d_parts[0]), p_core))
    r_across = permute(r_far, p_y)
    r_got = permute(after(r_give1, d_parts[0]), p_core)
    dq_near, kept = attend_back(ix, q, k, v, quarter, qrow, krow, lse_near, near_parts, 0, ())
    dq_far, dkv = attend_back(ix, q, k, v, quarter, qrow, krow, lse_far, far_parts, 2, (after(kept, r_far),))

    def placed(one, two):
        return [permute(one, p_back[0]), permute(two, p_back[1])]

    r_own = (after(hidden, dq_far) + r_keep0 + r_got.astype(F32) + r_across.astype(F32)).astype(BF16)
    back_out = placed(r_own[:run], r_own[run:])
    n_rows = dkv.shape[0] // quads
    if quads > 1:
        total = dkv[:n_rows].astype(F32)
        for s in range(1, quads):
            total = total + permute(dkv[s * n_rows : (s + 1) * n_rows], group_perm(-s)).astype(F32)
        dkv = total.astype(BF16)

    keep_one, give_one, columns = call(
        functools.partial(project_back_kernel, run),
        "project_back",
        (ix, *taken, dq_near, dq_far, dkv, full_qkv, after(sums_two, r_own)),
        [shape_of((2 * own, width), F32), shape_of((2 * own, width)), shape_of((width, 128))],
        scratch=[pltpu.VMEM((128, width), F32)],
        grid=(4,),
        flops=2 * 4 * own * width * 3 * quarter,
        in_specs={
            6: pl.BlockSpec((own, 2 * quarter), lambda i: (jnp.where(i == 0, 1, jnp.where(i == 1, 3, (i - 2) * 2)), 0)),
        },
    )
    got_one = permute(give_one, p_core)
    grad_near, grad_far = call(
        out_grad_kernel,
        "out_grad",
        (ix, after(mixed_own, give_one), d_low),
        [shape_of((width, half), F32), shape_of((width, half))],
        flops=2 * own * width * width,
    )
    far_one = far_sum(keep_one[own:], after(got_one, grad_near)[own:])
    across_one = permute(far_one, p_y)
    at_terms = grads(
        "grad_at",
        [after(n_one, far_one)],
        [[jnp.concatenate([dq_near, dq_far], 0)], [dkv]],
        blocks,
        (grad_near, permute(grad_far, p_core), columns),
    )
    one_sum = ring_sum(after(at_terms, ff_sum, back_out))

    def home(name, summed):
        return quad_swap(call(home_kernel, name, (ix, summed), [shape_of((rows, summed.shape[1]))] * 4))

    def in_batches(one, two):
        return jnp.stack([jnp.where(z % 2 == 0, one, two), jnp.where(z % 2 == 0, two, one)], 0)

    d_one, d_two = call(
        functools.partial(tokens_back_kernel, run),
        "tokens_back",
        (ix, keep_one, got_one, across_one, taken[0], d_hidden, after(gains, ff_sum, back_out)),
        [shape_of((run, width))] * 2,
    )
    back_grad = placed(d_one, d_two)
    at_home = home("home_at", after(one_sum, back_out, back_grad))
    output = in_batches(*after(back_out, at_home[0]))
    input_grad = in_batches(*after(back_grad, at_home[0])).astype(F32)
    ff_home = home("home_up", after(up_sum, d_one))
    own_down = down_sum.astype(F32)
    if aligned:
        (own_up,) = call(
            functools.partial(settle_ff_kernel, spots), "settle_ff", (ix, *ff_home), [shape_of((rows, 4 * units), F32)])
    else:
        ups = [b.reshape(rows, pc.nodes, hid) for b in ff_home]
        at_spot = [[spots.index((nx, nz)) for nz in range(pc.zs)] for nx in range(pc.xs)]
        ups = by_rank([jnp.stack([jnp.stack([b[:, i] for i in row], 1) for row in at_spot], 1) for b in ups])
        own_up = (
            jnp.stack([jnp.stack([ups[0], ups[2]], 3), jnp.stack([ups[1], ups[3]], 3)], 2)
            .reshape(rows, 4 * units)
            .astype(F32)
        )
    own_qkv, own_out, vectors = call(
        settle_kernel,
        "settle",
        (ix, *at_home),
        [shape_of((rows, 3 * width), F32), shape_of((rows, width), F32), shape_of((8, 128), F32)],
        scratch=[pltpu.VMEM((128, 128), F32)],
    )
    return (output, input_grad, own_qkv, own_out, own_up, own_down) + tuple(vectors[i, :rows] for i in range(4))


def solution(mesh):
    vector, matrix, batch = P(AXES), P(AXES, None), P(None, AXES, None)
    return jax.shard_map(
        functools.partial(body, Places(mesh)),
        mesh=mesh,
        in_specs=(batch, P(None, "dp", "fsdp")) + (matrix,) * 4 + (vector,) * 4 + (batch,),
        out_specs=(batch, batch) + (matrix,) * 4 + (vector,) * 4,
        check_vma=False,
    )
```

```python
import functools
import math

import jax
import jax.numpy as jnp
from jax import lax
from jax.experimental import pallas as pl
from jax.experimental.pallas import tpu as pltpu
from jax.sharding import PartitionSpec as P

AXES = ("dp", "fsdp")
HEAD_DIM = 64
EPS = 1e-05
LOWEST = -1000000000.0
F32 = jnp.float32
BF16 = jnp.bfloat16
NT = (((1,), (1,)), ((), ()))
TN = (((0,), (0,)), ((), ()))
NN = (((1,), (0,)), ((), ()))
ROOM = 20
IN_HBM = ("grad_ff", "grad_at")
HINTS = {"home_at": 1000, "settle": 8, "mix_out": 0, "grad_ff": 3, "hidden_units": 8, "hidden_back": 300, "attend_back": 4, "grad_down": 0, "home_up": 0, "settle_ff": 0, "out_grad": 0, "project_back": 0, "grad_at": 0, "tokens_back": 0, "down": 8}


def dot(left, right, dims):
    return lax.dot_general(left, right, dims, preferred_element_type=F32)


def at(start, size, step):
    return pl.ds(pl.multiple_of(start, step), size)


def call(kernel, name, args, outs, scratch=(), grid=None, flops=0, transcendentals=0, in_specs=None, out_specs=None, room=ROOM):
    whole = pl.BlockSpec(memory_space=pltpu.VMEM) if grid is None else None

    def spec(shape):
        return whole or pl.BlockSpec(shape, lambda i, n=len(shape): (0,) * n)

    specs = [pl.BlockSpec(memory_space=pltpu.SMEM)]
    specs += [(in_specs or {}).get(n) or spec(a.shape) for n, a in enumerate(args[1:])]
    size = sum(math.prod(a.shape) * a.dtype.itemsize for a in list(args) + list(outs))
    return pl.pallas_call(
        kernel,
        out_shape=tuple(pltpu.HBM(o.shape, o.dtype) for o in outs) if name in IN_HBM else tuple(outs),
        in_specs=specs,
        out_specs=tuple((out_specs or {}).get(n) or spec(o.shape) for n, o in enumerate(outs)),
        scratch_shapes=list(scratch),
        compiler_params=pltpu.CompilerParams(vmem_limit_bytes=min(room, 58) * 1024 * 1024),
        cost_estimate=pl.CostEstimate(
            flops=HINTS.get(name, 8) * flops, bytes_accessed=HINTS.get(name, 8) * size, transcendentals=transcendentals
        ),
        name=name,
        **({} if grid is None else {"grid": grid}),
    )(*args)


def shape_of(shape, dtype=BF16):
    return jax.ShapeDtypeStruct(shape, dtype)


def centre(v):
    c = v - jnp.mean(v, axis=-1, keepdims=True)
    inv = lax.rsqrt(jnp.mean(c * c, axis=-1, keepdims=True) + EPS)
    return c * inv, inv


def norm_back(d_norm, std, inv, gain):
    d_std = d_norm * gain
    return inv * (
        d_std - jnp.mean(d_std, axis=-1, keepdims=True) - std * jnp.mean(d_std * std, axis=-1, keepdims=True)
    )


def pack_kernel(aligned, spots, ix, qkv, out, gains, tokens, scenes, dy, up, *refs):
    parts, ups, (one, two, dy_one, dy_two, tile) = refs[:4], refs[4:8], refs[8:]
    rank, core, odd, y = ix[0], ix[1], ix[2], ix[3]
    rows, width = qkv.shape[0], out.shape[1]
    quarter, half = width // 4, width // 2
    tile[...] = jnp.zeros_like(tile)
    tile[0:4, 0:rows] = gains[...].astype(F32)
    small = tile[...].T[:rows].astype(BF16)
    c1, c2 = 3 * quarter, 3 * quarter + half
    hid, units = 128, up.shape[1] // 4
    zs = len(spots) // 2
    for p in range(4):
        a = rank ^ p
        for t in range(3):
            parts[p][:, t * quarter : (t + 1) * quarter] = qkv[:, at(t * width + a * quarter, quarter, 128)]
        parts[p][:, c1:c2] = out[:, at((core ^ (p & 1)) * half, half, 128)]
        parts[p][:, c2 : c2 + 128] = small
        if aligned:
            for b, (nx, nz) in enumerate(spots):
                src = ((nx * 2 + (core ^ (p & 1))) * zs + nz) * 2 + (y ^ (p >> 1))
                ups[p][:, b * hid : (b + 1) * hid] = up[:, at(src * hid, hid, 128)]
        else:
            ups[p][...] = up[:, p * units : (p + 1) * units]
    run = tokens.shape[1]
    for ref, low, m in ((one, dy_one, odd), (two, dy_two, 1 - odd)):
        ref[0:run, :] = tokens[m]
        ref[run:, :] = jnp.zeros((ref.shape[0] - run, width), BF16)
        ref[run : run + 1, 0:run] = scenes[pl.ds(m, 1), :].astype(F32).astype(BF16)
        low[...] = dy[m]


def row_blocks(spots, size):
    zs = len(spots) // 2
    return [
        ((2 * i + c) * size, ((nx * 2 + c) * zs + nz) * size, size) for i, (nx, nz) in enumerate(spots) for c in (0, 1)
    ]


def project_kernel(blocks, run, ix, *refs):
    taken, first = refs[:4], refs[4]
    n_ref, p_ref, w_ref, near_ref, gains_ref, scene_ref, g_all = refs[5:]
    step = pl.program_id(0)
    c_out, c_small = w_ref.shape[1], w_ref.shape[1] + near_ref.shape[1]

    @pl.when(step == 0)
    def _():
        for src, dst, size in blocks:
            v = first[src : src + size, :]
            w_ref[dst : dst + size, :] = v[:, :c_out]
            near_ref[dst : dst + size, :] = v[:, c_out:c_small]
            g_all[dst : dst + size, :] = v[:, c_small:].astype(F32)
        gains_ref[...] = g_all[...].T[0:8, :]
        for p in range(4):
            for s in range(2):
                row = taken[p][s * (run + 8) + run : s * (run + 8) + run + 1, 0:run]
                scene_ref[0:1, (2 * p + s) * run : (2 * p + s + 1) * run] = row.astype(F32)

    for p in range(4):

        @pl.when(step == p)
        def _():
            x = taken[p]
            v = jnp.concatenate([x[0:run, :], x[run + 8 : 2 * run + 8, :]], 0).astype(F32)
            std, _ = centre(v)
            n = (std * gains_ref[0:1, :] + gains_ref[1:2, :]).astype(BF16)
            n_ref[...] = n
            p_ref[...] = dot(n, w_ref[...], NN).astype(BF16)


def head_lanes(rows, width, head):
    lane = lax.broadcasted_iota(jnp.int32, (rows, width), 1)
    return (lane >= head * HEAD_DIM) & (lane < (head + 1) * HEAD_DIM)


def column(row):
    return jnp.broadcast_to(row, (128, row.shape[1])).T


def same_scene(ksc, qrow):
    return jnp.concatenate([ksc == qrow[:, i : i + 128] for i in range(0, qrow.shape[1], 128)], 1)


def attend_kernel(heads, ix, krow_ref, qrow_ref, q_ref, k_ref, v_ref, *refs):
    outs_ref, (lse_ref, vt_ref, ksc_ref) = refs[:2], refs[2:]
    step = pl.program_id(0)

    @pl.when(step == 0)
    def _():
        vt_ref[...] = v_ref[...].astype(F32).T.astype(BF16)
        ksc_ref[...] = column(krow_ref[...])

    rows, width = q_ref.shape
    same = same_scene(ksc_ref[...], qrow_ref[...])
    q = q_ref[...].astype(F32) * (1.0 / math.sqrt(HEAD_DIM))
    outs = []
    for h in range(heads):
        qh = jnp.where(head_lanes(rows, width, h), q, 0.0).astype(BF16)
        s = jnp.where(same, dot(k_ref[...], qh, NT), LOWEST)
        peak = jnp.max(s, axis=0, keepdims=True)
        e = jnp.exp(s - peak)
        total = jnp.sum(e, axis=0, keepdims=True)
        lse_ref[h : h + 1, :] = peak + jnp.log(total)
        p = (e * (1.0 / total)).astype(BF16)
        outs.append(dot(vt_ref[h * HEAD_DIM : (h + 1) * HEAD_DIM, :], p, NN))
    mixed = jnp.concatenate(outs, axis=0).T.astype(BF16)
    for i in range(2):

        @pl.when(step == i)
        def _():
            outs_ref[i][...] = mixed


def attend(ix, q, k, v, quarter, qrow, krow, first):
    rows, keys = q[0].shape[0], k[0].shape[0]
    heads, block = quarter // HEAD_DIM, rows // 4
    return call(
        functools.partial(attend_kernel, heads),
        "attend",
        (ix, krow, qrow, q[0], k[0], v[0]),
        [shape_of((block, quarter))] * 2 + [shape_of((heads, 2 * block), F32)],
        scratch=[pltpu.VMEM((quarter, keys), BF16), pltpu.VMEM((keys, 128), F32)],
        grid=(2,),
        room=ROOM * keys // rows,
        flops=2 * rows * keys * quarter,
        transcendentals=rows * keys * heads // 2,
        in_specs={
            1: pl.BlockSpec((1, block), lambda i: (0, i + first)),
            2: pl.BlockSpec((block, quarter), lambda i, c=q[1]: (i + first, c)),
            3: pl.BlockSpec((keys, quarter), lambda i, c=k[1]: (0, c)),
            4: pl.BlockSpec((keys, quarter), lambda i, c=v[1]: (0, c)),
        },
        out_specs={2: pl.BlockSpec((heads, block), lambda i: (0, i))},
    )


def attend_back_kernel(heads, more, ix, krow_ref, qrow_ref, lse_ref, q_ref, k_ref, v_ref, *refs):
    do_refs, kept, refs = refs[:2], refs[2 : 2 + more], refs[2 + more :]
    dq_ref, dkv_ref, kt_ref, ksc_ref, dka_ref, dva_ref, do_ref = refs
    width = q_ref.shape[1]
    step = pl.program_id(0)

    @pl.when(step == 0)
    def _():
        kt_ref[...] = k_ref[...].astype(F32).T.astype(BF16)
        ksc_ref[...] = column(krow_ref[...])
        if more:
            dka_ref[...] = kept[0][:, :width]
            dva_ref[...] = kept[0][:, width:]
        else:
            dka_ref[...] = jnp.zeros_like(dka_ref)
            dva_ref[...] = jnp.zeros_like(dva_ref)

    for i in range(2):

        @pl.when(step == i)
        def _():
            do_ref[...] = do_refs[i][...].astype(F32)

    rows, width = q_ref.shape
    scale = 1.0 / math.sqrt(HEAD_DIM)
    same = same_scene(ksc_ref[...], qrow_ref[...])
    q = q_ref[...].astype(F32) * scale
    do = do_ref[...]
    outs = []
    for h in range(heads):
        mine = head_lanes(rows, width, h)
        qh = jnp.where(mine, q, 0.0).astype(BF16)
        doh = jnp.where(mine, do, 0.0).astype(BF16)
        s = jnp.where(same, dot(k_ref[...], qh, NT), LOWEST)
        p = jnp.exp(s - lse_ref[h : h + 1, :])
        dp = dot(v_ref[...], doh, NT)
        inner = jnp.sum(p * dp, axis=0, keepdims=True)
        ds = (p * (dp - inner)).astype(BF16)
        dva_ref[...] += dot(p.astype(BF16), doh, NN)
        dka_ref[...] += dot(ds, qh, NN)
        outs.append(dot(kt_ref[h * HEAD_DIM : (h + 1) * HEAD_DIM, :], ds, NN))
    dq_ref[...] = (jnp.concatenate(outs, axis=0).T * scale).astype(BF16)

    @pl.when(step == pl.num_programs(0) - 1)
    def _():
        dkv_ref[:, :width] = dka_ref[...].astype(dkv_ref.dtype)
        dkv_ref[:, width:] = dva_ref[...].astype(dkv_ref.dtype)


def attend_back(ix, q, k, v, quarter, qrow, krow, lse, do, first, kept):
    rows, keys = q[0].shape[0], k[0].shape[0]
    heads, block = quarter // HEAD_DIM, rows // 4
    return call(
        functools.partial(attend_back_kernel, heads, len(kept)),
        "attend_back",
        (ix, krow, qrow, lse, q[0], k[0], v[0], *do, *kept),
        [shape_of((2 * block, quarter)), shape_of((keys, 2 * quarter), BF16 if kept else F32)],
        scratch=[
            pltpu.VMEM((quarter, keys), BF16),
            pltpu.VMEM((keys, 128), F32),
            pltpu.VMEM((keys, quarter), F32),
            pltpu.VMEM((keys, quarter), F32),
            pltpu.VMEM((block, quarter), F32),
        ],
        grid=(2,),
        room=ROOM * keys // rows,
        flops=5 * rows * keys * quarter,
        transcendentals=rows * keys * heads // 2,
        in_specs={
            1: pl.BlockSpec((1, block), lambda i: (0, i + first)),
            2: pl.BlockSpec((heads, block), lambda i: (0, i)),
            3: pl.BlockSpec((block, quarter), lambda i, c=q[1]: (i + first, c)),
            4: pl.BlockSpec((keys, quarter), lambda i, c=k[1]: (0, c)),
            5: pl.BlockSpec((keys, quarter), lambda i, c=v[1]: (0, c)),
        },
        out_specs={0: pl.BlockSpec((block, quarter), lambda i: (i, 0))},
    )


def mix_out_kernel(run, ix, m0, m1, m2, m3, near, far, x, gains, mixed_ref, hidden_ref, n_ref):
    rank, core = ix[0], ix[1]
    quarter, half = m0.shape[1], near.shape[1]
    for p, m in enumerate((m0, m1, m2, m3)):
        mixed_ref[:, at((rank ^ p) * quarter, quarter, 128)] = m[...]
    mixed = mixed_ref[...]
    hidden_ref[0:run, :] = x[0:run, :].astype(F32)
    hidden_ref[run:, :] = x[run + 8 : 2 * run + 8, :].astype(F32)
    hidden_ref[:, at(core * half, half, 128)] += dot(mixed, near[...], NN)
    hidden_ref[:, at((1 - core) * half, half, 128)] += dot(mixed, far[...], NN)
    std, _ = centre(hidden_ref[...])
    n_ref[...] = (std * gains[2:3, :] + gains[3:4, :]).astype(BF16)


def hidden_units_kernel(parts, blocks, ix, *refs):
    n, rows = len(parts), refs[0].shape[0]
    norms, dys, refs = refs[:n], refs[n : 2 * n], refs[2 * n :]
    if blocks:
        second, act_ref, dup_ref, *term_refs, up_ref, down_ref = refs
        units = up_ref.shape[1]
        for src, dst, size in blocks:
            up_ref[dst : dst + size, :] = second[src : src + size, :units]
        down_ref[...] = second[:, units:]
    else:
        up_ref, down_ref, act_ref, dup_ref, *term_refs = refs
    for i in range(n):
        span = slice(i * rows, (i + 1) * rows)
        u = dot(norms[i][...], up_ref[...], NN)
        cdf = 0.5 * (1.0 + lax.erf(u * math.sqrt(0.5)))
        act = (u * cdf).astype(BF16)
        act_ref[span, :] = act
        term_refs[n + i][...] = dot(act, down_ref[...], NN).astype(term_refs[n + i].dtype)
        slope = cdf + u * jnp.exp(-0.5 * u * u) * (1.0 / math.sqrt(2.0 * math.pi))
        dup = (dot(dys[i][...], down_ref[...], NT) * slope).astype(BF16)
        dup_ref[span, :] = dup
        term_refs[i][...] = dot(dup, up_ref[...], NT).astype(term_refs[i].dtype)


def hidden_back_kernel(ix, keep, got, across, hidden, dy, gains, near, far, *refs):
    parts, (dh_ref, low_ref, sums_ref) = refs[:4], refs[4:]
    rank, core = ix[0], ix[1]
    rows = hidden.shape[0]
    half, quarter = near.shape[1], parts[0].shape[1]
    d_norm = keep[...] + got[...].astype(F32) + across[...].astype(F32)
    std, inv = centre(hidden[...])
    sums_ref[...] = jnp.zeros_like(sums_ref)
    sums_ref[2:3, :] = jnp.sum(d_norm * std, axis=0, keepdims=True)
    sums_ref[3:4, :] = jnp.sum(d_norm, axis=0, keepdims=True)
    d_hidden = dy[...].astype(F32) + norm_back(d_norm, std, inv, gains[2:3, :])
    dh_ref[...] = d_hidden
    low_ref[...] = d_hidden.astype(BF16)
    a, b = low_ref[:, at(core * half, half, 128)], low_ref[:, at((1 - core) * half, half, 128)]
    for p in range(4):
        rows_p = at((rank ^ p) * quarter, quarter, 16)
        parts[p][...] = (dot(a, near[rows_p, :], NT) + dot(b, far[rows_p, :], NT)).astype(BF16)


def out_grad_kernel(ix, mixed, low, near_ref, far_ref):
    core, half = ix[1], near_ref.shape[1]
    left = mixed[...].astype(F32).T.astype(BF16)
    near_ref[...] = dot(left, low[:, at(core * half, half, 128)], NN)
    far_ref[...] = dot(left, low[:, at((1 - core) * half, half, 128)], NN).astype(BF16)


def project_back_kernel(run, ix, *refs):
    taken, (dq_a, dq_b, dkv, w, sums2, keep_ref, give_ref, cols_ref, sums) = refs[:4], refs[4:]
    step = pl.program_id(0)
    quarter, rows = dq_a.shape[1], dkv.shape[0]

    @pl.when(step == 0)
    def _():
        sums[...] = jnp.zeros_like(sums)
        sums[0:8, :] = sums2[...]

    for i, p in enumerate((1, 3, 0, 2)):

        @pl.when(step == i)
        def _():
            x = taken[p]
            std, _ = centre(jnp.concatenate([x[0:run, :], x[run + 8 : 2 * run + 8, :]], 0).astype(F32))
            dq = (dq_a, dq_b)[p >> 1][(p & 1) * rows : ((p & 1) + 1) * rows, :]
            part = dot(dq, w[:, 0:quarter], NT) + dot(dkv[...], w[:, quarter:], NT)
            sums[0:1, :] += jnp.sum(part * std, axis=0, keepdims=True)
            sums[1:2, :] += jnp.sum(part, axis=0, keepdims=True)
            if p & 1:
                give_ref[(p >> 1) * rows : ((p >> 1) + 1) * rows, :] = part.astype(BF16)
            else:
                keep_ref[(p >> 1) * rows : ((p >> 1) + 1) * rows, :] = part

    @pl.when(step == 3)
    def _():
        cols_ref[...] = sums[...].T.astype(BF16)


def tokens_back_kernel(run, ix, keep, got, across, x, d_hidden, gains, one_ref, two_ref):
    rows = d_hidden.shape[0]
    d_norm = keep[0:rows, :] + got[0:rows, :].astype(F32) + across[...].astype(F32)
    std, inv = centre(jnp.concatenate([x[0:run, :], x[run + 8 : 2 * run + 8, :]], 0).astype(F32))
    d = (d_hidden[...] + norm_back(d_norm, std, inv, gains[0:1, :])).astype(BF16)
    one_ref[...] = d[0:run]
    two_ref[...] = d[run:]


def grads_kernel(blocks, n_left, widths, n_right, extra, ix, *refs):
    lefts, refs = refs[:n_left], refs[n_left:]
    rights, refs = [refs[i * n_right : (i + 1) * n_right] for i in range(len(widths))], refs[len(widths) * n_right :]
    out_ref, left_t, *right_refs = refs[extra:]
    step = pl.program_id(0)
    cols = sum(widths)

    @pl.when(step == 0)
    def _():
        at_col = 0
        for piece in lefts:
            t = piece[...].T
            stop = at_col + t.shape[1]
            for dst, src, size in blocks:
                left_t[dst : dst + size, at_col:stop] = t[src : src + size, :]
            at_col = stop
        for pieces, ref in zip(rights, right_refs):
            row = 0
            for piece in pieces:
                ref[row : row + piece.shape[0], :] = piece[...]
                row += piece.shape[0]

    rows = out_ref.shape[0]
    mine = left_t[at(step * rows, rows, 16), :]
    start = 0
    for ref, w in zip(right_refs, widths):
        out_ref[:, start : start + w] = dot(mine, ref[...], NN).astype(BF16)
        start += w
    if extra:
        near, far, columns = refs[:3]
        half = near.shape[1]
        for i in range(left_t.shape[0] // rows):

            @pl.when(step == i)
            def _():
                for dst, src, size in blocks:
                    if i * rows <= dst < (i + 1) * rows:
                        span = slice(dst - i * rows, dst - i * rows + size)
                        both = near[src : src + size, :] + far[src : src + size, :].astype(F32)
                        out_ref[span, cols : cols + half] = both.astype(BF16)
                        out_ref[span, cols + half :] = columns[src : src + size, :]


def grad_ff_kernel(blocks, ix, n3, n2, n1, n0, u3, u2, u10, a3, a2, a10, d3, d2, d1, d0, out_ref, nt, at_t, up, dy):
    step = pl.program_id(0)
    depth = n3.shape[0]

    @pl.when(step == 0)
    def _():
        for i, (n, d) in enumerate(((n3, d3), (n2, d2), (n1, d1), (n0, d0))):
            span = slice(i * depth, (i + 1) * depth)
            t = n[...].T
            for dst, src, size in blocks:
                nt[dst : dst + size, span] = t[src : src + size, :]
            dy[span, :] = d[...]
        for first, a, u in ((0, a3, u3), (1, a2, u2), (2, a10, u10)):
            span = slice(first * depth, first * depth + a.shape[0])
            at_t[:, span] = a[...].T
            up[span, :] = u[...]

    rows, units = out_ref.shape[0], up.shape[1]
    mine = at(step * rows, rows, 16)
    out_ref[:, :units] = dot(nt[mine, :], up[...], NN).astype(BF16)
    out_ref[:, units:] = dot(at_t[mine, :], dy[...], NN).astype(BF16)


def home_kernel(ix, summed, *parts):
    core, y = ix[1], ix[3]
    rows, cols = parts[0].shape
    for p in range(4):
        block = (core ^ (p & 1)) * 2 + (y ^ (p >> 1))
        parts[p][...] = summed[at(block * rows, rows, 8), 0:cols]


def settle_kernel(ix, p0, p1, p2, p3, qkv_ref, out_ref, vec_ref, tile):
    rank, core = ix[0], ix[1]
    parts = (p0, p1, p2, p3)
    rows, width = out_ref.shape
    quarter, half = width // 4, width // 2
    for p in range(4):
        a = rank ^ p
        for t in range(3):
            qkv_ref[:, at(t * width + a * quarter, quarter, 128)] = parts[p][:, t * quarter : (t + 1) * quarter].astype(F32)
    c1, c2 = 3 * quarter, 3 * quarter + half
    for p in range(2):
        out_ref[:, at((core ^ p) * half, half, 128)] = parts[p][:, c1:c2].astype(F32) + parts[p + 2][:, c1:c2].astype(F32)
    tile[...] = jnp.zeros_like(tile)
    tile[0:rows, :] = sum(v[:, c2:].astype(F32) for v in parts)
    vec_ref[...] = tile[...].T[0:8, :]


def settle_ff_kernel(spots, ix, p0, p1, p2, p3, up_ref):
    core, y = ix[1], ix[3]
    hid, zs = 128, len(spots) // 2
    for p, part in enumerate((p0, p1, p2, p3)):
        c2, y2 = core ^ (p & 1), y ^ (p >> 1)
        for b, (nx, nz) in enumerate(spots):
            dst = ((nx * 2 + c2) * zs + nz) * 2 + y2
            up_ref[:, at(dst * hid, hid, 128)] = part[:, b * hid : (b + 1) * hid].astype(F32)


class Places:
    def __init__(self, mesh):
        self.n_dp, self.n_fsdp = mesh.shape["dp"], mesh.shape["fsdp"]
        self.xs, self.zs = self.n_dp // 2, self.n_fsdp // 2
        self.nodes = self.xs * self.zs
        self.all = [
            (x, c, z, y) for x in range(self.xs) for c in range(2) for z in range(self.zs) for y in range(2)
        ]

    def lin(self, x, c, z, y):
        return (x * 2 + c) * self.n_fsdp + z * 2 + y

    def perm(self, move):
        return [(self.lin(*d), self.lin(*move(*d))) for d in self.all]

    def spot(self, x, z):
        return x * self.zs + (z if x % 2 == 0 else self.zs - 1 - z)

    def node(self, spot):
        x, z = spot // self.zs, spot % self.zs
        return (x, z if x % 2 == 0 else self.zs - 1 - z)

    def rings(self):
        return [
            [self.lin(x, c, z, y) for x, z in map(self.node, range(self.nodes))] for c in range(2) for y in range(2)
        ]


def permute(array, pairs):
    return lax.ppermute(array, AXES, pairs)


def after(value, *done):
    return lax.optimization_barrier((value,) + done)[0]


def body(pc, tokens, scene_ids, w_qkv, w_out, w_up, w_down, gain_one, bias_one, gain_two, bias_two, cotangent):
    micro, run, width = tokens.shape
    rows = w_qkv.shape[0]
    ff = w_up.shape[1]
    units = ff // 4
    hid = w_down.shape[0]
    quarter, half = width // 4, width // 2
    own = micro * run
    dp, fsdp = lax.axis_index("dp"), lax.axis_index("fsdp")
    x, core, z, y = dp // 2, dp % 2, fsdp // 2, fsdp % 2
    rank = y * 2 + core
    groups = micro * 2
    quads = pc.zs // groups
    rings = pc.rings()
    spots = [pc.node(i) for i in range(pc.nodes)]
    blocks = row_blocks(spots, 2 * rows)
    aligned = hid % 128 == 0

    p_core = pc.perm(lambda x, c, z, y: (x, 1 - c, z, y))
    p_y = pc.perm(lambda x, c, z, y: (x, c, z, 1 - y))
    p_diag = pc.perm(lambda x, c, z, y: (x, 1 - c, z, 1 - y))

    def place_perm(flip):
        def move(x, c, z, y):
            m = (z % 2) ^ flip
            return (x, (z // 2) % 2, (m * 2 + c) * quads + z // 4, y)

        return pc.perm(move)

    p_place = [place_perm(0), place_perm(1)]
    p_back = [[(b, a) for a, b in pairs] for pairs in p_place]

    def group_perm(by):
        return pc.perm(lambda x, c, z, y: (x, c, z // quads * quads + (z + by) % quads, y))

    ix = jnp.stack([rank, core, z % 2, y]).astype(jnp.int32)

    def quad_swap(parts):
        return [parts[0], permute(parts[1], p_core), permute(parts[2], p_y), permute(parts[3], p_diag)]

    def by_rank(parts):
        odd, top = rank % 2 == 1, rank // 2 == 1
        parts = [jnp.where(odd, parts[i ^ 1], parts[i]) for i in range(4)]
        return [jnp.where(top, parts[i ^ 2], parts[i]) for i in range(4)]

    def by_rows(parts):
        r = by_rank(parts)
        return jnp.concatenate([r[0], r[2], r[1], r[3]], 0)

    def ring_gather(shard):
        return lax.all_gather(shard, AXES, axis=0, tiled=True, axis_index_groups=rings)

    def ring_sum(terms):
        return lax.psum_scatter(terms, AXES, scatter_dimension=0, tiled=True, axis_index_groups=rings)

    c_out, c_small, wide = 3 * quarter, 3 * quarter + half, 3 * quarter + half + 128
    wu = w_up
    if not aligned:
        wu = w_up.reshape(rows, pc.xs, 2, pc.zs, 2, hid)
        wu = [
            lax.dynamic_slice(
                wu, (0, 0, core ^ (p & 1), 0, y ^ (p >> 1), 0), (rows, pc.xs, 1, pc.zs, 1, hid)
            ).reshape(rows, pc.xs, pc.zs, hid)
            for p in range(4)
        ]
        wu = jnp.concatenate([w[:, nx, nz] for w in wu for nx, nz in spots], 1)
    *packed, x_one, x_two, dy_one, dy_two = call(
        functools.partial(pack_kernel, aligned, spots),
        "pack",
        (
            ix,
            w_qkv,
            w_out,
            jnp.stack([gain_one, bias_one, gain_two, bias_two]),
            tokens,
            scene_ids.reshape(micro, run),
            cotangent,
            wu,
        ),
        [shape_of((rows, wide))] * 4 + [shape_of((rows, units))] * 4 + [shape_of((run + 8, width))] * 2 + [shape_of((run, width))] * 2,
        scratch=[pltpu.VMEM((128, 128), F32)],
        room=58,
    )
    shard = by_rows(quad_swap(packed[:4]))
    x_own = jnp.concatenate([permute(x_one, p_place[0]), permute(x_two, p_place[1])], 0)
    first = ring_gather(after(shard, x_own))
    x_across = permute(x_own, p_y)
    taken = [x_own, permute(x_own, p_core), x_across, permute(x_across, p_core)]
    up_shard = by_rows(quad_swap(after(packed[4:], x_across)))
    second = ring_gather(after(jnp.concatenate([up_shard, w_down], 1), taken))
    dy_one, dy_two = after((dy_one, dy_two), first)
    dy_own = jnp.concatenate([permute(dy_one, p_place[0]), permute(dy_two, p_place[1])], 0)

    block = (own, width)
    n_one, projected, full_qkv, near_out, gains, qrow = call(
        functools.partial(project_kernel, blocks, run),
        "project",
        (ix, *taken, first),
        [
            shape_of((4 * own, width)),
            shape_of((4 * own, 3 * quarter)),
            shape_of((width, 3 * quarter)),
            shape_of((width, half)),
            shape_of((8, width), F32),
            shape_of((1, 4 * own), F32),
        ],
        scratch=[pltpu.VMEM((width, 128), F32)],
        grid=(4,),
        flops=2 * 4 * own * width * 3 * quarter,
        out_specs={
            0: pl.BlockSpec(block, lambda i: (i, 0)),
            1: pl.BlockSpec((own, 3 * quarter), lambda i: (i, 0)),
        },
    )
    far_out = permute(near_out, p_core)
    if quads == 1:
        q, k, v, krow = (projected, 0), (projected, 1), (projected, 2), qrow
    else:
        kv = projected[:, quarter:]
        kv_all = jnp.concatenate([kv] + [permute(kv, group_perm(s)) for s in range(1, quads)], 0)
        krow = jnp.concatenate([qrow] + [permute(qrow, group_perm(s)) for s in range(1, quads)], 1)
        q, k, v = (projected, 0), (kv_all, 0), (kv_all, 1)
    *m_far, lse_far = attend(ix, q, k, v, quarter, qrow, krow, 2)
    dy_across = permute(after(dy_own, m_far), p_y)
    *m_near, lse_near = attend(ix, q, k, v, quarter, after(qrow, m_far, dy_own), krow, 0)
    mixed = quad_swap([*m_near, *m_far])
    mixed_own, hidden, n_two = call(
        functools.partial(mix_out_kernel, run),
        "mix_out",
        (ix, *mixed, near_out, far_out, taken[0], gains),
        [shape_of(block), shape_of(block, F32), shape_of(block)],
        flops=2 * own * width * width,
    )
    def far_sum(keep, got):
        return (keep + got.astype(F32)).astype(BF16)

    n_across = permute(after(n_two, dy_across), p_y)
    norms = [n_two, permute(n_two, p_core), n_across, permute(n_across, p_core)]
    dys = [dy_own, permute(dy_own, p_core), dy_across, permute(dy_across, p_core)]

    def hidden_units(parts, weights, kinds, order):
        outs = [shape_of((len(parts) * own, units))] * 2 + [shape_of(block, kind) for kind in kinds * 2]
        return call(
            functools.partial(hidden_units_kernel, parts, order),
            "hidden_units",
            (ix, *[norms[p] for p in parts], *[dys[p] for p in parts], *weights),
            outs + ([shape_of((width, units)), shape_of((units, width))] if order else []),
            flops=8 * len(parts) * own * width * units,
            transcendentals=2 * len(parts) * own * units,
        )

    act3, up3, give3, r_give3, full_up, full_down = hidden_units((3,), (second,), (BF16,), blocks)
    got3 = permute(give3, p_core)
    act2, up2, keep2, r_keep2 = hidden_units((2,), (after(full_up, give3), full_down), (F32,), None)
    far = far_sum(keep2, got3)
    across = permute(far, p_y)
    act10, up10, give1, keep0, r_give1, r_keep0 = hidden_units((1, 0), (after(full_up, far), full_down), (BF16, F32), None)
    got = permute(give1, p_core)
    in_order = [(i, i, n) for i, _, n in blocks]

    def grads(name, lefts, rights, order, extra=()):
        widths = tuple(r[0].shape[1] for r in rights)
        depth, cols = sum(a.shape[0] for a in lefts), sum(widths)
        height = lefts[0].shape[1]
        total = cols + sum(e.shape[1] for e in extra[1:])
        return call(
            functools.partial(grads_kernel, order, len(lefts), widths, len(rights[0]), len(extra)),
            name,
            (ix, *lefts, *[piece for r in rights for piece in r], *extra),
            [shape_of((height, total))],
            scratch=[pltpu.VMEM((height, depth), BF16)] + [pltpu.VMEM((depth, w), BF16) for w in widths],
            grid=(4,),
            flops=2 * depth * height * cols,
            out_specs={0: pl.BlockSpec((height // 4, total), lambda i: (i, 0))},
        )[0]

    order = (3, 2, 1, 0)
    (ff_terms,) = call(
        functools.partial(grad_ff_kernel, blocks),
        "grad_ff",
        (ix, *[norms[p] for p in order], up3, up2, up10, act3, act2, act10, *[dys[p] for p in order]),
        [shape_of((width, units + width))],
        scratch=[pltpu.VMEM((width, 4 * own), BF16), pltpu.VMEM((units, 4 * own), BF16)]
        + [pltpu.VMEM((4 * own, units), BF16), pltpu.VMEM((4 * own, width), BF16)],
        grid=(4,),
        flops=2 * 4 * own * width * 2 * units,
        out_specs={0: pl.BlockSpec((width // 4, units + width), lambda i: (i, 0))},
    )
    ff_sum = ring_sum(ff_terms)
    up_sum, down_sum = ff_sum[:, :units], ff_sum[:, units:]
    *d_parts, d_hidden, d_low, sums_two = call(
        hidden_back_kernel,
        "hidden_back",
        (ix, keep0, got, across, hidden, dys[0], after(gains, ff_terms), near_out, far_out),
        [shape_of((own, quarter))] * 4 + [shape_of(block, F32), shape_of(block), shape_of((8, width), F32)],
        flops=2 * own * width * width,
    )
    d_mixed = quad_swap(d_parts)
    near_parts, far_parts = d_mixed[:2], d_mixed[2:]
    r_far = far_sum(r_keep2, permute(after(r_give3, d_parts[0]), p_core))
    r_across = permute(r_far, p_y)
    r_got = permute(after(r_give1, d_parts[0]), p_core)
    dq_near, kept = attend_back(ix, q, k, v, quarter, qrow, krow, lse_near, near_parts, 0, ())
    dq_far, dkv = attend_back(ix, q, k, v, quarter, qrow, krow, lse_far, far_parts, 2, (after(kept, r_far),))

    def placed(one, two):
        return [permute(one, p_back[0]), permute(two, p_back[1])]

    r_own = (after(hidden, dq_far) + r_keep0 + r_got.astype(F32) + r_across.astype(F32)).astype(BF16)
    back_out = placed(r_own[:run], r_own[run:])
    n_rows = dkv.shape[0] // quads
    if quads > 1:
        total = dkv[:n_rows].astype(F32)
        for s in range(1, quads):
            total = total + permute(dkv[s * n_rows : (s + 1) * n_rows], group_perm(-s)).astype(F32)
        dkv = total.astype(BF16)

    keep_one, give_one, columns = call(
        functools.partial(project_back_kernel, run),
        "project_back",
        (ix, *taken, dq_near, dq_far, dkv, full_qkv, after(sums_two, r_own)),
        [shape_of((2 * own, width), F32), shape_of((2 * own, width)), shape_of((width, 128))],
        scratch=[pltpu.VMEM((128, width), F32)],
        grid=(4,),
        flops=2 * 4 * own * width * 3 * quarter,
        in_specs={
            6: pl.BlockSpec((own, 2 * quarter), lambda i: (jnp.where(i == 0, 1, jnp.where(i == 1, 3, (i - 2) * 2)), 0)),
        },
    )
    got_one = permute(give_one, p_core)
    grad_near, grad_far = call(
        out_grad_kernel,
        "out_grad",
        (ix, after(mixed_own, give_one), d_low),
        [shape_of((width, half), F32), shape_of((width, half))],
        flops=2 * own * width * width,
    )
    far_one = far_sum(keep_one[own:], after(got_one, grad_near)[own:])
    across_one = permute(far_one, p_y)
    at_terms = grads(
        "grad_at",
        [after(n_one, far_one)],
        [[jnp.concatenate([dq_near, dq_far], 0)], [dkv]],
        blocks,
        (grad_near, permute(grad_far, p_core), columns),
    )
    one_sum = ring_sum(after(at_terms, ff_sum, back_out))

    def home(name, summed):
        return quad_swap(call(home_kernel, name, (ix, summed), [shape_of((rows, summed.shape[1]))] * 4))

    def in_batches(one, two):
        return jnp.stack([jnp.where(z % 2 == 0, one, two), jnp.where(z % 2 == 0, two, one)], 0)

    d_one, d_two = call(
        functools.partial(tokens_back_kernel, run),
        "tokens_back",
        (ix, keep_one, got_one, across_one, taken[0], d_hidden, after(gains, ff_sum, back_out)),
        [shape_of((run, width))] * 2,
    )
    ff_home = home("home_up", after(up_sum, d_one))
    own_down = down_sum.astype(F32)
    if aligned:
        (own_up,) = call(
            functools.partial(settle_ff_kernel, spots), "settle_ff", (ix, *ff_home), [shape_of((rows, 4 * units), F32)])
    else:
        ups = [b.reshape(rows, pc.nodes, hid) for b in ff_home]
        at_spot = [[spots.index((nx, nz)) for nz in range(pc.zs)] for nx in range(pc.xs)]
        ups = by_rank([jnp.stack([jnp.stack([b[:, i] for i in row], 1) for row in at_spot], 1) for b in ups])
        own_up = (
            jnp.stack([jnp.stack([ups[0], ups[2]], 3), jnp.stack([ups[1], ups[3]], 3)], 2)
            .reshape(rows, 4 * units)
            .astype(F32)
        )
    back_grad = placed(*after((d_one, d_two), own_up))
    at_home = home("home_at", after(one_sum, back_out))
    output = in_batches(*after(back_out, at_home[0]))
    own_qkv, own_out, vectors = call(
        settle_kernel,
        "settle",
        (ix, *at_home),
        [shape_of((rows, 3 * width), F32), shape_of((rows, width), F32), shape_of((8, 128), F32)],
        scratch=[pltpu.VMEM((128, 128), F32)],
    )
    input_grad = in_batches(*after(back_grad, own_qkv)).astype(F32)
    return (output, input_grad, own_qkv, own_out, own_up, own_down) + tuple(vectors[i, :rows] for i in range(4))


def solution(mesh):
    vector, matrix, batch = P(AXES), P(AXES, None), P(None, AXES, None)
    return jax.shard_map(
        functools.partial(body, Places(mesh)),
        mesh=mesh,
        in_specs=(batch, P(None, "dp", "fsdp")) + (matrix,) * 4 + (vector,) * 4 + (batch,),
        out_specs=(batch, batch) + (matrix,) * 4 + (vector,) * 4,
        check_vma=False,
    )
```

```python
import functools
import math

import jax
import jax.numpy as jnp
from jax import lax
from jax.experimental import pallas as pl
from jax.experimental.pallas import tpu as pltpu
from jax.sharding import PartitionSpec as P

AXES = ("dp", "fsdp")
HEAD_DIM = 64
EPS = 1e-05
LOWEST = -1000000000.0
F32 = jnp.float32
BF16 = jnp.bfloat16
NT = (((1,), (1,)), ((), ()))
TN = (((0,), (0,)), ((), ()))
NN = (((1,), (0,)), ((), ()))
ROOM = 20
IN_HBM = ("grad_ff", "grad_at")
HINTS = {"home_at": 1000, "settle": 8, "mix_out": 0, "grad_ff": 3, "hidden_units": 8, "hidden_back": 300, "attend_back": 4, "grad_down": 0, "home_up": 0, "settle_ff": 0, "out_grad": 0, "project_back": 0, "grad_at": 0, "tokens_back": 0, "down": 8}


def dot(left, right, dims):
    return lax.dot_general(left, right, dims, preferred_element_type=F32)


def at(start, size, step):
    return pl.ds(pl.multiple_of(start, step), size)


def call(kernel, name, args, outs, scratch=(), grid=None, flops=0, transcendentals=0, in_specs=None, out_specs=None, room=ROOM):
    whole = pl.BlockSpec(memory_space=pltpu.VMEM) if grid is None else None

    def spec(shape):
        return whole or pl.BlockSpec(shape, lambda i, n=len(shape): (0,) * n)

    specs = [pl.BlockSpec(memory_space=pltpu.SMEM)]
    specs += [(in_specs or {}).get(n) or spec(a.shape) for n, a in enumerate(args[1:])]
    size = sum(math.prod(a.shape) * a.dtype.itemsize for a in list(args) + list(outs))
    return pl.pallas_call(
        kernel,
        out_shape=tuple(pltpu.HBM(o.shape, o.dtype) for o in outs) if name in IN_HBM else tuple(outs),
        in_specs=specs,
        out_specs=tuple((out_specs or {}).get(n) or spec(o.shape) for n, o in enumerate(outs)),
        scratch_shapes=list(scratch),
        compiler_params=pltpu.CompilerParams(vmem_limit_bytes=min(room, 58) * 1024 * 1024),
        cost_estimate=pl.CostEstimate(
            flops=HINTS.get(name, 8) * flops, bytes_accessed=HINTS.get(name, 8) * size, transcendentals=transcendentals
        ),
        name=name,
        **({} if grid is None else {"grid": grid}),
    )(*args)


def shape_of(shape, dtype=BF16):
    return jax.ShapeDtypeStruct(shape, dtype)


def centre(v):
    c = v - jnp.mean(v, axis=-1, keepdims=True)
    inv = lax.rsqrt(jnp.mean(c * c, axis=-1, keepdims=True) + EPS)
    return c * inv, inv


def norm_back(d_norm, std, inv, gain):
    d_std = d_norm * gain
    return inv * (
        d_std - jnp.mean(d_std, axis=-1, keepdims=True) - std * jnp.mean(d_std * std, axis=-1, keepdims=True)
    )


def pack_kernel(aligned, spots, ix, qkv, out, gains, tokens, scenes, dy, up, *refs):
    parts, ups, (one, two, dy_one, dy_two, tile) = refs[:4], refs[4:8], refs[8:]
    rank, core, odd, y = ix[0], ix[1], ix[2], ix[3]
    rows, width = qkv.shape[0], out.shape[1]
    quarter, half = width // 4, width // 2
    tile[...] = jnp.zeros_like(tile)
    tile[0:4, 0:rows] = gains[...].astype(F32)
    small = tile[...].T[:rows].astype(BF16)
    c1, c2 = 3 * quarter, 3 * quarter + half
    hid, units = 128, up.shape[1] // 4
    zs = len(spots) // 2
    for p in range(4):
        a = rank ^ p
        for t in range(3):
            parts[p][:, t * quarter : (t + 1) * quarter] = qkv[:, at(t * width + a * quarter, quarter, 128)]
        parts[p][:, c1:c2] = out[:, at((core ^ (p & 1)) * half, half, 128)]
        parts[p][:, c2 : c2 + 128] = small
        if aligned:
            for b, (nx, nz) in enumerate(spots):
                src = ((nx * 2 + (core ^ (p & 1))) * zs + nz) * 2 + (y ^ (p >> 1))
                ups[p][:, b * hid : (b + 1) * hid] = up[:, at(src * hid, hid, 128)]
        else:
            ups[p][...] = up[:, p * units : (p + 1) * units]
    run = tokens.shape[1]
    for ref, low, m in ((one, dy_one, odd), (two, dy_two, 1 - odd)):
        ref[0:run, :] = tokens[m]
        ref[run:, :] = jnp.zeros((ref.shape[0] - run, width), BF16)
        ref[run : run + 1, 0:run] = scenes[pl.ds(m, 1), :].astype(F32).astype(BF16)
        low[...] = dy[m]


def row_blocks(spots, size):
    zs = len(spots) // 2
    return [
        ((2 * i + c) * size, ((nx * 2 + c) * zs + nz) * size, size) for i, (nx, nz) in enumerate(spots) for c in (0, 1)
    ]


def project_kernel(blocks, run, ix, *refs):
    taken, first = refs[:4], refs[4]
    n_ref, p_ref, w_ref, near_ref, gains_ref, scene_ref, g_all = refs[5:]
    step = pl.program_id(0)
    c_out, c_small = w_ref.shape[1], w_ref.shape[1] + near_ref.shape[1]

    @pl.when(step == 0)
    def _():
        for src, dst, size in blocks:
            v = first[src : src + size, :]
            w_ref[dst : dst + size, :] = v[:, :c_out]
            near_ref[dst : dst + size, :] = v[:, c_out:c_small]
            g_all[dst : dst + size, :] = v[:, c_small:].astype(F32)
        gains_ref[...] = g_all[...].T[0:8, :]
        for p in range(4):
            for s in range(2):
                row = taken[p][s * (run + 8) + run : s * (run + 8) + run + 1, 0:run]
                scene_ref[0:1, (2 * p + s) * run : (2 * p + s + 1) * run] = row.astype(F32)

    for p in range(4):

        @pl.when(step == p)
        def _():
            x = taken[p]
            v = jnp.concatenate([x[0:run, :], x[run + 8 : 2 * run + 8, :]], 0).astype(F32)
            std, _ = centre(v)
            n = (std * gains_ref[0:1, :] + gains_ref[1:2, :]).astype(BF16)
            n_ref[...] = n
            p_ref[...] = dot(n, w_ref[...], NN).astype(BF16)


def head_lanes(rows, width, head):
    lane = lax.broadcasted_iota(jnp.int32, (rows, width), 1)
    return (lane >= head * HEAD_DIM) & (lane < (head + 1) * HEAD_DIM)


def column(row):
    return jnp.broadcast_to(row, (128, row.shape[1])).T


def same_scene(ksc, qrow):
    return jnp.concatenate([ksc == qrow[:, i : i + 128] for i in range(0, qrow.shape[1], 128)], 1)


def attend_kernel(heads, ix, krow_ref, qrow_ref, q_ref, k_ref, v_ref, *refs):
    outs_ref, (lse_ref, vt_ref, ksc_ref) = refs[:2], refs[2:]
    step = pl.program_id(0)

    @pl.when(step == 0)
    def _():
        vt_ref[...] = v_ref[...].astype(F32).T.astype(BF16)
        ksc_ref[...] = column(krow_ref[...])

    rows, width = q_ref.shape
    same = same_scene(ksc_ref[...], qrow_ref[...])
    q = q_ref[...].astype(F32) * (1.0 / math.sqrt(HEAD_DIM))
    outs = []
    for h in range(heads):
        qh = jnp.where(head_lanes(rows, width, h), q, 0.0).astype(BF16)
        s = jnp.where(same, dot(k_ref[...], qh, NT), LOWEST)
        peak = jnp.max(s, axis=0, keepdims=True)
        e = jnp.exp(s - peak)
        total = jnp.sum(e, axis=0, keepdims=True)
        lse_ref[h : h + 1, :] = peak + jnp.log(total)
        p = (e * (1.0 / total)).astype(BF16)
        outs.append(dot(vt_ref[h * HEAD_DIM : (h + 1) * HEAD_DIM, :], p, NN))
    mixed = jnp.concatenate(outs, axis=0).T.astype(BF16)
    for i in range(2):

        @pl.when(step == i)
        def _():
            outs_ref[i][...] = mixed


def attend(ix, q, k, v, quarter, qrow, krow, first):
    rows, keys = q[0].shape[0], k[0].shape[0]
    heads, block = quarter // HEAD_DIM, rows // 4
    return call(
        functools.partial(attend_kernel, heads),
        "attend",
        (ix, krow, qrow, q[0], k[0], v[0]),
        [shape_of((block, quarter))] * 2 + [shape_of((heads, 2 * block), F32)],
        scratch=[pltpu.VMEM((quarter, keys), BF16), pltpu.VMEM((keys, 128), F32)],
        grid=(2,),
        room=ROOM * keys // rows,
        flops=2 * rows * keys * quarter,
        transcendentals=rows * keys * heads // 2,
        in_specs={
            1: pl.BlockSpec((1, block), lambda i: (0, i + first)),
            2: pl.BlockSpec((block, quarter), lambda i, c=q[1]: (i + first, c)),
            3: pl.BlockSpec((keys, quarter), lambda i, c=k[1]: (0, c)),
            4: pl.BlockSpec((keys, quarter), lambda i, c=v[1]: (0, c)),
        },
        out_specs={2: pl.BlockSpec((heads, block), lambda i: (0, i))},
    )


def attend_back_kernel(heads, more, ix, krow_ref, qrow_ref, lse_ref, q_ref, k_ref, v_ref, *refs):
    do_refs, kept, refs = refs[:2], refs[2 : 2 + more], refs[2 + more :]
    dq_ref, dkv_ref, kt_ref, ksc_ref, dka_ref, dva_ref, do_ref = refs
    width = q_ref.shape[1]
    step = pl.program_id(0)

    @pl.when(step == 0)
    def _():
        kt_ref[...] = k_ref[...].astype(F32).T.astype(BF16)
        ksc_ref[...] = column(krow_ref[...])
        if more:
            dka_ref[...] = kept[0][:, :width]
            dva_ref[...] = kept[0][:, width:]
        else:
            dka_ref[...] = jnp.zeros_like(dka_ref)
            dva_ref[...] = jnp.zeros_like(dva_ref)

    for i in range(2):

        @pl.when(step == i)
        def _():
            do_ref[...] = do_refs[i][...].astype(F32)

    rows, width = q_ref.shape
    scale = 1.0 / math.sqrt(HEAD_DIM)
    same = same_scene(ksc_ref[...], qrow_ref[...])
    q = q_ref[...].astype(F32) * scale
    do = do_ref[...]
    outs = []
    for h in range(heads):
        mine = head_lanes(rows, width, h)
        qh = jnp.where(mine, q, 0.0).astype(BF16)
        doh = jnp.where(mine, do, 0.0).astype(BF16)
        s = jnp.where(same, dot(k_ref[...], qh, NT), LOWEST)
        p = jnp.exp(s - lse_ref[h : h + 1, :])
        dp = dot(v_ref[...], doh, NT)
        inner = jnp.sum(p * dp, axis=0, keepdims=True)
        ds = (p * (dp - inner)).astype(BF16)
        dva_ref[...] += dot(p.astype(BF16), doh, NN)
        dka_ref[...] += dot(ds, qh, NN)
        outs.append(dot(kt_ref[h * HEAD_DIM : (h + 1) * HEAD_DIM, :], ds, NN))
    dq_ref[...] = (jnp.concatenate(outs, axis=0).T * scale).astype(BF16)

    @pl.when(step == pl.num_programs(0) - 1)
    def _():
        dkv_ref[:, :width] = dka_ref[...].astype(dkv_ref.dtype)
        dkv_ref[:, width:] = dva_ref[...].astype(dkv_ref.dtype)


def attend_back(ix, q, k, v, quarter, qrow, krow, lse, do, first, kept):
    rows, keys = q[0].shape[0], k[0].shape[0]
    heads, block = quarter // HEAD_DIM, rows // 4
    return call(
        functools.partial(attend_back_kernel, heads, len(kept)),
        "attend_back",
        (ix, krow, qrow, lse, q[0], k[0], v[0], *do, *kept),
        [shape_of((2 * block, quarter)), shape_of((keys, 2 * quarter), BF16 if kept else F32)],
        scratch=[
            pltpu.VMEM((quarter, keys), BF16),
            pltpu.VMEM((keys, 128), F32),
            pltpu.VMEM((keys, quarter), F32),
            pltpu.VMEM((keys, quarter), F32),
            pltpu.VMEM((block, quarter), F32),
        ],
        grid=(2,),
        room=ROOM * keys // rows,
        flops=5 * rows * keys * quarter,
        transcendentals=rows * keys * heads // 2,
        in_specs={
            1: pl.BlockSpec((1, block), lambda i: (0, i + first)),
            2: pl.BlockSpec((heads, block), lambda i: (0, i)),
            3: pl.BlockSpec((block, quarter), lambda i, c=q[1]: (i + first, c)),
            4: pl.BlockSpec((keys, quarter), lambda i, c=k[1]: (0, c)),
            5: pl.BlockSpec((keys, quarter), lambda i, c=v[1]: (0, c)),
        },
        out_specs={0: pl.BlockSpec((block, quarter), lambda i: (i, 0))},
    )


def mix_out_kernel(run, ix, m0, m1, m2, m3, near, far, x, gains, mixed_ref, hidden_ref, n_ref):
    rank, core = ix[0], ix[1]
    quarter, half = m0.shape[1], near.shape[1]
    for p, m in enumerate((m0, m1, m2, m3)):
        mixed_ref[:, at((rank ^ p) * quarter, quarter, 128)] = m[...]
    mixed = mixed_ref[...]
    hidden_ref[0:run, :] = x[0:run, :].astype(F32)
    hidden_ref[run:, :] = x[run + 8 : 2 * run + 8, :].astype(F32)
    hidden_ref[:, at(core * half, half, 128)] += dot(mixed, near[...], NN)
    hidden_ref[:, at((1 - core) * half, half, 128)] += dot(mixed, far[...], NN)
    std, _ = centre(hidden_ref[...])
    n_ref[...] = (std * gains[2:3, :] + gains[3:4, :]).astype(BF16)


def hidden_units_kernel(parts, blocks, ix, *refs):
    n, rows = len(parts), refs[0].shape[0]
    norms, dys, refs = refs[:n], refs[n : 2 * n], refs[2 * n :]
    if blocks:
        second, act_ref, dup_ref, *term_refs, up_ref, down_ref = refs
        units = up_ref.shape[1]
        for src, dst, size in blocks:
            up_ref[dst : dst + size, :] = second[src : src + size, :units]
        down_ref[...] = second[:, units:]
    else:
        up_ref, down_ref, act_ref, dup_ref, *term_refs = refs
    for i in range(n):
        span = slice(i * rows, (i + 1) * rows)
        u = dot(norms[i][...], up_ref[...], NN)
        cdf = 0.5 * (1.0 + lax.erf(u * math.sqrt(0.5)))
        act = (u * cdf).astype(BF16)
        act_ref[span, :] = act
        term_refs[n + i][...] = dot(act, down_ref[...], NN).astype(term_refs[n + i].dtype)
        slope = cdf + u * jnp.exp(-0.5 * u * u) * (1.0 / math.sqrt(2.0 * math.pi))
        dup = (dot(dys[i][...], down_ref[...], NT) * slope).astype(BF16)
        dup_ref[span, :] = dup
        term_refs[i][...] = dot(dup, up_ref[...], NT).astype(term_refs[i].dtype)


def hidden_back_kernel(ix, keep, got, across, hidden, dy, gains, near, far, *refs):
    parts, (dh_ref, low_ref, sums_ref) = refs[:4], refs[4:]
    rank, core = ix[0], ix[1]
    rows = hidden.shape[0]
    half, quarter = near.shape[1], parts[0].shape[1]
    d_norm = keep[...] + got[...].astype(F32) + across[...].astype(F32)
    std, inv = centre(hidden[...])
    sums_ref[...] = jnp.zeros_like(sums_ref)
    sums_ref[2:3, :] = jnp.sum(d_norm * std, axis=0, keepdims=True)
    sums_ref[3:4, :] = jnp.sum(d_norm, axis=0, keepdims=True)
    d_hidden = dy[...].astype(F32) + norm_back(d_norm, std, inv, gains[2:3, :])
    dh_ref[...] = d_hidden
    low_ref[...] = d_hidden.astype(BF16)
    a, b = low_ref[:, at(core * half, half, 128)], low_ref[:, at((1 - core) * half, half, 128)]
    for p in range(4):
        rows_p = at((rank ^ p) * quarter, quarter, 16)
        parts[p][...] = (dot(a, near[rows_p, :], NT) + dot(b, far[rows_p, :], NT)).astype(BF16)


def out_grad_kernel(ix, mixed, low, near_ref, far_ref):
    core, half = ix[1], near_ref.shape[1]
    left = mixed[...].astype(F32).T.astype(BF16)
    near_ref[...] = dot(left, low[:, at(core * half, half, 128)], NN)
    far_ref[...] = dot(left, low[:, at((1 - core) * half, half, 128)], NN).astype(BF16)


def project_back_kernel(run, ix, *refs):
    taken, (dq_a, dq_b, dkv, w, sums2, keep_ref, give_ref, cols_ref, sums) = refs[:4], refs[4:]
    step = pl.program_id(0)
    quarter, rows = dq_a.shape[1], dkv.shape[0]

    @pl.when(step == 0)
    def _():
        sums[...] = jnp.zeros_like(sums)
        sums[0:8, :] = sums2[...]

    for i, p in enumerate((1, 3, 0, 2)):

        @pl.when(step == i)
        def _():
            x = taken[p]
            std, _ = centre(jnp.concatenate([x[0:run, :], x[run + 8 : 2 * run + 8, :]], 0).astype(F32))
            dq = (dq_a, dq_b)[p >> 1][(p & 1) * rows : ((p & 1) + 1) * rows, :]
            part = dot(dq, w[:, 0:quarter], NT) + dot(dkv[...], w[:, quarter:], NT)
            sums[0:1, :] += jnp.sum(part * std, axis=0, keepdims=True)
            sums[1:2, :] += jnp.sum(part, axis=0, keepdims=True)
            if p & 1:
                give_ref[(p >> 1) * rows : ((p >> 1) + 1) * rows, :] = part.astype(BF16)
            else:
                keep_ref[(p >> 1) * rows : ((p >> 1) + 1) * rows, :] = part

    @pl.when(step == 3)
    def _():
        cols_ref[...] = sums[...].T.astype(BF16)


def tokens_back_kernel(run, ix, keep, got, across, x, d_hidden, gains, one_ref, two_ref):
    rows = d_hidden.shape[0]
    d_norm = keep[0:rows, :] + got[0:rows, :].astype(F32) + across[...].astype(F32)
    std, inv = centre(jnp.concatenate([x[0:run, :], x[run + 8 : 2 * run + 8, :]], 0).astype(F32))
    d = (d_hidden[...] + norm_back(d_norm, std, inv, gains[0:1, :])).astype(BF16)
    one_ref[...] = d[0:run]
    two_ref[...] = d[run:]


def grads_kernel(blocks, n_left, widths, n_right, extra, ix, *refs):
    lefts, refs = refs[:n_left], refs[n_left:]
    rights, refs = [refs[i * n_right : (i + 1) * n_right] for i in range(len(widths))], refs[len(widths) * n_right :]
    out_ref, left_t, *right_refs = refs[extra:]
    step = pl.program_id(0)
    cols = sum(widths)

    @pl.when(step == 0)
    def _():
        at_col = 0
        for piece in lefts:
            t = piece[...].T
            stop = at_col + t.shape[1]
            for dst, src, size in blocks:
                left_t[dst : dst + size, at_col:stop] = t[src : src + size, :]
            at_col = stop
        for pieces, ref in zip(rights, right_refs):
            row = 0
            for piece in pieces:
                ref[row : row + piece.shape[0], :] = piece[...]
                row += piece.shape[0]

    rows = out_ref.shape[0]
    mine = left_t[at(step * rows, rows, 16), :]
    start = 0
    for ref, w in zip(right_refs, widths):
        out_ref[:, start : start + w] = dot(mine, ref[...], NN).astype(BF16)
        start += w
    if extra:
        near, far, columns = refs[:3]
        half = near.shape[1]
        for i in range(left_t.shape[0] // rows):

            @pl.when(step == i)
            def _():
                for dst, src, size in blocks:
                    if i * rows <= dst < (i + 1) * rows:
                        span = slice(dst - i * rows, dst - i * rows + size)
                        both = near[src : src + size, :] + far[src : src + size, :].astype(F32)
                        out_ref[span, cols : cols + half] = both.astype(BF16)
                        out_ref[span, cols + half :] = columns[src : src + size, :]


def grad_ff_kernel(blocks, ix, n3, n2, n1, n0, u3, u2, u10, a3, a2, a10, d3, d2, d1, d0, out_ref, nt, at_t, up, dy):
    step = pl.program_id(0)
    depth = n3.shape[0]

    @pl.when(step == 0)
    def _():
        for i, (n, d) in enumerate(((n3, d3), (n2, d2), (n1, d1), (n0, d0))):
            span = slice(i * depth, (i + 1) * depth)
            t = n[...].T
            for dst, src, size in blocks:
                nt[dst : dst + size, span] = t[src : src + size, :]
            dy[span, :] = d[...]
        for first, a, u in ((0, a3, u3), (1, a2, u2), (2, a10, u10)):
            span = slice(first * depth, first * depth + a.shape[0])
            at_t[:, span] = a[...].T
            up[span, :] = u[...]

    rows, units = out_ref.shape[0], up.shape[1]
    mine = at(step * rows, rows, 16)
    out_ref[:, :units] = dot(nt[mine, :], up[...], NN).astype(BF16)
    out_ref[:, units:] = dot(at_t[mine, :], dy[...], NN).astype(BF16)


def spread_kernel(ix, one, two, out_ref):
    odd = ix[2]
    out_ref[odd] = one[...].astype(F32)
    out_ref[1 - odd] = two[...].astype(F32)


def home_kernel(ix, summed, *parts):
    core, y = ix[1], ix[3]
    rows, cols = parts[0].shape
    for p in range(4):
        block = (core ^ (p & 1)) * 2 + (y ^ (p >> 1))
        parts[p][...] = summed[at(block * rows, rows, 8), 0:cols]


def settle_kernel(ix, p0, p1, p2, p3, qkv_ref, out_ref, vec_ref, tile):
    rank, core = ix[0], ix[1]
    parts = (p0, p1, p2, p3)
    rows, width = out_ref.shape
    quarter, half = width // 4, width // 2
    for p in range(4):
        a = rank ^ p
        for t in range(3):
            qkv_ref[:, at(t * width + a * quarter, quarter, 128)] = parts[p][:, t * quarter : (t + 1) * quarter].astype(F32)
    c1, c2 = 3 * quarter, 3 * quarter + half
    for p in range(2):
        out_ref[:, at((core ^ p) * half, half, 128)] = parts[p][:, c1:c2].astype(F32) + parts[p + 2][:, c1:c2].astype(F32)
    tile[...] = jnp.zeros_like(tile)
    tile[0:rows, :] = sum(v[:, c2:].astype(F32) for v in parts)
    vec_ref[...] = tile[...].T[0:8, :]


def settle_ff_kernel(spots, ix, p0, p1, p2, p3, up_ref):
    core, y = ix[1], ix[3]
    hid, zs = 128, len(spots) // 2
    for p, part in enumerate((p0, p1, p2, p3)):
        c2, y2 = core ^ (p & 1), y ^ (p >> 1)
        for b, (nx, nz) in enumerate(spots):
            dst = ((nx * 2 + c2) * zs + nz) * 2 + y2
            up_ref[:, at(dst * hid, hid, 128)] = part[:, b * hid : (b + 1) * hid].astype(F32)


class Places:
    def __init__(self, mesh):
        self.n_dp, self.n_fsdp = mesh.shape["dp"], mesh.shape["fsdp"]
        self.xs, self.zs = self.n_dp // 2, self.n_fsdp // 2
        self.nodes = self.xs * self.zs
        self.all = [
            (x, c, z, y) for x in range(self.xs) for c in range(2) for z in range(self.zs) for y in range(2)
        ]

    def lin(self, x, c, z, y):
        return (x * 2 + c) * self.n_fsdp + z * 2 + y

    def perm(self, move):
        return [(self.lin(*d), self.lin(*move(*d))) for d in self.all]

    def spot(self, x, z):
        return x * self.zs + (z if x % 2 == 0 else self.zs - 1 - z)

    def node(self, spot):
        x, z = spot // self.zs, spot % self.zs
        return (x, z if x % 2 == 0 else self.zs - 1 - z)

    def rings(self):
        return [
            [self.lin(x, c, z, y) for x, z in map(self.node, range(self.nodes))] for c in range(2) for y in range(2)
        ]


def permute(array, pairs):
    return lax.ppermute(array, AXES, pairs)


def after(value, *done):
    return lax.optimization_barrier((value,) + done)[0]


def body(pc, tokens, scene_ids, w_qkv, w_out, w_up, w_down, gain_one, bias_one, gain_two, bias_two, cotangent):
    micro, run, width = tokens.shape
    rows = w_qkv.shape[0]
    ff = w_up.shape[1]
    units = ff // 4
    hid = w_down.shape[0]
    quarter, half = width // 4, width // 2
    own = micro * run
    dp, fsdp = lax.axis_index("dp"), lax.axis_index("fsdp")
    x, core, z, y = dp // 2, dp % 2, fsdp // 2, fsdp % 2
    rank = y * 2 + core
    groups = micro * 2
    quads = pc.zs // groups
    rings = pc.rings()
    spots = [pc.node(i) for i in range(pc.nodes)]
    blocks = row_blocks(spots, 2 * rows)
    aligned = hid % 128 == 0

    p_core = pc.perm(lambda x, c, z, y: (x, 1 - c, z, y))
    p_y = pc.perm(lambda x, c, z, y: (x, c, z, 1 - y))
    p_diag = pc.perm(lambda x, c, z, y: (x, 1 - c, z, 1 - y))

    def place_perm(flip):
        def move(x, c, z, y):
            m = (z % 2) ^ flip
            return (x, (z // 2) % 2, (m * 2 + c) * quads + z // 4, y)

        return pc.perm(move)

    p_place = [place_perm(0), place_perm(1)]
    p_back = [[(b, a) for a, b in pairs] for pairs in p_place]

    def group_perm(by):
        return pc.perm(lambda x, c, z, y: (x, c, z // quads * quads + (z + by) % quads, y))

    ix = jnp.stack([rank, core, z % 2, y]).astype(jnp.int32)

    def quad_swap(parts):
        return [parts[0], permute(parts[1], p_core), permute(parts[2], p_y), permute(parts[3], p_diag)]

    def by_rank(parts):
        odd, top = rank % 2 == 1, rank // 2 == 1
        parts = [jnp.where(odd, parts[i ^ 1], parts[i]) for i in range(4)]
        return [jnp.where(top, parts[i ^ 2], parts[i]) for i in range(4)]

    def by_rows(parts):
        r = by_rank(parts)
        return jnp.concatenate([r[0], r[2], r[1], r[3]], 0)

    def ring_gather(shard):
        return lax.all_gather(shard, AXES, axis=0, tiled=True, axis_index_groups=rings)

    def ring_sum(terms):
        return lax.psum_scatter(terms, AXES, scatter_dimension=0, tiled=True, axis_index_groups=rings)

    c_out, c_small, wide = 3 * quarter, 3 * quarter + half, 3 * quarter + half + 128
    wu = w_up
    if not aligned:
        wu = w_up.reshape(rows, pc.xs, 2, pc.zs, 2, hid)
        wu = [
            lax.dynamic_slice(
                wu, (0, 0, core ^ (p & 1), 0, y ^ (p >> 1), 0), (rows, pc.xs, 1, pc.zs, 1, hid)
            ).reshape(rows, pc.xs, pc.zs, hid)
            for p in range(4)
        ]
        wu = jnp.concatenate([w[:, nx, nz] for w in wu for nx, nz in spots], 1)
    *packed, x_one, x_two, dy_one, dy_two = call(
        functools.partial(pack_kernel, aligned, spots),
        "pack",
        (
            ix,
            w_qkv,
            w_out,
            jnp.stack([gain_one, bias_one, gain_two, bias_two]),
            tokens,
            scene_ids.reshape(micro, run),
            cotangent,
            wu,
        ),
        [shape_of((rows, wide))] * 4 + [shape_of((rows, units))] * 4 + [shape_of((run + 8, width))] * 2 + [shape_of((run, width))] * 2,
        scratch=[pltpu.VMEM((128, 128), F32)],
        room=58,
    )
    shard = by_rows(quad_swap(packed[:4]))
    x_first = permute(x_one, p_place[0])
    x_own = jnp.concatenate([x_first, permute(x_two, p_place[1])], 0)
    first = ring_gather(after(shard, x_first))
    x_across = permute(x_own, p_y)
    taken = [x_own, permute(x_own, p_core), x_across, permute(x_across, p_core)]
    up_shard = by_rows(quad_swap(after(packed[4:], x_across)))
    second = ring_gather(after(jnp.concatenate([up_shard, w_down], 1), taken))
    dy_one, dy_two = after((dy_one, dy_two), first)
    dy_own = jnp.concatenate([permute(dy_one, p_place[0]), permute(dy_two, p_place[1])], 0)

    block = (own, width)
    n_one, projected, full_qkv, near_out, gains, qrow = call(
        functools.partial(project_kernel, blocks, run),
        "project",
        (ix, *taken, first),
        [
            shape_of((4 * own, width)),
            shape_of((4 * own, 3 * quarter)),
            shape_of((width, 3 * quarter)),
            shape_of((width, half)),
            shape_of((8, width), F32),
            shape_of((1, 4 * own), F32),
        ],
        scratch=[pltpu.VMEM((width, 128), F32)],
        grid=(4,),
        flops=2 * 4 * own * width * 3 * quarter,
        out_specs={
            0: pl.BlockSpec(block, lambda i: (i, 0)),
            1: pl.BlockSpec((own, 3 * quarter), lambda i: (i, 0)),
        },
    )
    far_out = permute(near_out, p_core)
    if quads == 1:
        q, k, v, krow = (projected, 0), (projected, 1), (projected, 2), qrow
    else:
        kv = projected[:, quarter:]
        kv_all = jnp.concatenate([kv] + [permute(kv, group_perm(s)) for s in range(1, quads)], 0)
        krow = jnp.concatenate([qrow] + [permute(qrow, group_perm(s)) for s in range(1, quads)], 1)
        q, k, v = (projected, 0), (kv_all, 0), (kv_all, 1)
    *m_far, lse_far = attend(ix, q, k, v, quarter, qrow, krow, 2)
    dy_across = permute(after(dy_own, m_far), p_y)
    *m_near, lse_near = attend(ix, q, k, v, quarter, after(qrow, m_far, dy_own), krow, 0)
    mixed = quad_swap([*m_near, *m_far])
    mixed_own, hidden, n_two = call(
        functools.partial(mix_out_kernel, run),
        "mix_out",
        (ix, *mixed, near_out, far_out, taken[0], gains),
        [shape_of(block), shape_of(block, F32), shape_of(block)],
        flops=2 * own * width * width,
    )
    def far_sum(keep, got):
        return (keep + got.astype(F32)).astype(BF16)

    n_across = permute(after(n_two, dy_across), p_y)
    norms = [n_two, permute(n_two, p_core), n_across, permute(n_across, p_core)]
    dys = [dy_own, permute(dy_own, p_core), dy_across, permute(dy_across, p_core)]

    def hidden_units(parts, weights, kinds, order):
        outs = [shape_of((len(parts) * own, units))] * 2 + [shape_of(block, kind) for kind in kinds * 2]
        return call(
            functools.partial(hidden_units_kernel, parts, order),
            "hidden_units",
            (ix, *[norms[p] for p in parts], *[dys[p] for p in parts], *weights),
            outs + ([shape_of((width, units)), shape_of((units, width))] if order else []),
            flops=8 * len(parts) * own * width * units,
            transcendentals=2 * len(parts) * own * units,
        )

    act3, up3, give3, r_give3, full_up, full_down = hidden_units((3,), (second,), (BF16,), blocks)
    got3 = permute(give3, p_core)
    act2, up2, keep2, r_keep2 = hidden_units((2,), (after(full_up, give3), full_down), (F32,), None)
    far = far_sum(keep2, got3)
    across = permute(far, p_y)
    act10, up10, give1, keep0, r_give1, r_keep0 = hidden_units((1, 0), (after(full_up, far), full_down), (BF16, F32), None)
    got = permute(give1, p_core)
    in_order = [(i, i, n) for i, _, n in blocks]

    def grads(name, lefts, rights, order, extra=()):
        widths = tuple(r[0].shape[1] for r in rights)
        depth, cols = sum(a.shape[0] for a in lefts), sum(widths)
        height = lefts[0].shape[1]
        total = cols + sum(e.shape[1] for e in extra[1:])
        return call(
            functools.partial(grads_kernel, order, len(lefts), widths, len(rights[0]), len(extra)),
            name,
            (ix, *lefts, *[piece for r in rights for piece in r], *extra),
            [shape_of((height, total))],
            scratch=[pltpu.VMEM((height, depth), BF16)] + [pltpu.VMEM((depth, w), BF16) for w in widths],
            grid=(4,),
            flops=2 * depth * height * cols,
            out_specs={0: pl.BlockSpec((height // 4, total), lambda i: (i, 0))},
        )[0]

    order = (3, 2, 1, 0)
    (ff_terms,) = call(
        functools.partial(grad_ff_kernel, blocks),
        "grad_ff",
        (ix, *[norms[p] for p in order], up3, up2, up10, act3, act2, act10, *[dys[p] for p in order]),
        [shape_of((width, units + width))],
        scratch=[pltpu.VMEM((width, 4 * own), BF16), pltpu.VMEM((units, 4 * own), BF16)]
        + [pltpu.VMEM((4 * own, units), BF16), pltpu.VMEM((4 * own, width), BF16)],
        grid=(4,),
        flops=2 * 4 * own * width * 2 * units,
        out_specs={0: pl.BlockSpec((width // 4, units + width), lambda i: (i, 0))},
    )
    ff_sum = ring_sum(ff_terms)
    up_sum, down_sum = ff_sum[:, :units], ff_sum[:, units:]
    *d_parts, d_hidden, d_low, sums_two = call(
        hidden_back_kernel,
        "hidden_back",
        (ix, keep0, got, across, hidden, dys[0], after(gains, ff_terms), near_out, far_out),
        [shape_of((own, quarter))] * 4 + [shape_of(block, F32), shape_of(block), shape_of((8, width), F32)],
        flops=2 * own * width * width,
    )
    d_mixed = quad_swap(d_parts)
    near_parts, far_parts = d_mixed[:2], d_mixed[2:]
    r_far = far_sum(r_keep2, permute(after(r_give3, d_parts[0]), p_core))
    r_across = permute(r_far, p_y)
    r_got = permute(after(r_give1, d_parts[0]), p_core)
    dq_near, kept = attend_back(ix, q, k, v, quarter, qrow, krow, lse_near, near_parts, 0, ())
    dq_far, dkv = attend_back(ix, q, k, v, quarter, qrow, krow, lse_far, far_parts, 2, (after(kept, r_far),))

    def placed(one, two):
        return [permute(one, p_back[0]), permute(two, p_back[1])]

    r_own = (after(hidden, dq_far) + r_keep0 + r_got.astype(F32) + r_across.astype(F32)).astype(BF16)
    back_out = placed(r_own[:run], r_own[run:])
    n_rows = dkv.shape[0] // quads
    if quads > 1:
        total = dkv[:n_rows].astype(F32)
        for s in range(1, quads):
            total = total + permute(dkv[s * n_rows : (s + 1) * n_rows], group_perm(-s)).astype(F32)
        dkv = total.astype(BF16)

    keep_one, give_one, columns = call(
        functools.partial(project_back_kernel, run),
        "project_back",
        (ix, *taken, dq_near, dq_far, dkv, full_qkv, after(sums_two, r_own)),
        [shape_of((2 * own, width), F32), shape_of((2 * own, width)), shape_of((width, 128))],
        scratch=[pltpu.VMEM((128, width), F32)],
        grid=(4,),
        flops=2 * 4 * own * width * 3 * quarter,
        in_specs={
            6: pl.BlockSpec((own, 2 * quarter), lambda i: (jnp.where(i == 0, 1, jnp.where(i == 1, 3, (i - 2) * 2)), 0)),
        },
    )
    got_one = permute(give_one, p_core)
    grad_near, grad_far = call(
        out_grad_kernel,
        "out_grad",
        (ix, after(mixed_own, give_one), d_low),
        [shape_of((width, half), F32), shape_of((width, half))],
        flops=2 * own * width * width,
    )
    far_one = far_sum(keep_one[own:], after(got_one, grad_near)[own:])
    across_one = permute(far_one, p_y)
    at_terms = grads(
        "grad_at",
        [after(n_one, far_one)],
        [[jnp.concatenate([dq_near, dq_far], 0)], [dkv]],
        blocks,
        (grad_near, permute(grad_far, p_core), columns),
    )
    one_sum = ring_sum(after(at_terms, ff_sum, back_out))

    def home(name, summed):
        return quad_swap(call(home_kernel, name, (ix, summed), [shape_of((rows, summed.shape[1]))] * 4))

    def in_batches(one, two):
        return jnp.stack([jnp.where(z % 2 == 0, one, two), jnp.where(z % 2 == 0, two, one)], 0)

    d_one, d_two = call(
        functools.partial(tokens_back_kernel, run),
        "tokens_back",
        (ix, keep_one, got_one, across_one, taken[0], d_hidden, after(gains, ff_sum, back_out)),
        [shape_of((run, width))] * 2,
    )
    ff_home = home("home_up", after(up_sum, d_one))
    own_down = down_sum.astype(F32)
    if aligned:
        (own_up,) = call(
            functools.partial(settle_ff_kernel, spots), "settle_ff", (ix, *ff_home), [shape_of((rows, 4 * units), F32)])
    else:
        ups = [b.reshape(rows, pc.nodes, hid) for b in ff_home]
        at_spot = [[spots.index((nx, nz)) for nz in range(pc.zs)] for nx in range(pc.xs)]
        ups = by_rank([jnp.stack([jnp.stack([b[:, i] for i in row], 1) for row in at_spot], 1) for b in ups])
        own_up = (
            jnp.stack([jnp.stack([ups[0], ups[2]], 3), jnp.stack([ups[1], ups[3]], 3)], 2)
            .reshape(rows, 4 * units)
            .astype(F32)
        )
    back_grad = placed(*after((d_one, d_two), own_up))
    at_home = home("home_at", after(one_sum, back_out))
    output = in_batches(*after(back_out, d_one))
    own_qkv, own_out, vectors = call(
        settle_kernel,
        "settle",
        (ix, *at_home),
        [shape_of((rows, 3 * width), F32), shape_of((rows, width), F32), shape_of((8, 128), F32)],
        scratch=[pltpu.VMEM((128, 128), F32)],
    )
    (input_grad,) = call(
        spread_kernel, "spread", (ix, *after(back_grad, own_qkv)), [shape_of((micro, run, width), F32)]
    )
    return (output, input_grad, own_qkv, own_out, own_up, own_down) + tuple(vectors[i, :rows] for i in range(4))


def solution(mesh):
    vector, matrix, batch = P(AXES), P(AXES, None), P(None, AXES, None)
    return jax.shard_map(
        functools.partial(body, Places(mesh)),
        mesh=mesh,
        in_specs=(batch, P(None, "dp", "fsdp")) + (matrix,) * 4 + (vector,) * 4 + (batch,),
        out_specs=(batch, batch) + (matrix,) * 4 + (vector,) * 4,
        check_vma=False,
    )
```

```python
import functools
import math

import jax
import jax.numpy as jnp
from jax import lax
from jax.experimental import pallas as pl
from jax.experimental.pallas import tpu as pltpu
from jax.sharding import PartitionSpec as P

AXES = ("dp", "fsdp")
HEAD_DIM = 64
EPS = 1e-05
LOWEST = -1000000000.0
F32 = jnp.float32
BF16 = jnp.bfloat16
NT = (((1,), (1,)), ((), ()))
TN = (((0,), (0,)), ((), ()))
NN = (((1,), (0,)), ((), ()))
ROOM = 20
IN_HBM = ("grad_ff", "grad_at")
HINTS = {"home_at": 1000, "settle": 8, "mix_out": 0, "grad_ff": 3, "hidden_units": 8, "hidden_back": 300, "attend_back": 4, "grad_down": 0, "home_up": 0, "settle_ff": 0, "out_grad": 0, "project_back": 0, "grad_at": 0, "tokens_back": 0, "down": 8}


def dot(left, right, dims):
    return lax.dot_general(left, right, dims, preferred_element_type=F32)


def at(start, size, step):
    return pl.ds(pl.multiple_of(start, step), size)


def call(kernel, name, args, outs, scratch=(), grid=None, flops=0, transcendentals=0, in_specs=None, out_specs=None, room=ROOM):
    whole = pl.BlockSpec(memory_space=pltpu.VMEM) if grid is None else None

    def spec(shape):
        return whole or pl.BlockSpec(shape, lambda i, n=len(shape): (0,) * n)

    specs = [pl.BlockSpec(memory_space=pltpu.SMEM)]
    specs += [(in_specs or {}).get(n) or spec(a.shape) for n, a in enumerate(args[1:])]
    size = sum(math.prod(a.shape) * a.dtype.itemsize for a in list(args) + list(outs))
    return pl.pallas_call(
        kernel,
        out_shape=tuple(pltpu.HBM(o.shape, o.dtype) for o in outs) if name in IN_HBM else tuple(outs),
        in_specs=specs,
        out_specs=tuple((out_specs or {}).get(n) or spec(o.shape) for n, o in enumerate(outs)),
        scratch_shapes=list(scratch),
        compiler_params=pltpu.CompilerParams(vmem_limit_bytes=min(room, 58) * 1024 * 1024),
        cost_estimate=pl.CostEstimate(
            flops=HINTS.get(name, 8) * flops, bytes_accessed=HINTS.get(name, 8) * size, transcendentals=transcendentals
        ),
        name=name,
        **({} if grid is None else {"grid": grid}),
    )(*args)


def shape_of(shape, dtype=BF16):
    return jax.ShapeDtypeStruct(shape, dtype)


def centre(v):
    c = v - jnp.mean(v, axis=-1, keepdims=True)
    inv = lax.rsqrt(jnp.mean(c * c, axis=-1, keepdims=True) + EPS)
    return c * inv, inv


def norm_back(d_norm, std, inv, gain):
    d_std = d_norm * gain
    return inv * (
        d_std - jnp.mean(d_std, axis=-1, keepdims=True) - std * jnp.mean(d_std * std, axis=-1, keepdims=True)
    )


def pack_kernel(aligned, spots, ix, qkv, out, gains, tokens, scenes, dy, up, *refs):
    parts, ups, (one, two, dy_one, dy_two, tile) = refs[:4], refs[4:8], refs[8:]
    rank, core, odd, y = ix[0], ix[1], ix[2], ix[3]
    rows, width = qkv.shape[0], out.shape[1]
    quarter, half = width // 4, width // 2
    tile[...] = jnp.zeros_like(tile)
    tile[0:4, 0:rows] = gains[...].astype(F32)
    small = tile[...].T[:rows].astype(BF16)
    c1, c2 = 3 * quarter, 3 * quarter + half
    hid, units = 128, up.shape[1] // 4
    zs = len(spots) // 2
    for p in range(4):
        a = rank ^ p
        for t in range(3):
            parts[p][:, t * quarter : (t + 1) * quarter] = qkv[:, at(t * width + a * quarter, quarter, 128)]
        parts[p][:, c1:c2] = out[:, at((core ^ (p & 1)) * half, half, 128)]
        parts[p][:, c2 : c2 + 128] = small
        if aligned:
            for b, (nx, nz) in enumerate(spots):
                src = ((nx * 2 + (core ^ (p & 1))) * zs + nz) * 2 + (y ^ (p >> 1))
                ups[p][:, b * hid : (b + 1) * hid] = up[:, at(src * hid, hid, 128)]
        else:
            ups[p][...] = up[:, p * units : (p + 1) * units]
    run = tokens.shape[1]
    for ref, low, m in ((one, dy_one, odd), (two, dy_two, 1 - odd)):
        ref[0:run, :] = tokens[m]
        ref[run:, :] = jnp.zeros((ref.shape[0] - run, width), BF16)
        ref[run : run + 1, 0:run] = scenes[pl.ds(m, 1), :].astype(F32).astype(BF16)
        low[...] = dy[m]


def row_blocks(spots, size):
    zs = len(spots) // 2
    return [
        ((2 * i + c) * size, ((nx * 2 + c) * zs + nz) * size, size) for i, (nx, nz) in enumerate(spots) for c in (0, 1)
    ]


def project_kernel(blocks, run, ix, *refs):
    taken, first = refs[:4], refs[4]
    n_ref, p_ref, w_ref, near_ref, gains_ref, scene_ref, g_all = refs[5:]
    step = pl.program_id(0)
    c_out, c_small = w_ref.shape[1], w_ref.shape[1] + near_ref.shape[1]

    @pl.when(step == 0)
    def _():
        for src, dst, size in blocks:
            v = first[src : src + size, :]
            w_ref[dst : dst + size, :] = v[:, :c_out]
            near_ref[dst : dst + size, :] = v[:, c_out:c_small]
            g_all[dst : dst + size, :] = v[:, c_small:].astype(F32)
        gains_ref[...] = g_all[...].T[0:8, :]
        for p in range(4):
            for s in range(2):
                row = taken[p][s * (run + 8) + run : s * (run + 8) + run + 1, 0:run]
                scene_ref[0:1, (2 * p + s) * run : (2 * p + s + 1) * run] = row.astype(F32)

    for p in range(4):

        @pl.when(step == p)
        def _():
            x = taken[p]
            v = jnp.concatenate([x[0:run, :], x[run + 8 : 2 * run + 8, :]], 0).astype(F32)
            std, _ = centre(v)
            n = (std * gains_ref[0:1, :] + gains_ref[1:2, :]).astype(BF16)
            n_ref[...] = n
            p_ref[...] = dot(n, w_ref[...], NN).astype(BF16)


def head_lanes(rows, width, head):
    lane = lax.broadcasted_iota(jnp.int32, (rows, width), 1)
    return (lane >= head * HEAD_DIM) & (lane < (head + 1) * HEAD_DIM)


def column(row):
    return jnp.broadcast_to(row, (128, row.shape[1])).T


def same_scene(ksc, qrow):
    return jnp.concatenate([ksc == qrow[:, i : i + 128] for i in range(0, qrow.shape[1], 128)], 1)


def attend_kernel(heads, ix, krow_ref, qrow_ref, q_ref, k_ref, v_ref, *refs):
    outs_ref, (lse_ref, vt_ref, ksc_ref) = refs[:2], refs[2:]
    step = pl.program_id(0)

    @pl.when(step == 0)
    def _():
        vt_ref[...] = v_ref[...].astype(F32).T.astype(BF16)
        ksc_ref[...] = column(krow_ref[...])

    rows, width = q_ref.shape
    same = same_scene(ksc_ref[...], qrow_ref[...])
    q = q_ref[...].astype(F32) * (1.0 / math.sqrt(HEAD_DIM))
    outs = []
    for h in range(heads):
        qh = jnp.where(head_lanes(rows, width, h), q, 0.0).astype(BF16)
        s = jnp.where(same, dot(k_ref[...], qh, NT), LOWEST)
        peak = jnp.max(s, axis=0, keepdims=True)
        e = jnp.exp(s - peak)
        total = jnp.sum(e, axis=0, keepdims=True)
        lse_ref[h : h + 1, :] = peak + jnp.log(total)
        p = (e * (1.0 / total)).astype(BF16)
        outs.append(dot(vt_ref[h * HEAD_DIM : (h + 1) * HEAD_DIM, :], p, NN))
    mixed = jnp.concatenate(outs, axis=0).T.astype(BF16)
    for i in range(2):

        @pl.when(step == i)
        def _():
            outs_ref[i][...] = mixed


def attend(ix, q, k, v, quarter, qrow, krow, first):
    rows, keys = q[0].shape[0], k[0].shape[0]
    heads, block = quarter // HEAD_DIM, rows // 4
    return call(
        functools.partial(attend_kernel, heads),
        "attend",
        (ix, krow, qrow, q[0], k[0], v[0]),
        [shape_of((block, quarter))] * 2 + [shape_of((heads, 2 * block), F32)],
        scratch=[pltpu.VMEM((quarter, keys), BF16), pltpu.VMEM((keys, 128), F32)],
        grid=(2,),
        room=ROOM * keys // rows,
        flops=2 * rows * keys * quarter,
        transcendentals=rows * keys * heads // 2,
        in_specs={
            1: pl.BlockSpec((1, block), lambda i: (0, i + first)),
            2: pl.BlockSpec((block, quarter), lambda i, c=q[1]: (i + first, c)),
            3: pl.BlockSpec((keys, quarter), lambda i, c=k[1]: (0, c)),
            4: pl.BlockSpec((keys, quarter), lambda i, c=v[1]: (0, c)),
        },
        out_specs={2: pl.BlockSpec((heads, block), lambda i: (0, i))},
    )


def attend_back_kernel(heads, more, ix, krow_ref, qrow_ref, lse_ref, q_ref, k_ref, v_ref, *refs):
    do_refs, kept, refs = refs[:2], refs[2 : 2 + more], refs[2 + more :]
    dq_ref, dkv_ref, kt_ref, ksc_ref, dka_ref, dva_ref, do_ref = refs
    width = q_ref.shape[1]
    step = pl.program_id(0)

    @pl.when(step == 0)
    def _():
        kt_ref[...] = k_ref[...].astype(F32).T.astype(BF16)
        ksc_ref[...] = column(krow_ref[...])
        if more:
            dka_ref[...] = kept[0][:, :width]
            dva_ref[...] = kept[0][:, width:]
        else:
            dka_ref[...] = jnp.zeros_like(dka_ref)
            dva_ref[...] = jnp.zeros_like(dva_ref)

    for i in range(2):

        @pl.when(step == i)
        def _():
            do_ref[...] = do_refs[i][...].astype(F32)

    rows, width = q_ref.shape
    scale = 1.0 / math.sqrt(HEAD_DIM)
    same = same_scene(ksc_ref[...], qrow_ref[...])
    q = q_ref[...].astype(F32) * scale
    do = do_ref[...]
    outs = []
    for h in range(heads):
        mine = head_lanes(rows, width, h)
        qh = jnp.where(mine, q, 0.0).astype(BF16)
        doh = jnp.where(mine, do, 0.0).astype(BF16)
        s = jnp.where(same, dot(k_ref[...], qh, NT), LOWEST)
        p = jnp.exp(s - lse_ref[h : h + 1, :])
        dp = dot(v_ref[...], doh, NT)
        inner = jnp.sum(p * dp, axis=0, keepdims=True)
        ds = (p * (dp - inner)).astype(BF16)
        dva_ref[...] += dot(p.astype(BF16), doh, NN)
        dka_ref[...] += dot(ds, qh, NN)
        outs.append(dot(kt_ref[h * HEAD_DIM : (h + 1) * HEAD_DIM, :], ds, NN))
    dq_ref[...] = (jnp.concatenate(outs, axis=0).T * scale).astype(BF16)

    @pl.when(step == pl.num_programs(0) - 1)
    def _():
        dkv_ref[:, :width] = dka_ref[...].astype(dkv_ref.dtype)
        dkv_ref[:, width:] = dva_ref[...].astype(dkv_ref.dtype)


def attend_back(ix, q, k, v, quarter, qrow, krow, lse, do, first, kept):
    rows, keys = q[0].shape[0], k[0].shape[0]
    heads, block = quarter // HEAD_DIM, rows // 4
    return call(
        functools.partial(attend_back_kernel, heads, len(kept)),
        "attend_back",
        (ix, krow, qrow, lse, q[0], k[0], v[0], *do, *kept),
        [shape_of((2 * block, quarter)), shape_of((keys, 2 * quarter), BF16 if kept else F32)],
        scratch=[
            pltpu.VMEM((quarter, keys), BF16),
            pltpu.VMEM((keys, 128), F32),
            pltpu.VMEM((keys, quarter), F32),
            pltpu.VMEM((keys, quarter), F32),
            pltpu.VMEM((block, quarter), F32),
        ],
        grid=(2,),
        room=ROOM * keys // rows,
        flops=5 * rows * keys * quarter,
        transcendentals=rows * keys * heads // 2,
        in_specs={
            1: pl.BlockSpec((1, block), lambda i: (0, i + first)),
            2: pl.BlockSpec((heads, block), lambda i: (0, i)),
            3: pl.BlockSpec((block, quarter), lambda i, c=q[1]: (i + first, c)),
            4: pl.BlockSpec((keys, quarter), lambda i, c=k[1]: (0, c)),
            5: pl.BlockSpec((keys, quarter), lambda i, c=v[1]: (0, c)),
        },
        out_specs={0: pl.BlockSpec((block, quarter), lambda i: (i, 0))},
    )


def mix_out_kernel(run, ix, m0, m1, m2, m3, near, far, x, gains, mixed_ref, hidden_ref, n_ref):
    rank, core = ix[0], ix[1]
    quarter, half = m0.shape[1], near.shape[1]
    for p, m in enumerate((m0, m1, m2, m3)):
        mixed_ref[:, at((rank ^ p) * quarter, quarter, 128)] = m[...]
    mixed = mixed_ref[...]
    hidden_ref[0:run, :] = x[0:run, :].astype(F32)
    hidden_ref[run:, :] = x[run + 8 : 2 * run + 8, :].astype(F32)
    hidden_ref[:, at(core * half, half, 128)] += dot(mixed, near[...], NN)
    hidden_ref[:, at((1 - core) * half, half, 128)] += dot(mixed, far[...], NN)
    std, _ = centre(hidden_ref[...])
    n_ref[...] = (std * gains[2:3, :] + gains[3:4, :]).astype(BF16)


def hidden_units_kernel(parts, blocks, ix, *refs):
    n, rows = len(parts), refs[0].shape[0]
    norms, dys, refs = refs[:n], refs[n : 2 * n], refs[2 * n :]
    if blocks:
        second, act_ref, dup_ref, *term_refs, up_ref, down_ref = refs
        units = up_ref.shape[1]
        for src, dst, size in blocks:
            up_ref[dst : dst + size, :] = second[src : src + size, :units]
        down_ref[...] = second[:, units:]
    else:
        up_ref, down_ref, act_ref, dup_ref, *term_refs = refs
    for i in range(n):
        span = slice(i * rows, (i + 1) * rows)
        u = dot(norms[i][...], up_ref[...], NN)
        cdf = 0.5 * (1.0 + lax.erf(u * math.sqrt(0.5)))
        act = (u * cdf).astype(BF16)
        act_ref[span, :] = act
        term_refs[n + i][...] = dot(act, down_ref[...], NN).astype(term_refs[n + i].dtype)
        slope = cdf + u * jnp.exp(-0.5 * u * u) * (1.0 / math.sqrt(2.0 * math.pi))
        dup = (dot(dys[i][...], down_ref[...], NT) * slope).astype(BF16)
        dup_ref[span, :] = dup
        term_refs[i][...] = dot(dup, up_ref[...], NT).astype(term_refs[i].dtype)


def hidden_back_kernel(ix, keep, got, across, hidden, dy, gains, near, far, *refs):
    parts, (dh_ref, low_ref, sums_ref) = refs[:4], refs[4:]
    rank, core = ix[0], ix[1]
    rows = hidden.shape[0]
    half, quarter = near.shape[1], parts[0].shape[1]
    d_norm = keep[...] + got[...].astype(F32) + across[...].astype(F32)
    std, inv = centre(hidden[...])
    sums_ref[...] = jnp.zeros_like(sums_ref)
    sums_ref[2:3, :] = jnp.sum(d_norm * std, axis=0, keepdims=True)
    sums_ref[3:4, :] = jnp.sum(d_norm, axis=0, keepdims=True)
    d_hidden = dy[...].astype(F32) + norm_back(d_norm, std, inv, gains[2:3, :])
    dh_ref[...] = d_hidden
    low_ref[...] = d_hidden.astype(BF16)
    a, b = low_ref[:, at(core * half, half, 128)], low_ref[:, at((1 - core) * half, half, 128)]
    for p in range(4):
        rows_p = at((rank ^ p) * quarter, quarter, 16)
        parts[p][...] = (dot(a, near[rows_p, :], NT) + dot(b, far[rows_p, :], NT)).astype(BF16)


def out_grad_kernel(ix, mixed, low, near_ref, far_ref):
    core, half = ix[1], near_ref.shape[1]
    left = mixed[...].astype(F32).T.astype(BF16)
    near_ref[...] = dot(left, low[:, at(core * half, half, 128)], NN)
    far_ref[...] = dot(left, low[:, at((1 - core) * half, half, 128)], NN).astype(BF16)


def project_back_kernel(run, ix, *refs):
    taken, (dq_a, dq_b, dkv, w, sums2, keep_ref, give_ref, cols_ref, sums) = refs[:4], refs[4:]
    step = pl.program_id(0)
    quarter, rows = dq_a.shape[1], dkv.shape[0]

    @pl.when(step == 0)
    def _():
        sums[...] = jnp.zeros_like(sums)
        sums[0:8, :] = sums2[...]

    for i, p in enumerate((1, 3, 0, 2)):

        @pl.when(step == i)
        def _():
            x = taken[p]
            std, _ = centre(jnp.concatenate([x[0:run, :], x[run + 8 : 2 * run + 8, :]], 0).astype(F32))
            dq = (dq_a, dq_b)[p >> 1][(p & 1) * rows : ((p & 1) + 1) * rows, :]
            part = dot(dq, w[:, 0:quarter], NT) + dot(dkv[...], w[:, quarter:], NT)
            sums[0:1, :] += jnp.sum(part * std, axis=0, keepdims=True)
            sums[1:2, :] += jnp.sum(part, axis=0, keepdims=True)
            if p & 1:
                give_ref[(p >> 1) * rows : ((p >> 1) + 1) * rows, :] = part.astype(BF16)
            else:
                keep_ref[(p >> 1) * rows : ((p >> 1) + 1) * rows, :] = part

    @pl.when(step == 3)
    def _():
        cols_ref[...] = sums[...].T.astype(BF16)


def tokens_back_kernel(run, ix, keep, got, across, x, d_hidden, gains, one_ref, two_ref):
    rows = d_hidden.shape[0]
    d_norm = keep[0:rows, :] + got[0:rows, :].astype(F32) + across[...].astype(F32)
    std, inv = centre(jnp.concatenate([x[0:run, :], x[run + 8 : 2 * run + 8, :]], 0).astype(F32))
    d = (d_hidden[...] + norm_back(d_norm, std, inv, gains[0:1, :])).astype(BF16)
    one_ref[...] = d[0:run]
    two_ref[...] = d[run:]


def grads_kernel(blocks, n_left, widths, n_right, extra, ix, *refs):
    lefts, refs = refs[:n_left], refs[n_left:]
    rights, refs = [refs[i * n_right : (i + 1) * n_right] for i in range(len(widths))], refs[len(widths) * n_right :]
    out_ref, left_t, *right_refs = refs[extra:]
    step = pl.program_id(0)
    cols = sum(widths)

    @pl.when(step == 0)
    def _():
        at_col = 0
        for piece in lefts:
            t = piece[...].T
            stop = at_col + t.shape[1]
            for dst, src, size in blocks:
                left_t[dst : dst + size, at_col:stop] = t[src : src + size, :]
            at_col = stop
        for pieces, ref in zip(rights, right_refs):
            row = 0
            for piece in pieces:
                ref[row : row + piece.shape[0], :] = piece[...]
                row += piece.shape[0]

    rows = out_ref.shape[0]
    mine = left_t[at(step * rows, rows, 16), :]
    start = 0
    for ref, w in zip(right_refs, widths):
        out_ref[:, start : start + w] = dot(mine, ref[...], NN).astype(BF16)
        start += w
    if extra:
        near, far, columns = refs[:3]
        half = near.shape[1]
        for i in range(left_t.shape[0] // rows):

            @pl.when(step == i)
            def _():
                for dst, src, size in blocks:
                    if i * rows <= dst < (i + 1) * rows:
                        span = slice(dst - i * rows, dst - i * rows + size)
                        both = near[src : src + size, :] + far[src : src + size, :].astype(F32)
                        out_ref[span, cols : cols + half] = both.astype(BF16)
                        out_ref[span, cols + half :] = columns[src : src + size, :]


def grad_ff_kernel(blocks, ix, n3, n2, n1, n0, u3, u2, u10, a3, a2, a10, d3, d2, d1, d0, out_ref, nt, at_t, up, dy):
    step = pl.program_id(0)
    depth = n3.shape[0]

    @pl.when(step == 0)
    def _():
        for i, (n, d) in enumerate(((n3, d3), (n2, d2), (n1, d1), (n0, d0))):
            span = slice(i * depth, (i + 1) * depth)
            t = n[...].T
            for dst, src, size in blocks:
                nt[dst : dst + size, span] = t[src : src + size, :]
            dy[span, :] = d[...]
        for first, a, u in ((0, a3, u3), (1, a2, u2), (2, a10, u10)):
            span = slice(first * depth, first * depth + a.shape[0])
            at_t[:, span] = a[...].T
            up[span, :] = u[...]

    rows, units = out_ref.shape[0], up.shape[1]
    mine = at(step * rows, rows, 16)
    out_ref[:, :units] = dot(nt[mine, :], up[...], NN).astype(BF16)
    out_ref[:, units:] = dot(at_t[mine, :], dy[...], NN).astype(BF16)


def spread_kernel(ix, one, two, out_ref):
    odd = ix[2]
    out_ref[odd] = one[...].astype(F32)
    out_ref[1 - odd] = two[...].astype(F32)


def home_kernel(ix, summed, *parts):
    core, y = ix[1], ix[3]
    rows, cols = parts[0].shape
    for p in range(4):
        block = (core ^ (p & 1)) * 2 + (y ^ (p >> 1))
        parts[p][...] = summed[at(block * rows, rows, 8), 0:cols]


def settle_kernel(ix, p0, p1, p2, p3, qkv_ref, out_ref, vec_ref, tile):
    rank, core = ix[0], ix[1]
    parts = (p0, p1, p2, p3)
    rows, width = out_ref.shape
    quarter, half = width // 4, width // 2
    for p in range(4):
        a = rank ^ p
        for t in range(3):
            qkv_ref[:, at(t * width + a * quarter, quarter, 128)] = parts[p][:, t * quarter : (t + 1) * quarter].astype(F32)
    c1, c2 = 3 * quarter, 3 * quarter + half
    for p in range(2):
        out_ref[:, at((core ^ p) * half, half, 128)] = parts[p][:, c1:c2].astype(F32) + parts[p + 2][:, c1:c2].astype(F32)
    tile[...] = jnp.zeros_like(tile)
    tile[0:rows, :] = sum(v[:, c2:].astype(F32) for v in parts)
    vec_ref[...] = tile[...].T[0:8, :]


def settle_ff_kernel(spots, ix, p0, p1, p2, p3, up_ref):
    core, y = ix[1], ix[3]
    hid, zs = 128, len(spots) // 2
    for p, part in enumerate((p0, p1, p2, p3)):
        c2, y2 = core ^ (p & 1), y ^ (p >> 1)
        for b, (nx, nz) in enumerate(spots):
            dst = ((nx * 2 + c2) * zs + nz) * 2 + y2
            up_ref[:, at(dst * hid, hid, 128)] = part[:, b * hid : (b + 1) * hid].astype(F32)


class Places:
    def __init__(self, mesh):
        self.n_dp, self.n_fsdp = mesh.shape["dp"], mesh.shape["fsdp"]
        self.xs, self.zs = self.n_dp // 2, self.n_fsdp // 2
        self.nodes = self.xs * self.zs
        self.all = [
            (x, c, z, y) for x in range(self.xs) for c in range(2) for z in range(self.zs) for y in range(2)
        ]

    def lin(self, x, c, z, y):
        return (x * 2 + c) * self.n_fsdp + z * 2 + y

    def perm(self, move):
        return [(self.lin(*d), self.lin(*move(*d))) for d in self.all]

    def spot(self, x, z):
        return x * self.zs + (z if x % 2 == 0 else self.zs - 1 - z)

    def node(self, spot):
        x, z = spot // self.zs, spot % self.zs
        return (x, z if x % 2 == 0 else self.zs - 1 - z)

    def rings(self):
        return [
            [self.lin(x, c, z, y) for x, z in map(self.node, range(self.nodes))] for c in range(2) for y in range(2)
        ]


def permute(array, pairs):
    return lax.ppermute(array, AXES, pairs)


def after(value, *done):
    return lax.optimization_barrier((value,) + done)[0]


def body(pc, tokens, scene_ids, w_qkv, w_out, w_up, w_down, gain_one, bias_one, gain_two, bias_two, cotangent):
    micro, run, width = tokens.shape
    rows = w_qkv.shape[0]
    ff = w_up.shape[1]
    units = ff // 4
    hid = w_down.shape[0]
    quarter, half = width // 4, width // 2
    own = micro * run
    dp, fsdp = lax.axis_index("dp"), lax.axis_index("fsdp")
    x, core, z, y = dp // 2, dp % 2, fsdp // 2, fsdp % 2
    rank = y * 2 + core
    groups = micro * 2
    quads = pc.zs // groups
    rings = pc.rings()
    spots = [pc.node(i) for i in range(pc.nodes)]
    blocks = row_blocks(spots, 2 * rows)
    aligned = hid % 128 == 0

    p_core = pc.perm(lambda x, c, z, y: (x, 1 - c, z, y))
    p_y = pc.perm(lambda x, c, z, y: (x, c, z, 1 - y))
    p_diag = pc.perm(lambda x, c, z, y: (x, 1 - c, z, 1 - y))

    def place_perm(flip):
        def move(x, c, z, y):
            m = (z % 2) ^ flip
            return (x, (z // 2) % 2, (m * 2 + c) * quads + z // 4, y)

        return pc.perm(move)

    p_place = [place_perm(0), place_perm(1)]
    p_back = [[(b, a) for a, b in pairs] for pairs in p_place]

    def group_perm(by):
        return pc.perm(lambda x, c, z, y: (x, c, z // quads * quads + (z + by) % quads, y))

    ix = jnp.stack([rank, core, z % 2, y]).astype(jnp.int32)

    def quad_swap(parts):
        return [parts[0], permute(parts[1], p_core), permute(parts[2], p_y), permute(parts[3], p_diag)]

    def by_rank(parts):
        odd, top = rank % 2 == 1, rank // 2 == 1
        parts = [jnp.where(odd, parts[i ^ 1], parts[i]) for i in range(4)]
        return [jnp.where(top, parts[i ^ 2], parts[i]) for i in range(4)]

    def by_rows(parts):
        r = by_rank(parts)
        return jnp.concatenate([r[0], r[2], r[1], r[3]], 0)

    def ring_gather(shard):
        return lax.all_gather(shard, AXES, axis=0, tiled=True, axis_index_groups=rings)

    def ring_sum(terms):
        return lax.psum_scatter(terms, AXES, scatter_dimension=0, tiled=True, axis_index_groups=rings)

    c_out, c_small, wide = 3 * quarter, 3 * quarter + half, 3 * quarter + half + 128
    wu = w_up
    if not aligned:
        wu = w_up.reshape(rows, pc.xs, 2, pc.zs, 2, hid)
        wu = [
            lax.dynamic_slice(
                wu, (0, 0, core ^ (p & 1), 0, y ^ (p >> 1), 0), (rows, pc.xs, 1, pc.zs, 1, hid)
            ).reshape(rows, pc.xs, pc.zs, hid)
            for p in range(4)
        ]
        wu = jnp.concatenate([w[:, nx, nz] for w in wu for nx, nz in spots], 1)
    *packed, x_one, x_two, dy_one, dy_two = call(
        functools.partial(pack_kernel, aligned, spots),
        "pack",
        (
            ix,
            w_qkv,
            w_out,
            jnp.stack([gain_one, bias_one, gain_two, bias_two]),
            tokens,
            scene_ids.reshape(micro, run),
            cotangent,
            wu,
        ),
        [shape_of((rows, wide))] * 4 + [shape_of((rows, units))] * 4 + [shape_of((run + 8, width))] * 2 + [shape_of((run, width))] * 2,
        scratch=[pltpu.VMEM((128, 128), F32)],
        room=58,
    )
    shard = by_rows(quad_swap(packed[:4]))
    x_first = permute(x_one, p_place[0])
    x_own = jnp.concatenate([x_first, permute(x_two, p_place[1])], 0)
    first = ring_gather(after(shard, x_first))
    x_across = permute(x_own, p_y)
    taken = [x_own, permute(x_own, p_core), x_across, permute(x_across, p_core)]
    up_shard = by_rows(quad_swap(after(packed[4:], x_across)))
    second = ring_gather(after(jnp.concatenate([up_shard, w_down], 1), taken))
    dy_one, dy_two = after((dy_one, dy_two), first)
    dy_own = jnp.concatenate([permute(dy_one, p_place[0]), permute(dy_two, p_place[1])], 0)

    block = (own, width)
    n_one, projected, full_qkv, near_out, gains, qrow = call(
        functools.partial(project_kernel, blocks, run),
        "project",
        (ix, *taken, first),
        [
            shape_of((4 * own, width)),
            shape_of((4 * own, 3 * quarter)),
            shape_of((width, 3 * quarter)),
            shape_of((width, half)),
            shape_of((8, width), F32),
            shape_of((1, 4 * own), F32),
        ],
        scratch=[pltpu.VMEM((width, 128), F32)],
        grid=(4,),
        flops=2 * 4 * own * width * 3 * quarter,
        out_specs={
            0: pl.BlockSpec(block, lambda i: (i, 0)),
            1: pl.BlockSpec((own, 3 * quarter), lambda i: (i, 0)),
        },
    )
    far_out = permute(near_out, p_core)
    if quads == 1:
        q, k, v, krow = (projected, 0), (projected, 1), (projected, 2), qrow
    else:
        kv = projected[:, quarter:]
        kv_all = jnp.concatenate([kv] + [permute(kv, group_perm(s)) for s in range(1, quads)], 0)
        krow = jnp.concatenate([qrow] + [permute(qrow, group_perm(s)) for s in range(1, quads)], 1)
        q, k, v = (projected, 0), (kv_all, 0), (kv_all, 1)
    *m_far, lse_far = attend(ix, q, k, v, quarter, qrow, krow, 2)
    dy_across = permute(after(dy_own, m_far), p_y)
    *m_near, lse_near = attend(ix, q, k, v, quarter, after(qrow, m_far, dy_own), krow, 0)
    mixed = quad_swap([*m_near, *m_far])
    mixed_own, hidden, n_two = call(
        functools.partial(mix_out_kernel, run),
        "mix_out",
        (ix, *mixed, near_out, far_out, taken[0], gains),
        [shape_of(block), shape_of(block, F32), shape_of(block)],
        flops=2 * own * width * width,
    )
    def far_sum(keep, got):
        return (keep + got.astype(F32)).astype(BF16)

    n_across = permute(after(n_two, dy_across), p_y)
    norms = [n_two, permute(n_two, p_core), n_across, permute(n_across, p_core)]
    dys = [dy_own, permute(dy_own, p_core), dy_across, permute(dy_across, p_core)]

    def hidden_units(parts, weights, kinds, order):
        outs = [shape_of((len(parts) * own, units))] * 2 + [shape_of(block, kind) for kind in kinds * 2]
        return call(
            functools.partial(hidden_units_kernel, parts, order),
            "hidden_units",
            (ix, *[norms[p] for p in parts], *[dys[p] for p in parts], *weights),
            outs + ([shape_of((width, units)), shape_of((units, width))] if order else []),
            flops=8 * len(parts) * own * width * units,
            transcendentals=2 * len(parts) * own * units,
        )

    act3, up3, give3, r_give3, full_up, full_down = hidden_units((3,), (second,), (BF16,), blocks)
    got3 = permute(give3, p_core)
    act2, up2, keep2, r_keep2 = hidden_units((2,), (after(full_up, give3), full_down), (F32,), None)
    far = far_sum(keep2, got3)
    across = permute(far, p_y)
    act10, up10, give1, keep0, r_give1, r_keep0 = hidden_units((1, 0), (after(full_up, far), full_down), (BF16, F32), None)
    got = permute(give1, p_core)
    in_order = [(i, i, n) for i, _, n in blocks]

    def grads(name, lefts, rights, order, extra=()):
        widths = tuple(r[0].shape[1] for r in rights)
        depth, cols = sum(a.shape[0] for a in lefts), sum(widths)
        height = lefts[0].shape[1]
        total = cols + sum(e.shape[1] for e in extra[1:])
        return call(
            functools.partial(grads_kernel, order, len(lefts), widths, len(rights[0]), len(extra)),
            name,
            (ix, *lefts, *[piece for r in rights for piece in r], *extra),
            [shape_of((height, total))],
            scratch=[pltpu.VMEM((height, depth), BF16)] + [pltpu.VMEM((depth, w), BF16) for w in widths],
            grid=(4,),
            flops=2 * depth * height * cols,
            out_specs={0: pl.BlockSpec((height // 4, total), lambda i: (i, 0))},
        )[0]

    order = (3, 2, 1, 0)
    (ff_terms,) = call(
        functools.partial(grad_ff_kernel, blocks),
        "grad_ff",
        (ix, *[norms[p] for p in order], up3, up2, up10, act3, act2, act10, *[dys[p] for p in order]),
        [shape_of((width, units + width))],
        scratch=[pltpu.VMEM((width, 4 * own), BF16), pltpu.VMEM((units, 4 * own), BF16)]
        + [pltpu.VMEM((4 * own, units), BF16), pltpu.VMEM((4 * own, width), BF16)],
        grid=(4,),
        flops=2 * 4 * own * width * 2 * units,
        out_specs={0: pl.BlockSpec((width // 4, units + width), lambda i: (i, 0))},
    )
    ff_sum = ring_sum(ff_terms)
    up_sum, down_sum = ff_sum[:, :units], ff_sum[:, units:]
    *d_parts, d_hidden, d_low, sums_two = call(
        hidden_back_kernel,
        "hidden_back",
        (ix, keep0, got, across, hidden, dys[0], after(gains, ff_terms), near_out, far_out),
        [shape_of((own, quarter))] * 4 + [shape_of(block, F32), shape_of(block), shape_of((8, width), F32)],
        flops=2 * own * width * width,
    )
    d_mixed = quad_swap(d_parts)
    near_parts, far_parts = d_mixed[:2], d_mixed[2:]
    r_far = far_sum(r_keep2, permute(after(r_give3, d_parts[0]), p_core))
    r_across = permute(r_far, p_y)
    r_got = permute(after(r_give1, d_parts[0]), p_core)
    dq_near, kept = attend_back(ix, q, k, v, quarter, qrow, krow, lse_near, near_parts, 0, ())
    dq_far, dkv = attend_back(ix, q, k, v, quarter, qrow, krow, lse_far, far_parts, 2, (after(kept, r_far),))

    def placed(one, two):
        return [permute(one, p_back[0]), permute(two, p_back[1])]

    r_own = (after(hidden, dq_far) + r_keep0 + r_got.astype(F32) + r_across.astype(F32)).astype(BF16)
    n_rows = dkv.shape[0] // quads
    if quads > 1:
        total = dkv[:n_rows].astype(F32)
        for s in range(1, quads):
            total = total + permute(dkv[s * n_rows : (s + 1) * n_rows], group_perm(-s)).astype(F32)
        dkv = total.astype(BF16)

    keep_one, give_one, columns = call(
        functools.partial(project_back_kernel, run),
        "project_back",
        (ix, *taken, dq_near, dq_far, dkv, full_qkv, after(sums_two, r_own)),
        [shape_of((2 * own, width), F32), shape_of((2 * own, width)), shape_of((width, 128))],
        scratch=[pltpu.VMEM((128, width), F32)],
        grid=(4,),
        flops=2 * 4 * own * width * 3 * quarter,
        in_specs={
            6: pl.BlockSpec((own, 2 * quarter), lambda i: (jnp.where(i == 0, 1, jnp.where(i == 1, 3, (i - 2) * 2)), 0)),
        },
    )
    got_one = permute(give_one, p_core)
    grad_near, grad_far = call(
        out_grad_kernel,
        "out_grad",
        (ix, after(mixed_own, give_one), d_low),
        [shape_of((width, half), F32), shape_of((width, half))],
        flops=2 * own * width * width,
    )
    far_one = far_sum(keep_one[own:], after(got_one, grad_near)[own:])
    across_one = permute(far_one, p_y)
    at_terms = grads(
        "grad_at",
        [after(n_one, far_one)],
        [[jnp.concatenate([dq_near, dq_far], 0)], [dkv]],
        blocks,
        (grad_near, permute(grad_far, p_core), columns),
    )
    one_sum = ring_sum(after(at_terms, ff_sum))
    back_out = placed(*after((r_own[:run], r_own[run:]), at_terms))

    def home(name, summed):
        return quad_swap(call(home_kernel, name, (ix, summed), [shape_of((rows, summed.shape[1]))] * 4))

    def in_batches(one, two):
        return jnp.stack([jnp.where(z % 2 == 0, one, two), jnp.where(z % 2 == 0, two, one)], 0)

    d_one, d_two = call(
        functools.partial(tokens_back_kernel, run),
        "tokens_back",
        (ix, keep_one, got_one, across_one, taken[0], d_hidden, after(gains, ff_sum, back_out)),
        [shape_of((run, width))] * 2,
    )
    ff_home = home("home_up", after(up_sum, d_one))
    own_down = down_sum.astype(F32)
    if aligned:
        (own_up,) = call(
            functools.partial(settle_ff_kernel, spots), "settle_ff", (ix, *ff_home), [shape_of((rows, 4 * units), F32)])
    else:
        ups = [b.reshape(rows, pc.nodes, hid) for b in ff_home]
        at_spot = [[spots.index((nx, nz)) for nz in range(pc.zs)] for nx in range(pc.xs)]
        ups = by_rank([jnp.stack([jnp.stack([b[:, i] for i in row], 1) for row in at_spot], 1) for b in ups])
        own_up = (
            jnp.stack([jnp.stack([ups[0], ups[2]], 3), jnp.stack([ups[1], ups[3]], 3)], 2)
            .reshape(rows, 4 * units)
            .astype(F32)
        )
    back_grad = placed(*after((d_one, d_two), own_up))
    at_home = home("home_at", after(one_sum, back_out))
    output = in_batches(*after(back_out, d_one))
    own_qkv, own_out, vectors = call(
        settle_kernel,
        "settle",
        (ix, *at_home),
        [shape_of((rows, 3 * width), F32), shape_of((rows, width), F32), shape_of((8, 128), F32)],
        scratch=[pltpu.VMEM((128, 128), F32)],
    )
    (input_grad,) = call(
        spread_kernel, "spread", (ix, *after(back_grad, own_qkv)), [shape_of((micro, run, width), F32)]
    )
    return (output, input_grad, own_qkv, own_out, own_up, own_down) + tuple(vectors[i, :rows] for i in range(4))


def solution(mesh):
    vector, matrix, batch = P(AXES), P(AXES, None), P(None, AXES, None)
    return jax.shard_map(
        functools.partial(body, Places(mesh)),
        mesh=mesh,
        in_specs=(batch, P(None, "dp", "fsdp")) + (matrix,) * 4 + (vector,) * 4 + (batch,),
        out_specs=(batch, batch) + (matrix,) * 4 + (vector,) * 4,
        check_vma=False,
    )
```

```python
import functools
import math

import jax
import jax.numpy as jnp
from jax import lax
from jax.experimental import pallas as pl
from jax.experimental.pallas import tpu as pltpu
from jax.sharding import PartitionSpec as P

AXES = ("dp", "fsdp")
HEAD_DIM = 64
EPS = 1e-05
LOWEST = -1000000000.0
F32 = jnp.float32
BF16 = jnp.bfloat16
NT = (((1,), (1,)), ((), ()))
TN = (((0,), (0,)), ((), ()))
NN = (((1,), (0,)), ((), ()))
ROOM = 20
IN_HBM = ("grad_ff", "grad_at")
HINTS = {"home_at": 1000, "settle": 8, "mix_out": 0, "grad_ff": 3, "hidden_units": 8, "hidden_back": 300, "attend_back": 4, "grad_down": 0, "home_up": 0, "settle_ff": 0, "out_grad": 0, "project_back": 0, "grad_at": 0, "tokens_back": 0, "down": 8}


def dot(left, right, dims):
    return lax.dot_general(left, right, dims, preferred_element_type=F32)


def at(start, size, step):
    return pl.ds(pl.multiple_of(start, step), size)


def call(kernel, name, args, outs, scratch=(), grid=None, flops=0, transcendentals=0, in_specs=None, out_specs=None, room=ROOM):
    whole = pl.BlockSpec(memory_space=pltpu.VMEM) if grid is None else None

    def spec(shape):
        return whole or pl.BlockSpec(shape, lambda i, n=len(shape): (0,) * n)

    specs = [pl.BlockSpec(memory_space=pltpu.SMEM)]
    specs += [(in_specs or {}).get(n) or spec(a.shape) for n, a in enumerate(args[1:])]
    size = sum(math.prod(a.shape) * a.dtype.itemsize for a in list(args) + list(outs))
    return pl.pallas_call(
        kernel,
        out_shape=tuple(pltpu.HBM(o.shape, o.dtype) for o in outs) if name in IN_HBM else tuple(outs),
        in_specs=specs,
        out_specs=tuple((out_specs or {}).get(n) or spec(o.shape) for n, o in enumerate(outs)),
        scratch_shapes=list(scratch),
        compiler_params=pltpu.CompilerParams(vmem_limit_bytes=min(room, 58) * 1024 * 1024),
        cost_estimate=pl.CostEstimate(
            flops=HINTS.get(name, 8) * flops, bytes_accessed=HINTS.get(name, 8) * size, transcendentals=transcendentals
        ),
        name=name,
        **({} if grid is None else {"grid": grid}),
    )(*args)


def shape_of(shape, dtype=BF16):
    return jax.ShapeDtypeStruct(shape, dtype)


def centre(v):
    c = v - jnp.mean(v, axis=-1, keepdims=True)
    inv = lax.rsqrt(jnp.mean(c * c, axis=-1, keepdims=True) + EPS)
    return c * inv, inv


def norm_back(d_norm, std, inv, gain):
    d_std = d_norm * gain
    return inv * (
        d_std - jnp.mean(d_std, axis=-1, keepdims=True) - std * jnp.mean(d_std * std, axis=-1, keepdims=True)
    )


def pack_kernel(aligned, spots, ix, qkv, out, g0, g1, g2, g3, tokens, scenes, dy, up, *refs):
    parts, ups, (one, two, dy_one, dy_two, tile) = refs[:4], refs[4:8], refs[8:]
    rank, core, odd, y = ix[0], ix[1], ix[2], ix[3]
    rows, width = qkv.shape[0], out.shape[1]
    quarter, half = width // 4, width // 2
    tile[...] = jnp.zeros_like(tile)
    for i, g in enumerate((g0, g1, g2, g3)):
        tile[i : i + 1, 0:rows] = g[...].astype(F32)
    small = tile[...].T[:rows].astype(BF16)
    c1, c2 = 3 * quarter, 3 * quarter + half
    hid, units = 128, up.shape[1] // 4
    zs = len(spots) // 2
    for p in range(4):
        a = rank ^ p
        for t in range(3):
            parts[p][:, t * quarter : (t + 1) * quarter] = qkv[:, at(t * width + a * quarter, quarter, 128)]
        parts[p][:, c1:c2] = out[:, at((core ^ (p & 1)) * half, half, 128)]
        parts[p][:, c2 : c2 + 128] = small
        if aligned:
            for b, (nx, nz) in enumerate(spots):
                src = ((nx * 2 + (core ^ (p & 1))) * zs + nz) * 2 + (y ^ (p >> 1))
                ups[p][:, b * hid : (b + 1) * hid] = up[:, at(src * hid, hid, 128)]
        else:
            ups[p][...] = up[:, p * units : (p + 1) * units]
    run = tokens.shape[1]
    for ref, low, m in ((one, dy_one, odd), (two, dy_two, 1 - odd)):
        ref[0:run, :] = tokens[m]
        ref[run:, :] = jnp.zeros((ref.shape[0] - run, width), BF16)
        ref[run : run + 1, 0:run] = scenes[pl.ds(m, 1), :].astype(F32).astype(BF16)
        low[...] = dy[m]


def row_blocks(spots, size):
    zs = len(spots) // 2
    return [
        ((2 * i + c) * size, ((nx * 2 + c) * zs + nz) * size, size) for i, (nx, nz) in enumerate(spots) for c in (0, 1)
    ]


def project_kernel(blocks, run, ix, *refs):
    taken, first = refs[:4], refs[4]
    n_ref, p_ref, w_ref, near_ref, gains_ref, scene_ref, g_all = refs[5:]
    step = pl.program_id(0)
    c_out, c_small = w_ref.shape[1], w_ref.shape[1] + near_ref.shape[1]

    @pl.when(step == 0)
    def _():
        for src, dst, size in blocks:
            v = first[src : src + size, :]
            w_ref[dst : dst + size, :] = v[:, :c_out]
            near_ref[dst : dst + size, :] = v[:, c_out:c_small]
            g_all[dst : dst + size, :] = v[:, c_small:].astype(F32)
        gains_ref[...] = g_all[...].T[0:8, :]
        for p in range(4):
            for s in range(2):
                row = taken[p][s * (run + 8) + run : s * (run + 8) + run + 1, 0:run]
                scene_ref[0:1, (2 * p + s) * run : (2 * p + s + 1) * run] = row.astype(F32)

    for p in range(4):

        @pl.when(step == p)
        def _():
            x = taken[p]
            v = jnp.concatenate([x[0:run, :], x[run + 8 : 2 * run + 8, :]], 0).astype(F32)
            std, _ = centre(v)
            n = (std * gains_ref[0:1, :] + gains_ref[1:2, :]).astype(BF16)
            n_ref[...] = n
            p_ref[...] = dot(n, w_ref[...], NN).astype(BF16)


def head_lanes(rows, width, head):
    lane = lax.broadcasted_iota(jnp.int32, (rows, width), 1)
    return (lane >= head * HEAD_DIM) & (lane < (head + 1) * HEAD_DIM)


def column(row):
    return jnp.broadcast_to(row, (128, row.shape[1])).T


def same_scene(ksc, qrow):
    return jnp.concatenate([ksc == qrow[:, i : i + 128] for i in range(0, qrow.shape[1], 128)], 1)


def attend_kernel(heads, ix, krow_ref, qrow_ref, q_ref, k_ref, v_ref, *refs):
    outs_ref, (lse_ref, vt_ref, ksc_ref) = refs[:2], refs[2:]
    step = pl.program_id(0)

    @pl.when(step == 0)
    def _():
        vt_ref[...] = v_ref[...].astype(F32).T.astype(BF16)
        ksc_ref[...] = column(krow_ref[...])

    rows, width = q_ref.shape
    same = same_scene(ksc_ref[...], qrow_ref[...])
    q = q_ref[...].astype(F32) * (1.0 / math.sqrt(HEAD_DIM))
    outs = []
    for h in range(heads):
        qh = jnp.where(head_lanes(rows, width, h), q, 0.0).astype(BF16)
        s = jnp.where(same, dot(k_ref[...], qh, NT), LOWEST)
        peak = jnp.max(s, axis=0, keepdims=True)
        e = jnp.exp(s - peak)
        total = jnp.sum(e, axis=0, keepdims=True)
        lse_ref[h : h + 1, :] = peak + jnp.log(total)
        p = (e * (1.0 / total)).astype(BF16)
        outs.append(dot(vt_ref[h * HEAD_DIM : (h + 1) * HEAD_DIM, :], p, NN))
    mixed = jnp.concatenate(outs, axis=0).T.astype(BF16)
    for i in range(2):

        @pl.when(step == i)
        def _():
            outs_ref[i][...] = mixed


def attend(ix, q, k, v, quarter, qrow, krow, first):
    rows, keys = q[0].shape[0], k[0].shape[0]
    heads, block = quarter // HEAD_DIM, rows // 4
    return call(
        functools.partial(attend_kernel, heads),
        "attend",
        (ix, krow, qrow, q[0], k[0], v[0]),
        [shape_of((block, quarter))] * 2 + [shape_of((heads, 2 * block), F32)],
        scratch=[pltpu.VMEM((quarter, keys), BF16), pltpu.VMEM((keys, 128), F32)],
        grid=(2,),
        room=ROOM * keys // rows,
        flops=2 * rows * keys * quarter,
        transcendentals=rows * keys * heads // 2,
        in_specs={
            1: pl.BlockSpec((1, block), lambda i: (0, i + first)),
            2: pl.BlockSpec((block, quarter), lambda i, c=q[1]: (i + first, c)),
            3: pl.BlockSpec((keys, quarter), lambda i, c=k[1]: (0, c)),
            4: pl.BlockSpec((keys, quarter), lambda i, c=v[1]: (0, c)),
        },
        out_specs={2: pl.BlockSpec((heads, block), lambda i: (0, i))},
    )


def attend_back_kernel(heads, more, ix, krow_ref, qrow_ref, lse_ref, q_ref, k_ref, v_ref, *refs):
    do_refs, kept, refs = refs[:2], refs[2 : 2 + more], refs[2 + more :]
    dq_ref, dkv_ref, kt_ref, ksc_ref, dka_ref, dva_ref, do_ref = refs
    width = q_ref.shape[1]
    step = pl.program_id(0)

    @pl.when(step == 0)
    def _():
        kt_ref[...] = k_ref[...].astype(F32).T.astype(BF16)
        ksc_ref[...] = column(krow_ref[...])
        if more:
            dka_ref[...] = kept[0][:, :width]
            dva_ref[...] = kept[0][:, width:]
        else:
            dka_ref[...] = jnp.zeros_like(dka_ref)
            dva_ref[...] = jnp.zeros_like(dva_ref)

    for i in range(2):

        @pl.when(step == i)
        def _():
            do_ref[...] = do_refs[i][...].astype(F32)

    rows, width = q_ref.shape
    scale = 1.0 / math.sqrt(HEAD_DIM)
    same = same_scene(ksc_ref[...], qrow_ref[...])
    q = q_ref[...].astype(F32) * scale
    do = do_ref[...]
    outs = []
    for h in range(heads):
        mine = head_lanes(rows, width, h)
        qh = jnp.where(mine, q, 0.0).astype(BF16)
        doh = jnp.where(mine, do, 0.0).astype(BF16)
        s = jnp.where(same, dot(k_ref[...], qh, NT), LOWEST)
        p = jnp.exp(s - lse_ref[h : h + 1, :])
        dp = dot(v_ref[...], doh, NT)
        inner = jnp.sum(p * dp, axis=0, keepdims=True)
        ds = (p * (dp - inner)).astype(BF16)
        dva_ref[...] += dot(p.astype(BF16), doh, NN)
        dka_ref[...] += dot(ds, qh, NN)
        outs.append(dot(kt_ref[h * HEAD_DIM : (h + 1) * HEAD_DIM, :], ds, NN))
    dq_ref[...] = (jnp.concatenate(outs, axis=0).T * scale).astype(BF16)

    @pl.when(step == pl.num_programs(0) - 1)
    def _():
        dkv_ref[:, :width] = dka_ref[...].astype(dkv_ref.dtype)
        dkv_ref[:, width:] = dva_ref[...].astype(dkv_ref.dtype)


def attend_back(ix, q, k, v, quarter, qrow, krow, lse, do, first, kept):
    rows, keys = q[0].shape[0], k[0].shape[0]
    heads, block = quarter // HEAD_DIM, rows // 4
    return call(
        functools.partial(attend_back_kernel, heads, len(kept)),
        "attend_back",
        (ix, krow, qrow, lse, q[0], k[0], v[0], *do, *kept),
        [shape_of((2 * block, quarter)), shape_of((keys, 2 * quarter), BF16 if kept else F32)],
        scratch=[
            pltpu.VMEM((quarter, keys), BF16),
            pltpu.VMEM((keys, 128), F32),
            pltpu.VMEM((keys, quarter), F32),
            pltpu.VMEM((keys, quarter), F32),
            pltpu.VMEM((block, quarter), F32),
        ],
        grid=(2,),
        room=ROOM * keys // rows,
        flops=5 * rows * keys * quarter,
        transcendentals=rows * keys * heads // 2,
        in_specs={
            1: pl.BlockSpec((1, block), lambda i: (0, i + first)),
            2: pl.BlockSpec((heads, block), lambda i: (0, i)),
            3: pl.BlockSpec((block, quarter), lambda i, c=q[1]: (i + first, c)),
            4: pl.BlockSpec((keys, quarter), lambda i, c=k[1]: (0, c)),
            5: pl.BlockSpec((keys, quarter), lambda i, c=v[1]: (0, c)),
        },
        out_specs={0: pl.BlockSpec((block, quarter), lambda i: (i, 0))},
    )


def mix_out_kernel(run, ix, m0, m1, m2, m3, near, far, x, gains, mixed_ref, hidden_ref, n_ref):
    rank, core = ix[0], ix[1]
    quarter, half = m0.shape[1], near.shape[1]
    for p, m in enumerate((m0, m1, m2, m3)):
        mixed_ref[:, at((rank ^ p) * quarter, quarter, 128)] = m[...]
    mixed = mixed_ref[...]
    hidden_ref[0:run, :] = x[0:run, :].astype(F32)
    hidden_ref[run:, :] = x[run + 8 : 2 * run + 8, :].astype(F32)
    hidden_ref[:, at(core * half, half, 128)] += dot(mixed, near[...], NN)
    hidden_ref[:, at((1 - core) * half, half, 128)] += dot(mixed, far[...], NN)
    std, _ = centre(hidden_ref[...])
    n_ref[...] = (std * gains[2:3, :] + gains[3:4, :]).astype(BF16)


def hidden_units_kernel(parts, blocks, ix, *refs):
    n, rows = len(parts), refs[0].shape[0]
    norms, dys, refs = refs[:n], refs[n : 2 * n], refs[2 * n :]
    if blocks:
        second, act_ref, dup_ref, *term_refs, up_ref, down_ref = refs
        units = up_ref.shape[1]
        for src, dst, size in blocks:
            up_ref[dst : dst + size, :] = second[src : src + size, :units]
        down_ref[...] = second[:, units:]
    else:
        up_ref, down_ref, act_ref, dup_ref, *term_refs = refs
    for i in range(n):
        span = slice(i * rows, (i + 1) * rows)
        u = dot(norms[i][...], up_ref[...], NN)
        cdf = 0.5 * (1.0 + lax.erf(u * math.sqrt(0.5)))
        act = (u * cdf).astype(BF16)
        act_ref[span, :] = act
        term_refs[n + i][...] = dot(act, down_ref[...], NN).astype(term_refs[n + i].dtype)
        slope = cdf + u * jnp.exp(-0.5 * u * u) * (1.0 / math.sqrt(2.0 * math.pi))
        dup = (dot(dys[i][...], down_ref[...], NT) * slope).astype(BF16)
        dup_ref[span, :] = dup
        term_refs[i][...] = dot(dup, up_ref[...], NT).astype(term_refs[i].dtype)


def hidden_back_kernel(ix, keep, got, across, hidden, dy, gains, near, far, *refs):
    parts, (dh_ref, low_ref, sums_ref) = refs[:4], refs[4:]
    rank, core = ix[0], ix[1]
    rows = hidden.shape[0]
    half, quarter = near.shape[1], parts[0].shape[1]
    d_norm = keep[...] + got[...].astype(F32) + across[...].astype(F32)
    std, inv = centre(hidden[...])
    sums_ref[...] = jnp.zeros_like(sums_ref)
    sums_ref[2:3, :] = jnp.sum(d_norm * std, axis=0, keepdims=True)
    sums_ref[3:4, :] = jnp.sum(d_norm, axis=0, keepdims=True)
    d_hidden = dy[...].astype(F32) + norm_back(d_norm, std, inv, gains[2:3, :])
    dh_ref[...] = d_hidden
    low_ref[...] = d_hidden.astype(BF16)
    a, b = low_ref[:, at(core * half, half, 128)], low_ref[:, at((1 - core) * half, half, 128)]
    for p in range(4):
        rows_p = at((rank ^ p) * quarter, quarter, 16)
        parts[p][...] = (dot(a, near[rows_p, :], NT) + dot(b, far[rows_p, :], NT)).astype(BF16)


def out_grad_kernel(ix, mixed, low, near_ref, far_ref):
    core, half = ix[1], near_ref.shape[1]
    left = mixed[...].astype(F32).T.astype(BF16)
    near_ref[...] = dot(left, low[:, at(core * half, half, 128)], NN)
    far_ref[...] = dot(left, low[:, at((1 - core) * half, half, 128)], NN).astype(BF16)


def project_back_kernel(run, ix, *refs):
    taken, (dq_a, dq_b, dkv, w, sums2, keep_ref, give_ref, cols_ref, sums) = refs[:4], refs[4:]
    step = pl.program_id(0)
    quarter, rows = dq_a.shape[1], dkv.shape[0]

    @pl.when(step == 0)
    def _():
        sums[...] = jnp.zeros_like(sums)
        sums[0:8, :] = sums2[...]

    for i, p in enumerate((1, 3, 0, 2)):

        @pl.when(step == i)
        def _():
            x = taken[p]
            std, _ = centre(jnp.concatenate([x[0:run, :], x[run + 8 : 2 * run + 8, :]], 0).astype(F32))
            dq = (dq_a, dq_b)[p >> 1][(p & 1) * rows : ((p & 1) + 1) * rows, :]
            part = dot(dq, w[:, 0:quarter], NT) + dot(dkv[...], w[:, quarter:], NT)
            sums[0:1, :] += jnp.sum(part * std, axis=0, keepdims=True)
            sums[1:2, :] += jnp.sum(part, axis=0, keepdims=True)
            if p & 1:
                give_ref[(p >> 1) * rows : ((p >> 1) + 1) * rows, :] = part.astype(BF16)
            else:
                keep_ref[(p >> 1) * rows : ((p >> 1) + 1) * rows, :] = part

    @pl.when(step == 3)
    def _():
        cols_ref[...] = sums[...].T.astype(BF16)


def tokens_back_kernel(run, ix, keep, got, across, x, d_hidden, gains, one_ref, two_ref):
    rows = d_hidden.shape[0]
    d_norm = keep[0:rows, :] + got[0:rows, :].astype(F32) + across[...].astype(F32)
    std, inv = centre(jnp.concatenate([x[0:run, :], x[run + 8 : 2 * run + 8, :]], 0).astype(F32))
    d = (d_hidden[...] + norm_back(d_norm, std, inv, gains[0:1, :])).astype(BF16)
    one_ref[...] = d[0:run]
    two_ref[...] = d[run:]


def grads_kernel(blocks, n_left, widths, n_right, extra, ix, *refs):
    lefts, refs = refs[:n_left], refs[n_left:]
    rights, refs = [refs[i * n_right : (i + 1) * n_right] for i in range(len(widths))], refs[len(widths) * n_right :]
    out_ref, left_t, *right_refs = refs[extra:]
    step = pl.program_id(0)
    cols = sum(widths)

    @pl.when(step == 0)
    def _():
        at_col = 0
        for piece in lefts:
            t = piece[...].T
            stop = at_col + t.shape[1]
            for dst, src, size in blocks:
                left_t[dst : dst + size, at_col:stop] = t[src : src + size, :]
            at_col = stop
        for pieces, ref in zip(rights, right_refs):
            row = 0
            for piece in pieces:
                ref[row : row + piece.shape[0], :] = piece[...]
                row += piece.shape[0]

    rows = out_ref.shape[0]
    mine = left_t[at(step * rows, rows, 16), :]
    start = 0
    for ref, w in zip(right_refs, widths):
        out_ref[:, start : start + w] = dot(mine, ref[...], NN).astype(BF16)
        start += w
    if extra:
        near, far, columns = refs[:3]
        half = near.shape[1]
        for i in range(left_t.shape[0] // rows):

            @pl.when(step == i)
            def _():
                for dst, src, size in blocks:
                    if i * rows <= dst < (i + 1) * rows:
                        span = slice(dst - i * rows, dst - i * rows + size)
                        both = near[src : src + size, :] + far[src : src + size, :].astype(F32)
                        out_ref[span, cols : cols + half] = both.astype(BF16)
                        out_ref[span, cols + half :] = columns[src : src + size, :]


def grad_ff_kernel(blocks, ix, n3, n2, n1, n0, u3, u2, u10, a3, a2, a10, d3, d2, d1, d0, out_ref, nt, at_t, up, dy):
    step = pl.program_id(0)
    depth = n3.shape[0]

    @pl.when(step == 0)
    def _():
        for i, (n, d) in enumerate(((n3, d3), (n2, d2), (n1, d1), (n0, d0))):
            span = slice(i * depth, (i + 1) * depth)
            t = n[...].T
            for dst, src, size in blocks:
                nt[dst : dst + size, span] = t[src : src + size, :]
            dy[span, :] = d[...]
        for first, a, u in ((0, a3, u3), (1, a2, u2), (2, a10, u10)):
            span = slice(first * depth, first * depth + a.shape[0])
            at_t[:, span] = a[...].T
            up[span, :] = u[...]

    rows, units = out_ref.shape[0], up.shape[1]
    mine = at(step * rows, rows, 16)
    out_ref[:, :units] = dot(nt[mine, :], up[...], NN).astype(BF16)
    out_ref[:, units:] = dot(at_t[mine, :], dy[...], NN).astype(BF16)


def spread_kernel(ix, one, two, out_ref):
    odd = ix[2]
    out_ref[odd] = one[...].astype(F32)
    out_ref[1 - odd] = two[...].astype(F32)


def home_kernel(ix, summed, *parts):
    core, y = ix[1], ix[3]
    rows, cols = parts[0].shape
    for p in range(4):
        block = (core ^ (p & 1)) * 2 + (y ^ (p >> 1))
        parts[p][...] = summed[at(block * rows, rows, 8), 0:cols]


def settle_kernel(ix, p0, p1, p2, p3, qkv_ref, out_ref, vec_ref, tile):
    rank, core = ix[0], ix[1]
    parts = (p0, p1, p2, p3)
    rows, width = out_ref.shape
    quarter, half = width // 4, width // 2
    for p in range(4):
        a = rank ^ p
        for t in range(3):
            qkv_ref[:, at(t * width + a * quarter, quarter, 128)] = parts[p][:, t * quarter : (t + 1) * quarter].astype(F32)
    c1, c2 = 3 * quarter, 3 * quarter + half
    for p in range(2):
        out_ref[:, at((core ^ p) * half, half, 128)] = parts[p][:, c1:c2].astype(F32) + parts[p + 2][:, c1:c2].astype(F32)
    tile[...] = jnp.zeros_like(tile)
    tile[0:rows, :] = sum(v[:, c2:].astype(F32) for v in parts)
    vec_ref[...] = tile[...].T[0:8, :]


def settle_ff_kernel(spots, ix, p0, p1, p2, p3, up_ref):
    core, y = ix[1], ix[3]
    hid, zs = 128, len(spots) // 2
    for p, part in enumerate((p0, p1, p2, p3)):
        c2, y2 = core ^ (p & 1), y ^ (p >> 1)
        for b, (nx, nz) in enumerate(spots):
            dst = ((nx * 2 + c2) * zs + nz) * 2 + y2
            up_ref[:, at(dst * hid, hid, 128)] = part[:, b * hid : (b + 1) * hid].astype(F32)


class Places:
    def __init__(self, mesh):
        self.n_dp, self.n_fsdp = mesh.shape["dp"], mesh.shape["fsdp"]
        self.xs, self.zs = self.n_dp // 2, self.n_fsdp // 2
        self.nodes = self.xs * self.zs
        self.all = [
            (x, c, z, y) for x in range(self.xs) for c in range(2) for z in range(self.zs) for y in range(2)
        ]

    def lin(self, x, c, z, y):
        return (x * 2 + c) * self.n_fsdp + z * 2 + y

    def perm(self, move):
        return [(self.lin(*d), self.lin(*move(*d))) for d in self.all]

    def spot(self, x, z):
        return x * self.zs + (z if x % 2 == 0 else self.zs - 1 - z)

    def node(self, spot):
        x, z = spot // self.zs, spot % self.zs
        return (x, z if x % 2 == 0 else self.zs - 1 - z)

    def rings(self):
        return [
            [self.lin(x, c, z, y) for x, z in map(self.node, range(self.nodes))] for c in range(2) for y in range(2)
        ]


def permute(array, pairs):
    return lax.ppermute(array, AXES, pairs)


def after(value, *done):
    return lax.optimization_barrier((value,) + done)[0]


def body(pc, tokens, scene_ids, w_qkv, w_out, w_up, w_down, gain_one, bias_one, gain_two, bias_two, cotangent):
    micro, run, width = tokens.shape
    rows = w_qkv.shape[0]
    ff = w_up.shape[1]
    units = ff // 4
    hid = w_down.shape[0]
    quarter, half = width // 4, width // 2
    own = micro * run
    dp, fsdp = lax.axis_index("dp"), lax.axis_index("fsdp")
    x, core, z, y = dp // 2, dp % 2, fsdp // 2, fsdp % 2
    rank = y * 2 + core
    groups = micro * 2
    quads = pc.zs // groups
    rings = pc.rings()
    spots = [pc.node(i) for i in range(pc.nodes)]
    blocks = row_blocks(spots, 2 * rows)
    aligned = hid % 128 == 0

    p_core = pc.perm(lambda x, c, z, y: (x, 1 - c, z, y))
    p_y = pc.perm(lambda x, c, z, y: (x, c, z, 1 - y))
    p_diag = pc.perm(lambda x, c, z, y: (x, 1 - c, z, 1 - y))

    def place_perm(flip):
        def move(x, c, z, y):
            m = (z % 2) ^ flip
            return (x, (z // 2) % 2, (m * 2 + c) * quads + z // 4, y)

        return pc.perm(move)

    p_place = [place_perm(0), place_perm(1)]
    p_back = [[(b, a) for a, b in pairs] for pairs in p_place]

    def group_perm(by):
        return pc.perm(lambda x, c, z, y: (x, c, z // quads * quads + (z + by) % quads, y))

    ix = jnp.stack([rank, core, z % 2, y]).astype(jnp.int32)

    def quad_swap(parts):
        return [parts[0], permute(parts[1], p_core), permute(parts[2], p_y), permute(parts[3], p_diag)]

    def by_rank(parts):
        odd, top = rank % 2 == 1, rank // 2 == 1
        parts = [jnp.where(odd, parts[i ^ 1], parts[i]) for i in range(4)]
        return [jnp.where(top, parts[i ^ 2], parts[i]) for i in range(4)]

    def by_rows(parts):
        r = by_rank(parts)
        return jnp.concatenate([r[0], r[2], r[1], r[3]], 0)

    def ring_gather(shard):
        return lax.all_gather(shard, AXES, axis=0, tiled=True, axis_index_groups=rings)

    def ring_sum(terms):
        return lax.psum_scatter(terms, AXES, scatter_dimension=0, tiled=True, axis_index_groups=rings)

    c_out, c_small, wide = 3 * quarter, 3 * quarter + half, 3 * quarter + half + 128
    wu = w_up
    if not aligned:
        wu = w_up.reshape(rows, pc.xs, 2, pc.zs, 2, hid)
        wu = [
            lax.dynamic_slice(
                wu, (0, 0, core ^ (p & 1), 0, y ^ (p >> 1), 0), (rows, pc.xs, 1, pc.zs, 1, hid)
            ).reshape(rows, pc.xs, pc.zs, hid)
            for p in range(4)
        ]
        wu = jnp.concatenate([w[:, nx, nz] for w in wu for nx, nz in spots], 1)
    *packed, x_one, x_two, dy_one, dy_two = call(
        functools.partial(pack_kernel, aligned, spots),
        "pack",
        (
            ix,
            w_qkv,
            w_out,
            *[g.reshape(1, rows) for g in (gain_one, bias_one, gain_two, bias_two)],
            tokens,
            scene_ids.reshape(micro, run),
            cotangent,
            wu,
        ),
        [shape_of((rows, wide))] * 4 + [shape_of((rows, units))] * 4 + [shape_of((run + 8, width))] * 2 + [shape_of((run, width))] * 2,
        scratch=[pltpu.VMEM((128, 128), F32)],
        room=58,
    )
    shard = by_rows(quad_swap(packed[:4]))
    x_first = permute(x_one, p_place[0])
    x_own = jnp.concatenate([x_first, permute(x_two, p_place[1])], 0)
    first = ring_gather(after(shard, x_first))
    x_across = permute(x_own, p_y)
    taken = [x_own, permute(x_own, p_core), x_across, permute(x_across, p_core)]
    up_shard = by_rows(quad_swap(after(packed[4:], x_across)))
    second = ring_gather(after(jnp.concatenate([up_shard, w_down], 1), taken))
    dy_one, dy_two = after((dy_one, dy_two), first)
    dy_own = jnp.concatenate([permute(dy_one, p_place[0]), permute(dy_two, p_place[1])], 0)

    block = (own, width)
    n_one, projected, full_qkv, near_out, gains, qrow = call(
        functools.partial(project_kernel, blocks, run),
        "project",
        (ix, *taken, first),
        [
            shape_of((4 * own, width)),
            shape_of((4 * own, 3 * quarter)),
            shape_of((width, 3 * quarter)),
            shape_of((width, half)),
            shape_of((8, width), F32),
            shape_of((1, 4 * own), F32),
        ],
        scratch=[pltpu.VMEM((width, 128), F32)],
        grid=(4,),
        flops=2 * 4 * own * width * 3 * quarter,
        out_specs={
            0: pl.BlockSpec(block, lambda i: (i, 0)),
            1: pl.BlockSpec((own, 3 * quarter), lambda i: (i, 0)),
        },
    )
    far_out = permute(near_out, p_core)
    if quads == 1:
        q, k, v, krow = (projected, 0), (projected, 1), (projected, 2), qrow
    else:
        kv = projected[:, quarter:]
        kv_all = jnp.concatenate([kv] + [permute(kv, group_perm(s)) for s in range(1, quads)], 0)
        krow = jnp.concatenate([qrow] + [permute(qrow, group_perm(s)) for s in range(1, quads)], 1)
        q, k, v = (projected, 0), (kv_all, 0), (kv_all, 1)
    *m_far, lse_far = attend(ix, q, k, v, quarter, qrow, krow, 2)
    dy_across = permute(after(dy_own, m_far), p_y)
    *m_near, lse_near = attend(ix, q, k, v, quarter, after(qrow, m_far, dy_own), krow, 0)
    mixed = quad_swap([*m_near, *m_far])
    mixed_own, hidden, n_two = call(
        functools.partial(mix_out_kernel, run),
        "mix_out",
        (ix, *mixed, near_out, far_out, taken[0], gains),
        [shape_of(block), shape_of(block, F32), shape_of(block)],
        flops=2 * own * width * width,
    )
    def far_sum(keep, got):
        return (keep + got.astype(F32)).astype(BF16)

    n_across = permute(after(n_two, dy_across), p_y)
    norms = [n_two, permute(n_two, p_core), n_across, permute(n_across, p_core)]
    dys = [dy_own, permute(dy_own, p_core), dy_across, permute(dy_across, p_core)]

    def hidden_units(parts, weights, kinds, order):
        outs = [shape_of((len(parts) * own, units))] * 2 + [shape_of(block, kind) for kind in kinds * 2]
        return call(
            functools.partial(hidden_units_kernel, parts, order),
            "hidden_units",
            (ix, *[norms[p] for p in parts], *[dys[p] for p in parts], *weights),
            outs + ([shape_of((width, units)), shape_of((units, width))] if order else []),
            flops=8 * len(parts) * own * width * units,
            transcendentals=2 * len(parts) * own * units,
        )

    act3, up3, give3, r_give3, full_up, full_down = hidden_units((3,), (second,), (BF16,), blocks)
    got3 = permute(give3, p_core)
    act2, up2, keep2, r_keep2 = hidden_units((2,), (after(full_up, give3), full_down), (F32,), None)
    far = far_sum(keep2, got3)
    across = permute(far, p_y)
    act10, up10, give1, keep0, r_give1, r_keep0 = hidden_units((1, 0), (after(full_up, far), full_down), (BF16, F32), None)
    got = permute(give1, p_core)
    in_order = [(i, i, n) for i, _, n in blocks]

    def grads(name, lefts, rights, order, extra=()):
        widths = tuple(r[0].shape[1] for r in rights)
        depth, cols = sum(a.shape[0] for a in lefts), sum(widths)
        height = lefts[0].shape[1]
        total = cols + sum(e.shape[1] for e in extra[1:])
        return call(
            functools.partial(grads_kernel, order, len(lefts), widths, len(rights[0]), len(extra)),
            name,
            (ix, *lefts, *[piece for r in rights for piece in r], *extra),
            [shape_of((height, total))],
            scratch=[pltpu.VMEM((height, depth), BF16)] + [pltpu.VMEM((depth, w), BF16) for w in widths],
            grid=(4,),
            flops=2 * depth * height * cols,
            out_specs={0: pl.BlockSpec((height // 4, total), lambda i: (i, 0))},
        )[0]

    order = (3, 2, 1, 0)
    (ff_terms,) = call(
        functools.partial(grad_ff_kernel, blocks),
        "grad_ff",
        (ix, *[norms[p] for p in order], up3, up2, up10, act3, act2, act10, *[dys[p] for p in order]),
        [shape_of((width, units + width))],
        scratch=[pltpu.VMEM((width, 4 * own), BF16), pltpu.VMEM((units, 4 * own), BF16)]
        + [pltpu.VMEM((4 * own, units), BF16), pltpu.VMEM((4 * own, width), BF16)],
        grid=(4,),
        flops=2 * 4 * own * width * 2 * units,
        out_specs={0: pl.BlockSpec((width // 4, units + width), lambda i: (i, 0))},
    )
    ff_sum = ring_sum(ff_terms)
    up_sum, down_sum = ff_sum[:, :units], ff_sum[:, units:]
    *d_parts, d_hidden, d_low, sums_two = call(
        hidden_back_kernel,
        "hidden_back",
        (ix, keep0, got, across, hidden, dys[0], after(gains, ff_terms), near_out, far_out),
        [shape_of((own, quarter))] * 4 + [shape_of(block, F32), shape_of(block), shape_of((8, width), F32)],
        flops=2 * own * width * width,
    )
    d_mixed = quad_swap(d_parts)
    near_parts, far_parts = d_mixed[:2], d_mixed[2:]
    r_far = far_sum(r_keep2, permute(after(r_give3, d_parts[0]), p_core))
    r_across = permute(r_far, p_y)
    r_got = permute(after(r_give1, d_parts[0]), p_core)
    dq_near, kept = attend_back(ix, q, k, v, quarter, qrow, krow, lse_near, near_parts, 0, ())
    dq_far, dkv = attend_back(ix, q, k, v, quarter, qrow, krow, lse_far, far_parts, 2, (after(kept, r_far),))

    def placed(one, two):
        return [permute(one, p_back[0]), permute(two, p_back[1])]

    r_own = (after(hidden, dq_far) + r_keep0 + r_got.astype(F32) + r_across.astype(F32)).astype(BF16)
    n_rows = dkv.shape[0] // quads
    if quads > 1:
        total = dkv[:n_rows].astype(F32)
        for s in range(1, quads):
            total = total + permute(dkv[s * n_rows : (s + 1) * n_rows], group_perm(-s)).astype(F32)
        dkv = total.astype(BF16)

    keep_one, give_one, columns = call(
        functools.partial(project_back_kernel, run),
        "project_back",
        (ix, *taken, dq_near, dq_far, dkv, full_qkv, after(sums_two, r_own)),
        [shape_of((2 * own, width), F32), shape_of((2 * own, width)), shape_of((width, 128))],
        scratch=[pltpu.VMEM((128, width), F32)],
        grid=(4,),
        flops=2 * 4 * own * width * 3 * quarter,
        in_specs={
            6: pl.BlockSpec((own, 2 * quarter), lambda i: (jnp.where(i == 0, 1, jnp.where(i == 1, 3, (i - 2) * 2)), 0)),
        },
    )
    got_one = permute(give_one, p_core)
    grad_near, grad_far = call(
        out_grad_kernel,
        "out_grad",
        (ix, after(mixed_own, give_one), d_low),
        [shape_of((width, half), F32), shape_of((width, half))],
        flops=2 * own * width * width,
    )
    far_one = far_sum(keep_one[own:], after(got_one, grad_near)[own:])
    across_one = permute(far_one, p_y)
    at_terms = grads(
        "grad_at",
        [after(n_one, far_one)],
        [[jnp.concatenate([dq_near, dq_far], 0)], [dkv]],
        blocks,
        (grad_near, permute(grad_far, p_core), columns),
    )
    one_sum = ring_sum(after(at_terms, ff_sum))
    back_out = placed(*after((r_own[:run], r_own[run:]), at_terms))

    def home(name, summed):
        return quad_swap(call(home_kernel, name, (ix, summed), [shape_of((rows, summed.shape[1]))] * 4))

    def in_batches(one, two):
        return jnp.stack([jnp.where(z % 2 == 0, one, two), jnp.where(z % 2 == 0, two, one)], 0)

    d_one, d_two = call(
        functools.partial(tokens_back_kernel, run),
        "tokens_back",
        (ix, keep_one, got_one, across_one, taken[0], d_hidden, after(gains, ff_sum, back_out)),
        [shape_of((run, width))] * 2,
    )
    ff_home = home("home_up", after(up_sum, d_one))
    own_down = down_sum.astype(F32)
    if aligned:
        (own_up,) = call(
            functools.partial(settle_ff_kernel, spots), "settle_ff", (ix, *ff_home), [shape_of((rows, 4 * units), F32)])
    else:
        ups = [b.reshape(rows, pc.nodes, hid) for b in ff_home]
        at_spot = [[spots.index((nx, nz)) for nz in range(pc.zs)] for nx in range(pc.xs)]
        ups = by_rank([jnp.stack([jnp.stack([b[:, i] for i in row], 1) for row in at_spot], 1) for b in ups])
        own_up = (
            jnp.stack([jnp.stack([ups[0], ups[2]], 3), jnp.stack([ups[1], ups[3]], 3)], 2)
            .reshape(rows, 4 * units)
            .astype(F32)
        )
    back_grad = placed(*after((d_one, d_two), own_up))
    at_home = home("home_at", after(one_sum, back_out))
    output = in_batches(*after(back_out, d_one))
    own_qkv, own_out, vectors = call(
        settle_kernel,
        "settle",
        (ix, *at_home),
        [shape_of((rows, 3 * width), F32), shape_of((rows, width), F32), shape_of((8, 128), F32)],
        scratch=[pltpu.VMEM((128, 128), F32)],
    )
    (input_grad,) = call(
        spread_kernel, "spread", (ix, *after(back_grad, own_qkv)), [shape_of((micro, run, width), F32)]
    )
    return (output, input_grad, own_qkv, own_out, own_up, own_down) + tuple(vectors[i, :rows] for i in range(4))


def solution(mesh):
    vector, matrix, batch = P(AXES), P(AXES, None), P(None, AXES, None)
    return jax.shard_map(
        functools.partial(body, Places(mesh)),
        mesh=mesh,
        in_specs=(batch, P(None, "dp", "fsdp")) + (matrix,) * 4 + (vector,) * 4 + (batch,),
        out_specs=(batch, batch) + (matrix,) * 4 + (vector,) * 4,
        check_vma=False,
    )
```
